32 devices in a mesh: req: 4 (over y, core), exp: 8 (over z, x).
Axes of the slice: x: 2, y: 2, z: 4, core: 2. Of those that a mesh axis runs over, the one named last changes fastest.
Arguments:
- hidden_in: bfloat16 [8, 256, 2880], P('exp', 'req'), may hold values from -6 to 6
- queries: bfloat16 [8, 256, 4096], P('exp', 'req'), may hold values from -115 to 115
- new_kv: bfloat16 [8, 256, 1024], P('exp', 'req'), may hold values from -6 to 6
- kv_pool: bfloat16 [8, 32, 16, 1024], P('exp', 'req'), may hold values from -6 to 6
- page_table: int32 [8, 16], P('exp'), may hold values from 0 to 31, as said below
- new_slots: int32 [8, 16], P('exp'), may hold values from 0 to 31
- cached_pages: int32 [8], P('exp'), may hold values from 1 to 16, as said below
- sinks: float32 [64], replicated, may hold values from 2 to 8
- out_weight: bfloat16 [4096, 2880], P('req', 'exp'), may hold values from -0.375 to 0.375
Outputs:
- layer_out: bfloat16 [8, 256, 2880], P('exp', 'req')
- pool_out: bfloat16 [8, 32, 16, 1024], P('exp', 'req')
The draws below stay inside these ranges and needn't reach their ends.
Inputs may be any that keep to these rules, and one draw needn't show every extreme that they name: For each request the entries of page_table and new_slots are 32 distinct slots. `cached_pages`: some request has exactly 16 cached pages.
All inputs are finite; a program needn't handle non-finite values.
Results may differ from the reference program's by a relative error of at most 0.009.
The reference program's roundings to bfloat16 on the way count: a program that leaves them out, or rounds other values in their place, can miss the bound.
Values may be sent and summed in bfloat16 or wider, within the bound.
No kernel may reach another device: no remote copies, remote signals or barrier semaphores. Data moves between devices by JAX's collectives and lax.ppermute only.
A program may use at most 64 MiB of HBM per device.

```python
import math
import jax
import jax.numpy as jnp
from jax import lax

D = 2880
HEADS = 64
KV_HEADS = 8
HD = 64
PAGE = 16
POOL_DEV = 8
REQS = 8
NEW = 256
SLOTS = 32
MAXPAGES = 16
NEWPAGES = 16
N_REQ = 4


def slot_order(key):
    owners = SLOTS // POOL_DEV

    def order_one(one_key):
        owner_key, slot_key = jax.random.split(one_key)
        shift_bits = jax.random.randint(owner_key, (owners,), 0, 5)
        noise_bits = jax.random.randint(slot_key, (owners, POOL_DEV), 0, 65536)
        order_key = jnp.right_shift(noise_bits, shift_bits[:, None]).reshape(-1) * SLOTS + jnp.arange(SLOTS)
        return jnp.argsort(order_key, stable=True).astype(jnp.int32)
    return jax.vmap(order_one)(jax.random.split(jax.random.fold_in(key, 11), REQS))


def draw_page_table(key, part):
    return slot_order(key)[:, :MAXPAGES]


def draw_new_slots(key, part):
    return slot_order(key)[:, MAXPAGES:MAXPAGES + NEWPAGES]


def draw_cached_pages(key, part):
    shift_key, pick_key = jax.random.split(jax.random.fold_in(key, 23))
    shift_bits = jax.random.randint(shift_key, (REQS,), 0, 7)
    page_count = jnp.maximum(jnp.right_shift(jnp.full((REQS,), MAXPAGES, jnp.int32), shift_bits), 1)
    longest = jax.random.randint(pick_key, (), 0, REQS)
    return jnp.where(jnp.arange(REQS) == longest, MAXPAGES, page_count).astype(jnp.int32)


def draw_queries(key, part):
    base_key = jax.random.fold_in(jax.random.fold_in(key, 31), 0)
    values = jax.random.normal(base_key, (REQS, NEW, HEADS * HD), jnp.float32)
    return values.astype(jnp.bfloat16)


def level_of(stream_key, extent, cuts, least, high):
    factor_of, own = 1.0, jax.random.fold_in(stream_key, 6)
    for position, blocks in cuts:
        draws = jnp.exp(jax.random.uniform(jax.random.fold_in(own, position), (blocks,), jnp.float32, least / len(cuts), high / len(cuts)))
        factor_of = factor_of * jnp.repeat(draws, extent[position] // blocks).reshape([-1 if axis == position else 1 for axis in range(len(extent))])
    return factor_of


def scatter_about(key, shape, scale, reach, cuts=(), kind=jnp.bfloat16):
    array = scale * jax.random.normal(key, shape, jnp.float32)
    if cuts:
        array = array * level_of(key, shape, cuts, -0.22, 0.18)
    return jnp.clip(array, -reach, reach).astype(kind)


def setup_inputs(seed: int = 0) -> dict:
    seeds = jax.random.split(jax.random.key(seed), 10)
    return {
        "hidden_in": scatter_about(seeds[0], (REQS, NEW, D), 1.0, 6.0, ((0, 8), (1, 4))),
        "queries": draw_queries(jax.random.fold_in(seeds[9], 71), 0),
        "new_kv": scatter_about(seeds[2], (REQS, NEW, 2 * KV_HEADS * HD), 1.0, 6.0, ((0, 8), (1, 4))),
        "kv_pool": scatter_about(seeds[3], (REQS, SLOTS, PAGE, 2 * KV_HEADS * HD), 1.0, 6.0, ((0, 8), (1, 4))),
        "page_table": draw_page_table(jax.random.fold_in(seeds[9], 71), 0),
        "new_slots": draw_new_slots(jax.random.fold_in(seeds[9], 71), 0),
        "cached_pages": draw_cached_pages(jax.random.fold_in(seeds[9], 71), 0),
        "sinks": jnp.clip(jax.random.uniform(seeds[7], (HEADS,), jnp.float32, 2.0, 8.0), 2.0, 8.0),
        "out_weight": scatter_about(seeds[8], (HEADS * HD, D), (HEADS * HD // 16) ** -0.5, 0.375, ((0, 4), (1, 8))),
    }


THETA = 150000.0
NEGATIVE = -1e+30

def rotate(values, positions):
    half_width = values.shape[-1] // 2
    frequency = THETA ** (-2.0 * jnp.arange(half_width).astype(jnp.float32) / values.shape[-1])
    angles = positions.astype(jnp.float32)[:, None] * frequency[None, :]
    cosine = jnp.cos(angles)[:, None, :]
    sine_part = jnp.sin(angles)[:, None, :]
    lower_half = values[..., :half_width]
    upper_half = values[..., half_width:]
    return jnp.concatenate([lower_half * cosine - upper_half * sine_part, upper_half * cosine + lower_half * sine_part], axis=-1)

def request_attention(sinks, out_weight, operands):
    query_rows, kv_rows, pool_pages, page_list, slot_list, page_count = operands
    kv_width = kv_rows.shape[1] // 2
    kv_heads = kv_width // HD
    per_group = HEADS // kv_heads
    positions = page_count * PAGE + jnp.arange(NEW).astype(jnp.int32)
    q_rot = rotate(query_rows.reshape(NEW, HEADS, HD).astype(jnp.float32), positions).astype(jnp.bfloat16)
    k_rot = rotate(kv_rows[:, :kv_width].reshape(NEW, kv_heads, HD).astype(jnp.float32), positions).astype(jnp.bfloat16)
    fresh = jnp.concatenate([k_rot.reshape(NEW, kv_width), kv_rows[:, kv_width:]], axis=1)
    cached = pool_pages[page_list].reshape(MAXPAGES * PAGE, 2 * kv_width)
    all_rows = jnp.concatenate([cached, fresh], axis=0)
    key_rows = jnp.transpose(all_rows[:, :kv_width].reshape(-1, kv_heads, HD).astype(jnp.float32), (1, 0, 2))
    value_rows = jnp.transpose(all_rows[:, kv_width:].reshape(-1, kv_heads, HD).astype(jnp.float32), (1, 0, 2))
    live_keys = jnp.arange(MAXPAGES * PAGE).astype(jnp.int32) // PAGE < page_count
    causal = jnp.arange(NEW)[None, :] <= jnp.arange(NEW)[:, None]
    key_mask = jnp.concatenate([jnp.broadcast_to(live_keys[None, :], (NEW, MAXPAGES * PAGE)), causal], axis=1)
    grouped = jnp.transpose(q_rot.reshape(NEW, kv_heads, per_group, HD).astype(jnp.float32), (1, 0, 2, 3))
    sink_logit = sinks.reshape(kv_heads, per_group)

    def one_group(group_operands):
        group_queries, group_keys, group_values, group_sinks = group_operands
        scores = jnp.einsum('thd,kd->thk', group_queries, group_keys) * (1.0 / math.sqrt(HD))
        scores = jnp.where(key_mask[:, None, :], scores, NEGATIVE)
        top_score = jnp.maximum(lax.optimization_barrier(jnp.max(scores, axis=-1)), group_sinks[None])
        weights = jnp.where(key_mask[:, None, :], jnp.exp(scores - top_score[..., None]), 0.0)
        denominator = lax.optimization_barrier(jnp.sum(weights, axis=-1)) + jnp.exp(group_sinks[None] - top_score)
        rounded = lax.optimization_barrier(weights.astype(jnp.bfloat16)).astype(jnp.float32)
        summed = jnp.einsum('thk,kd->thd', rounded, group_values)
        return (summed / denominator[..., None]).astype(jnp.bfloat16)
    context = lax.map(one_group, (grouped, key_rows, value_rows, sink_logit))
    context = jnp.transpose(context, (1, 0, 2, 3)).reshape(NEW, HEADS * HD)
    group_width = HEADS * HD // N_REQ
    context_wide = lax.optimization_barrier(context).astype(jnp.float32)
    terms = jnp.einsum('tnj,njd->tnd', context_wide.reshape(NEW, N_REQ, group_width), out_weight.reshape(N_REQ, group_width, D).astype(jnp.float32))
    attn = lax.optimization_barrier(jnp.sum(lax.optimization_barrier(terms.astype(jnp.bfloat16)).astype(jnp.float32), axis=1))
    pool_next = pool_pages.at[slot_list].set(fresh.reshape(NEWPAGES, PAGE, 2 * kv_width))
    return (attn, pool_next)

def partial_attention(sinks, out_weight):

    def apply_one(operands):
        return request_attention(sinks, out_weight, operands)
    return apply_one

def reference(hidden_in, queries, new_kv, kv_pool, page_table, new_slots, cached_pages, sinks, out_weight):
    attn, pool_out = lax.map(partial_attention(sinks, out_weight), (queries, new_kv, kv_pool, page_table, new_slots, cached_pages))
    layer_out = (hidden_in.astype(jnp.float32) + attn).astype(jnp.bfloat16)
    return (layer_out, pool_out)
```

```python
import functools
import math

import jax
import jax.numpy as jnp
from jax import lax
from jax.experimental import pallas as pl
from jax.experimental.pallas import tpu as pltpu
from jax.sharding import PartitionSpec as P

HD = 64


THETA = 150000.0
NEGATIVE = -1e30


def rotate(values, positions):
    half_width = values.shape[-1] // 2
    frequency = THETA ** (-2.0 * jnp.arange(half_width).astype(jnp.float32) / values.shape[-1])
    angles = positions.astype(jnp.float32)[:, None] * frequency[None, :]
    cosine = jnp.cos(angles)[:, None, :]
    sine_part = jnp.sin(angles)[:, None, :]
    lower_half = values[..., :half_width]
    upper_half = values[..., half_width:]
    return jnp.concatenate(
        [
            lower_half * cosine - upper_half * sine_part,
            upper_half * cosine + lower_half * sine_part,
        ],
        axis=-1,
    )


def spread_heads(rows, head_total, kv_heads, dev_count):
    per_dev = head_total // dev_count
    per_kv = head_total // kv_heads
    repeat = max(1, per_kv // per_dev)
    kv_dev = max(1, per_dev // per_kv)
    count = rows.shape[0]
    split = jnp.repeat(rows.reshape(count, 2, kv_heads, HD), repeat, axis=2)
    split = split.reshape(count, 2, dev_count, kv_dev * HD)
    return jnp.transpose(split, (0, 2, 1, 3)).reshape(count, dev_count, 2 * kv_dev * HD)


def general_plan(
    hidden_in, queries, new_kv, kv_pool, page_table, new_slots, cached_pages, sinks, out_weight
):
    tok_dev = hidden_in.shape[1]
    n_req = lax.axis_size("req")
    own_index = lax.axis_index("req")
    fresh_count = tok_dev * n_req
    head_count = sinks.shape[0]
    kv_width = new_kv.shape[2] // 2
    kv_heads = kv_width // HD
    per_kv = head_count // kv_heads
    heads_dev = head_count // n_req
    kv_dev = max(1, heads_dev // per_kv)
    per_dev_group = heads_dev // kv_dev
    head_width = 2 * kv_dev * HD
    slots_dev = kv_pool.shape[1]
    page_size = kv_pool.shape[2]
    slot_total = slots_dev * n_req
    page_limit = page_table.shape[1]
    fresh_pages = new_slots.shape[1]
    page_count = cached_pages[0]
    start_pos = page_count * page_size
    own_pos = start_pos + own_index * tok_dev + jnp.arange(tok_dev)
    q_rot = rotate(queries[0].reshape(tok_dev, head_count, HD).astype(jnp.float32), own_pos).astype(
        jnp.bfloat16
    )
    k_rot = rotate(
        new_kv[0, :, :kv_width].reshape(tok_dev, kv_heads, HD).astype(jnp.float32), own_pos
    ).astype(jnp.bfloat16)
    kv_rot = jnp.concatenate([k_rot.reshape(tok_dev, kv_width), new_kv[0, :, kv_width:]], axis=1)
    slot_all = jnp.arange(slot_total)
    page_index = jnp.arange(page_limit)
    cached_hit = (page_table[0][None, :] == slot_all[:, None]) & (page_index[None, :] < page_count)
    is_cached = jnp.any(cached_hit, axis=1)
    cached_base = jnp.sum(jnp.where(cached_hit, page_index[None, :], 0), axis=1) * page_size
    fresh_hit = new_slots[0][None, :] == slot_all[:, None]
    is_fresh = jnp.any(fresh_hit, axis=1)
    fresh_base = (
        start_pos
        + jnp.sum(jnp.where(fresh_hit, jnp.arange(fresh_pages)[None, :], 0), axis=1) * page_size
    )
    key_pos = (
        jnp.where(is_fresh, fresh_base, cached_base)[:, None] + jnp.arange(page_size)[None, :]
    ).reshape(-1)
    key_live = jnp.repeat(is_cached | is_fresh, page_size)
    all_fresh = lax.all_gather(kv_rot, "req", axis=0, tiled=True)
    own_hit = lax.dynamic_slice_in_dim(fresh_hit, own_index * slots_dev, slots_dev, 0)
    own_fresh = lax.dynamic_slice_in_dim(is_fresh, own_index * slots_dev, slots_dev, 0)
    appended = jnp.dot(
        own_hit.astype(jnp.bfloat16),
        all_fresh.reshape(fresh_pages, page_size * 2 * kv_width),
        preferred_element_type=jnp.float32,
    )
    appended = appended.astype(jnp.bfloat16).reshape(slots_dev, page_size, 2 * kv_width)
    local_pages = jnp.where(own_fresh[:, None, None], appended, kv_pool[0])
    head_pool = lax.all_to_all(
        spread_heads(
            local_pages.reshape(slots_dev * page_size, 2 * kv_width), head_count, kv_heads, n_req
        ),
        "req",
        split_axis=1,
        concat_axis=0,
        tiled=True,
    )
    head_pool = head_pool.reshape(slot_total * page_size, head_width)
    q_here = lax.all_to_all(
        q_rot.reshape(tok_dev, n_req, heads_dev * HD),
        "req",
        split_axis=1,
        concat_axis=0,
        tiled=True,
    )
    q_here = q_here.reshape(fresh_count, heads_dev * HD)
    key_total = slot_total * page_size
    all_keys = head_pool[:, : kv_dev * HD].reshape(key_total, kv_dev, HD)
    all_values = head_pool[:, kv_dev * HD :].reshape(key_total, kv_dev, HD)
    sink_mine = lax.dynamic_slice_in_dim(sinks, own_index * heads_dev, heads_dev, 0).reshape(
        kv_dev, per_dev_group
    )
    scale = 1.0 / math.sqrt(HD)
    query_block = math.gcd(fresh_count, 128)
    contexts = []
    for block_start in range(0, fresh_count, query_block):
        block_queries = q_here[block_start : block_start + query_block].reshape(
            query_block, kv_dev, per_dev_group, HD
        )
        query_pos = start_pos + block_start + jnp.arange(query_block)
        visible = key_live[None, :] & (key_pos[None, :] <= query_pos[:, None])
        scores = (
            jnp.einsum(
                "tghd,kgd->tghk", block_queries, all_keys, preferred_element_type=jnp.float32
            )
            * scale
        )
        scores = jnp.where(visible[:, None, None, :], scores, NEGATIVE)
        top_score = jnp.maximum(jnp.max(scores, axis=-1), sink_mine[None])
        expo = jnp.where(visible[:, None, None, :], jnp.exp(scores - top_score[..., None]), 0.0)
        denominator = jnp.sum(expo, axis=-1) + jnp.exp(sink_mine[None] - top_score)
        weighted = jnp.einsum(
            "tghk,kgd->tghd",
            expo.astype(jnp.bfloat16),
            all_values,
            preferred_element_type=jnp.float32,
        )
        contexts.append(
            (weighted / denominator[..., None])
            .astype(jnp.bfloat16)
            .reshape(query_block, heads_dev * HD)
        )
    context = jnp.concatenate(contexts, axis=0)
    terms = jnp.dot(
        context,
        lax.all_gather(out_weight, "exp", axis=1, tiled=True),
        preferred_element_type=jnp.float32,
    ).astype(jnp.bfloat16)
    width = terms.shape[1]
    arrived = lax.all_to_all(
        terms.reshape(n_req, tok_dev, width), "req", split_axis=0, concat_axis=0, tiled=True
    )
    attn = jnp.sum(arrived.astype(jnp.float32), axis=0)
    layer_out = (hidden_in[0].astype(jnp.float32) + attn).astype(jnp.bfloat16)
    return (layer_out[None], local_pages[None])


VMEM_LIMIT = 56 * 1024 * 1024
F32 = jnp.float32
BF16 = jnp.bfloat16

PAIR_BIT, NEAR_BIT, FAR_BIT = 2, 1, 4


def vmem():
    return pl.BlockSpec(memory_space=pltpu.VMEM)


def smem():
    return pl.BlockSpec(memory_space=pltpu.SMEM)


def anywhere():
    return pl.BlockSpec(memory_space=pl.ANY)


def params():
    return pltpu.CompilerParams(vmem_limit_bytes=VMEM_LIMIT)


def cost(flops, nbytes):
    return pl.CostEstimate(flops=int(flops), bytes_accessed=int(nbytes), transcendentals=0)


def swap(values, req_bits, exp_bits):
    if not exp_bits:
        return lax.ppermute(values, "req", [(i, i ^ req_bits) for i in range(lax.axis_size("req"))])
    if not req_bits:
        return lax.ppermute(values, "exp", [(i, i ^ exp_bits) for i in range(lax.axis_size("exp"))])
    rows, cols = lax.axis_size("req"), lax.axis_size("exp")
    pairs = [
        (i * cols + j, (i ^ req_bits) * cols + (j ^ exp_bits)) for i in range(rows) for j in range(cols)
    ]
    return lax.ppermute(values, ("req", "exp"), pairs)


def pack_kernel(q_ref, kv_ref, pool_ref, *rest):
    outs, sems = rest[:-1], rest[-1]
    n_req = len(outs)
    own = lax.axis_index("req")
    tok = q_ref.shape[0]
    q_width = q_ref.shape[1] // n_req
    kv_width = kv_ref.shape[1] // 2
    head_width = kv_width // n_req
    copies = []

    def copy(source, target):
        one = pltpu.make_async_copy(source, target, sems.at[len(copies)])
        one.start()
        copies.append(one)

    for k in (2, 3, 1, 0):
        dest = jnp.bitwise_xor(own, k)
        out = outs[k]
        q_col = pl.multiple_of(dest * q_width, 128)
        copy(q_ref.at[:, pl.ds(q_col, q_width)], out.at[:, pl.ds(0, q_width)])
        at = q_width
        blocks = [kv_ref]
        blocks += [pool_ref.at[pl.ds(i * tok, tok), :] for i in range(pool_ref.shape[0] // tok)]
        for block in blocks:
            for half in range(2):
                col = pl.multiple_of(half * kv_width + dest * head_width, 128)
                copy(block.at[:, pl.ds(col, head_width)], out.at[:, pl.ds(at, head_width)])
                at += head_width
    for one in copies:
        one.wait()


def pack(q, kv, pool, n_req):
    tok = q.shape[0]
    blocks = 1 + pool.shape[0] // tok
    width = (q.shape[1] + blocks * kv.shape[1]) // n_req
    return pl.pallas_call(
        pack_kernel,
        out_shape=[jax.ShapeDtypeStruct((tok, width), BF16)] * n_req,
        in_specs=[anywhere()] * 3,
        out_specs=[anywhere()] * n_req,
        scratch_shapes=[pltpu.SemaphoreType.DMA((n_req * (1 + 2 * blocks),))],
        compiler_params=params(),
        cost_estimate=cost(0, 4 * tok * width * n_req),
        name="pack",
    )(q, kv, pool)


def turn(values, cosine, sine):
    lane = lax.broadcasted_iota(jnp.int32, values.shape, 1)
    other = jnp.where(lane % HD < HD // 2, pltpu.roll(values, 128 - HD // 2, 1), pltpu.roll(values, HD // 2, 1))
    return values * cosine + other * sine


def attention_kernel(
    pages_ref, table_ref, sink_ref, cos_ref, sin_ref, *rest, kv_dev, per_kv, page_size
):
    n_req = len(rest) - 6
    pieces, out_ref = rest[:n_req], rest[n_req]
    q_scr, pool_scr, key_scr, value_scr, flat_scr = rest[n_req + 1 :]
    own = lax.axis_index("req")
    tok = pieces[0].shape[0]
    q_width = kv_dev * per_kv * HD
    head_width = kv_dev * HD
    page_limit = table_ref.shape[1]
    cached = page_limit * page_size
    fresh = tok * n_req
    total = cached + fresh
    pool_rows = pool_scr.shape[1]
    page_count = pages_ref[0]
    pairs = per_kv // 2
    for k in range(n_req):
        shard = jnp.bitwise_xor(own, k)
        row = pl.multiple_of(shard * tok, tok)
        cosine = cos_ref[pl.ds(row, tok), :]
        sine = sin_ref[pl.ds(row, tok), :]
        for g in range(kv_dev):
            for p in range(pairs):
                col = (g * pairs + p) * 2 * HD
                turned = turn(pieces[k][:, col : col + 2 * HD].astype(F32), cosine, sine).astype(BF16)
                q_scr[k, g, p * tok : (p + 1) * tok, :] = turned * jnp.asarray(1.0 / math.sqrt(HD), BF16)
        at = q_width
        key_row = pl.multiple_of(cached + row, tok)
        flat_scr[pl.ds(key_row, tok), :head_width] = turn(
            pieces[k][:, at : at + head_width].astype(F32), cosine, sine
        )
        flat_scr[pl.ds(key_row, tok), head_width:] = pieces[k][
            :, at + head_width : at + 2 * head_width
        ].astype(F32)
        at += 2 * head_width
        for i in range(pool_rows // tok):
            pool_scr[shard, i * tok : (i + 1) * tok, :] = pieces[k][:, at : at + 2 * head_width].astype(F32)
            at += 2 * head_width
    per_dev = pool_rows // page_size
    for j in range(page_limit):
        slot = table_ref[0, j]
        source = pl.multiple_of((slot % per_dev) * page_size, page_size)
        flat_scr[j * page_size : (j + 1) * page_size, :] = pool_scr[
            slot // per_dev, pl.ds(source, page_size), :
        ]
    for scr, at in ((key_scr, 0), (value_scr, head_width)):
        flat = flat_scr[:, at : at + head_width]
        rolled = pltpu.roll(flat, HD, 1)
        low = lax.broadcasted_iota(jnp.int32, flat.shape, 1) < HD
        zero = jnp.zeros_like(flat)
        scr[0, :total, :] = jnp.where(low, flat, zero).astype(BF16)
        scr[0, total:, :] = jnp.where(low, zero, rolled).astype(BF16)
        scr[1, :total, :] = jnp.where(low, rolled, zero).astype(BF16)
        scr[1, total:, :] = jnp.where(low, zero, flat).astype(BF16)
    live = page_count * page_size

    def one_shard(k, carry):
        shard = jnp.bitwise_xor(own, k)
        key = lax.broadcasted_iota(jnp.int32, (tok, total), 1)
        query = lax.broadcasted_iota(jnp.int32, (tok, total), 0) + shard * tok
        last = jnp.where(key < cached, live - 1, query + cached)
        bias = jnp.where(key > last, NEGATIVE, 0.0)
        bias = jnp.concatenate([bias] * pairs, axis=0)
        for g in range(kv_dev):
            scores = lax.dot_general(
                q_scr[k, g], key_scr[g], (((1,), (1,)), ((), ())), preferred_element_type=F32
            )
            weights, dens = [], []
            for a in range(2):
                part = scores[:, a * total : (a + 1) * total] + bias
                first = own * (kv_dev * per_kv) + g * per_kv + a
                sink = jnp.concatenate(
                    [jnp.full((tok, 1), sink_ref[first + 2 * p], F32) for p in range(pairs)], axis=0
                )
                top = jnp.maximum(jnp.max(part, axis=1, keepdims=True), sink)
                expo = jnp.exp(part - top)
                dens.append(jnp.sum(expo, axis=1, keepdims=True) + jnp.exp(sink - top))
                weights.append(expo.astype(BF16))
            summed = jnp.dot(weights[0], value_scr[g, :total, :], preferred_element_type=F32) + jnp.dot(
                weights[1], value_scr[g, total:, :], preferred_element_type=F32
            )
            low = lax.broadcasted_iota(jnp.int32, summed.shape, 1) < HD
            ctx = (summed / jnp.where(low, dens[0], dens[1])).astype(BF16)
            for p in range(pairs):
                col = (g * pairs + p) * 2 * HD
                out_ref[k, :, col : col + 2 * HD] = ctx[p * tok : (p + 1) * tok, :]
        return carry

    lax.fori_loop(0, n_req, one_shard, 0)


def attention(pages, table, sinks, cosine, sine, pieces, kv_dev, per_kv, pool_rows, page_size):
    n_req = len(pieces)
    tok = pieces[0].shape[0]
    total = table.shape[1] * page_size + n_req * tok
    q_width = kv_dev * per_kv * HD
    return pl.pallas_call(
        functools.partial(attention_kernel, kv_dev=kv_dev, per_kv=per_kv, page_size=page_size),
        out_shape=jax.ShapeDtypeStruct((n_req, tok, q_width), BF16),
        in_specs=[smem()] * 3 + [vmem()] * (2 + n_req),
        out_specs=vmem(),
        scratch_shapes=[
            pltpu.VMEM((n_req, kv_dev, per_kv // 2 * tok, 2 * HD), BF16),
            pltpu.VMEM((n_req, pool_rows, 2 * kv_dev * HD), F32),
            pltpu.VMEM((kv_dev, 2 * total, 2 * HD), BF16),
            pltpu.VMEM((kv_dev, 2 * total, 2 * HD), BF16),
            pltpu.VMEM((total, 2 * kv_dev * HD), F32),
        ],
        compiler_params=params(),
        cost_estimate=cost(3e9, 2**22),
        name="attention",
    )(pages, table, sinks, cosine, sine, *pieces)


def pool_kernel(slots_ref, cos_ref, sin_ref, pool_ref, *rest, page_size):
    pieces, out_ref, fresh_scr = rest[:-2], rest[-2], rest[-1]
    own = lax.axis_index("req")
    tok = pieces[0].shape[0]
    kv_width = pieces[0].shape[1] // 2
    for k, piece in enumerate(pieces):
        row = pl.multiple_of(jnp.bitwise_xor(own, k) * tok, tok)
        cosine = cos_ref[pl.ds(row, tok), :]
        sine = sin_ref[pl.ds(row, tok), :]
        for col in range(0, kv_width, 128):
            turned = turn(piece[:, col : col + 128].astype(F32), cosine, sine).astype(BF16)
            fresh_scr[pl.ds(row, tok), col : col + 128] = turned
        fresh_scr[pl.ds(row, tok), kv_width:] = piece[:, kv_width:]
    out_ref[...] = pool_ref[...]
    slots_dev = out_ref.shape[0]
    for n in range(slots_ref.shape[1]):
        slot = slots_ref[0, n]

        @pl.when(slot // slots_dev == own)
        def _(slot=slot, n=n):
            out_ref[slot % slots_dev] = fresh_scr[n * page_size : (n + 1) * page_size, :]


def write_pool(slots, cosine, sine, pool, pieces):
    tok, width = pieces[0].shape
    return pl.pallas_call(
        functools.partial(pool_kernel, page_size=pool.shape[1]),
        out_shape=jax.ShapeDtypeStruct(pool.shape, BF16),
        in_specs=[smem()] + [vmem()] * (3 + len(pieces)),
        out_specs=vmem(),
        scratch_shapes=[pltpu.VMEM((tok * len(pieces), width), BF16)],
        compiler_params=params(),
        cost_estimate=cost(1e8, 2**21),
        name="write_pool",
    )(slots, cosine, sine, pool, *pieces)


def project_kernel(*refs, n_ctx, chunks):
    contexts = refs[:n_ctx]
    weights = refs[n_ctx:-2]
    send_ref, keep_ref = refs[-2:]
    n_req, tok, depth = contexts[0].shape
    for i in range(n_ctx):
        ctx = contexts[i][...].reshape(n_req * tok, depth)
        at = 0
        for b, count in enumerate(chunks):
            total, row = None, 0
            for j in range(count):
                rows = weights[at].shape[0]
                part = jnp.dot(ctx[:, row : row + rows], weights[at][...], preferred_element_type=F32)
                total = part if total is None else total + part
                row += rows
                at += 1
            terms = total.astype(BF16)
            for k in range(n_req):
                target = send_ref if k % 2 else keep_ref
                target[i, b, k // 2] = terms[k * tok : (k + 1) * tok, :]


def project(contexts, blocks):
    n_req, tok, depth = contexts[0].shape
    cols = blocks[0][0].shape[1]
    shape = jax.ShapeDtypeStruct((len(contexts), len(blocks), n_req // 2, tok, cols), BF16)
    flat = [chunk for block in blocks for chunk in block]
    work = len(contexts) * len(blocks)
    return pl.pallas_call(
        functools.partial(project_kernel, n_ctx=len(contexts), chunks=tuple(len(b) for b in blocks)),
        out_shape=[shape, shape],
        in_specs=[vmem()] * (len(contexts) + len(flat)),
        out_specs=[vmem()] * 2,
        compiler_params=params(),
        cost_estimate=cost(work * 2 * n_req * tok * depth * cols, 2 * depth * cols * len(blocks)),
        name="project",
    )(*contexts, *flat)


def pair_kernel(keep_ref, got_ref, *out_refs):
    half = len(out_refs) // keep_ref.shape[0]
    for i in range(keep_ref.shape[0]):
        for k in range(half):
            out_refs[i * half + k][...] = (
                keep_ref[i, :, k].astype(F32) + got_ref[i, :, k].astype(F32)
            ).astype(BF16)


def pair_sum(keep, got):
    n_ctx, blocks, half, tok, cols = keep.shape
    return pl.pallas_call(
        pair_kernel,
        out_shape=[jax.ShapeDtypeStruct((blocks, tok, cols), BF16)] * (n_ctx * half),
        in_specs=[vmem()] * 2,
        out_specs=[vmem()] * (n_ctx * half),
        compiler_params=params(),
        cost_estimate=cost(1e6, 6 * keep.size),
        name="pair_sum",
    )(keep, got)


def final_kernel(hidden_ref, *rest, places):
    parts, out_ref, scr = rest[:-2], rest[-2], rest[-1]
    own = lax.axis_index("exp")
    cols = parts[0].shape[-1]
    for (first, second), bits in zip(zip(parts[0::2], parts[1::2]), places):
        for b, bit in enumerate(bits):
            scr[jnp.bitwise_xor(own, bit)] = first[b].astype(F32) + second[b].astype(F32)
    for b in range(scr.shape[0]):
        at = slice(b * cols, (b + 1) * cols)
        out_ref[:, at] = (hidden_ref[:, at].astype(F32) + scr[b]).astype(BF16)


def finish(hidden, parts, places):
    tok, width = hidden.shape
    n_exp = lax.axis_size("exp")
    return pl.pallas_call(
        functools.partial(final_kernel, places=places),
        out_shape=jax.ShapeDtypeStruct(hidden.shape, BF16),
        in_specs=[vmem()] * (1 + len(parts)),
        out_specs=vmem(),
        scratch_shapes=[pltpu.VMEM((n_exp, tok, width // n_exp), F32)],
        compiler_params=params(),
        cost_estimate=cost(1e6, 8 * hidden.size),
        name="finish",
    )(hidden, *parts)


CHUNKS = 4


def paired_plan(
    hidden_in, queries, new_kv, kv_pool, page_table, new_slots, cached_pages, sinks, out_weight
):
    tok = hidden_in.shape[1]
    n_req = lax.axis_size("req")
    head_count = sinks.shape[0]
    kv_width = new_kv.shape[2] // 2
    kv_heads = kv_width // HD
    slots_dev, page_size = kv_pool.shape[1:3]
    pool_rows = slots_dev * page_size
    depth = out_weight.shape[0]
    pieces = pack(queries[0], new_kv[0], kv_pool[0].reshape(pool_rows, 2 * kv_width), n_req)
    pieces = [pieces[0]] + [swap(pieces[k], k, 0) for k in range(1, n_req)]

    near = swap(out_weight, 0, NEAR_BIT)
    step = depth // CHUNKS
    own_chunks = [out_weight[i * step : (i + 1) * step] for i in range(CHUNKS)]
    far = [swap(chunk, 0, FAR_BIT) for chunk in own_chunks]
    both = [swap(chunk, 0, NEAR_BIT) for chunk in far]

    position = cached_pages[0] * page_size + jnp.arange(n_req * tok)
    frequency = THETA ** (-2.0 * jnp.arange(HD // 2).astype(F32) / HD)
    angles = position.astype(F32)[:, None] * frequency[None, :]
    cosine, sine = jnp.cos(angles), jnp.sin(angles)
    cosine = jnp.concatenate([cosine] * 4, axis=1)
    sine = jnp.concatenate([-sine, sine, -sine, sine], axis=1)

    ctx = attention(
        cached_pages, page_table, sinks, cosine, sine, pieces, kv_heads // n_req,
        head_count // kv_heads, pool_rows, page_size,
    )
    ctx_mate = swap(ctx, 0, PAIR_BIT)
    fresh = [new_kv[0]] + [swap(new_kv[0], k, 0) for k in range(1, n_req)]
    pool_out = write_pool(new_slots, cosine, sine, kv_pool[0], fresh)

    early = [[out_weight], [near], far]
    late = [both]
    parts = []
    send, keep = project([ctx], early)
    own_a, over_y = pair_sum(keep, swap(send, 1, 0))
    parts += [own_a, swap(over_y, 2, 0)]
    send, keep = project([ctx_mate], early)
    over_pair, over_both = pair_sum(keep, swap(send, 1, 0))
    parts += [swap(over_pair, 0, PAIR_BIT), swap(over_both, 2, PAIR_BIT)]
    send, keep = project([ctx, ctx_mate], late)
    own_c, over_y, over_pair, over_both = pair_sum(keep, swap(send, 1, 0))
    parts += [own_c, swap(over_y, 2, 0), swap(over_pair, 0, PAIR_BIT), swap(over_both, 2, PAIR_BIT)]
    early_bits = (0, NEAR_BIT, FAR_BIT)
    late_bits = (NEAR_BIT ^ FAR_BIT,)
    places = (
        early_bits,
        tuple(PAIR_BIT ^ b for b in early_bits),
        late_bits,
        tuple(PAIR_BIT ^ b for b in late_bits),
    )
    layer_out = finish(hidden_in[0], parts, places)
    return (layer_out[None], pool_out[None])


def solution(mesh):
    paired = mesh.shape["req"] == 4 and mesh.shape["exp"] == 8
    return jax.shard_map(
        paired_plan if paired else general_plan,
        mesh=mesh,
        in_specs=(
            P("exp", "req", None),
            P("exp", "req", None),
            P("exp", "req", None),
            P("exp", "req", None, None),
            P("exp", None),
            P("exp", None),
            P("exp"),
            P(),
            P("req", "exp"),
        ),
        out_specs=(P("exp", "req", None), P("exp", "req", None, None)),
        check_vma=False,
    )
```

```python
import functools
import math

import jax
import jax.numpy as jnp
from jax import lax
from jax.experimental import pallas as pl
from jax.experimental.pallas import tpu as pltpu
from jax.sharding import PartitionSpec as P

HD = 64


THETA = 150000.0
NEGATIVE = -1e30


def rotate(values, positions):
    half_width = values.shape[-1] // 2
    frequency = THETA ** (-2.0 * jnp.arange(half_width).astype(jnp.float32) / values.shape[-1])
    angles = positions.astype(jnp.float32)[:, None] * frequency[None, :]
    cosine = jnp.cos(angles)[:, None, :]
    sine_part = jnp.sin(angles)[:, None, :]
    lower_half = values[..., :half_width]
    upper_half = values[..., half_width:]
    return jnp.concatenate(
        [
            lower_half * cosine - upper_half * sine_part,
            upper_half * cosine + lower_half * sine_part,
        ],
        axis=-1,
    )


def spread_heads(rows, head_total, kv_heads, dev_count):
    per_dev = head_total // dev_count
    per_kv = head_total // kv_heads
    repeat = max(1, per_kv // per_dev)
    kv_dev = max(1, per_dev // per_kv)
    count = rows.shape[0]
    split = jnp.repeat(rows.reshape(count, 2, kv_heads, HD), repeat, axis=2)
    split = split.reshape(count, 2, dev_count, kv_dev * HD)
    return jnp.transpose(split, (0, 2, 1, 3)).reshape(count, dev_count, 2 * kv_dev * HD)


def general_plan(
    hidden_in, queries, new_kv, kv_pool, page_table, new_slots, cached_pages, sinks, out_weight
):
    tok_dev = hidden_in.shape[1]
    n_req = lax.axis_size("req")
    own_index = lax.axis_index("req")
    fresh_count = tok_dev * n_req
    head_count = sinks.shape[0]
    kv_width = new_kv.shape[2] // 2
    kv_heads = kv_width // HD
    per_kv = head_count // kv_heads
    heads_dev = head_count // n_req
    kv_dev = max(1, heads_dev // per_kv)
    per_dev_group = heads_dev // kv_dev
    head_width = 2 * kv_dev * HD
    slots_dev = kv_pool.shape[1]
    page_size = kv_pool.shape[2]
    slot_total = slots_dev * n_req
    page_limit = page_table.shape[1]
    fresh_pages = new_slots.shape[1]
    page_count = cached_pages[0]
    start_pos = page_count * page_size
    own_pos = start_pos + own_index * tok_dev + jnp.arange(tok_dev)
    q_rot = rotate(queries[0].reshape(tok_dev, head_count, HD).astype(jnp.float32), own_pos).astype(
        jnp.bfloat16
    )
    k_rot = rotate(
        new_kv[0, :, :kv_width].reshape(tok_dev, kv_heads, HD).astype(jnp.float32), own_pos
    ).astype(jnp.bfloat16)
    kv_rot = jnp.concatenate([k_rot.reshape(tok_dev, kv_width), new_kv[0, :, kv_width:]], axis=1)
    slot_all = jnp.arange(slot_total)
    page_index = jnp.arange(page_limit)
    cached_hit = (page_table[0][None, :] == slot_all[:, None]) & (page_index[None, :] < page_count)
    is_cached = jnp.any(cached_hit, axis=1)
    cached_base = jnp.sum(jnp.where(cached_hit, page_index[None, :], 0), axis=1) * page_size
    fresh_hit = new_slots[0][None, :] == slot_all[:, None]
    is_fresh = jnp.any(fresh_hit, axis=1)
    fresh_base = (
        start_pos
        + jnp.sum(jnp.where(fresh_hit, jnp.arange(fresh_pages)[None, :], 0), axis=1) * page_size
    )
    key_pos = (
        jnp.where(is_fresh, fresh_base, cached_base)[:, None] + jnp.arange(page_size)[None, :]
    ).reshape(-1)
    key_live = jnp.repeat(is_cached | is_fresh, page_size)
    all_fresh = lax.all_gather(kv_rot, "req", axis=0, tiled=True)
    own_hit = lax.dynamic_slice_in_dim(fresh_hit, own_index * slots_dev, slots_dev, 0)
    own_fresh = lax.dynamic_slice_in_dim(is_fresh, own_index * slots_dev, slots_dev, 0)
    appended = jnp.dot(
        own_hit.astype(jnp.bfloat16),
        all_fresh.reshape(fresh_pages, page_size * 2 * kv_width),
        preferred_element_type=jnp.float32,
    )
    appended = appended.astype(jnp.bfloat16).reshape(slots_dev, page_size, 2 * kv_width)
    local_pages = jnp.where(own_fresh[:, None, None], appended, kv_pool[0])
    head_pool = lax.all_to_all(
        spread_heads(
            local_pages.reshape(slots_dev * page_size, 2 * kv_width), head_count, kv_heads, n_req
        ),
        "req",
        split_axis=1,
        concat_axis=0,
        tiled=True,
    )
    head_pool = head_pool.reshape(slot_total * page_size, head_width)
    q_here = lax.all_to_all(
        q_rot.reshape(tok_dev, n_req, heads_dev * HD),
        "req",
        split_axis=1,
        concat_axis=0,
        tiled=True,
    )
    q_here = q_here.reshape(fresh_count, heads_dev * HD)
    key_total = slot_total * page_size
    all_keys = head_pool[:, : kv_dev * HD].reshape(key_total, kv_dev, HD)
    all_values = head_pool[:, kv_dev * HD :].reshape(key_total, kv_dev, HD)
    sink_mine = lax.dynamic_slice_in_dim(sinks, own_index * heads_dev, heads_dev, 0).reshape(
        kv_dev, per_dev_group
    )
    scale = 1.0 / math.sqrt(HD)
    query_block = math.gcd(fresh_count, 128)
    contexts = []
    for block_start in range(0, fresh_count, query_block):
        block_queries = q_here[block_start : block_start + query_block].reshape(
            query_block, kv_dev, per_dev_group, HD
        )
        query_pos = start_pos + block_start + jnp.arange(query_block)
        visible = key_live[None, :] & (key_pos[None, :] <= query_pos[:, None])
        scores = (
            jnp.einsum(
                "tghd,kgd->tghk", block_queries, all_keys, preferred_element_type=jnp.float32
            )
            * scale
        )
        scores = jnp.where(visible[:, None, None, :], scores, NEGATIVE)
        top_score = jnp.maximum(jnp.max(scores, axis=-1), sink_mine[None])
        expo = jnp.where(visible[:, None, None, :], jnp.exp(scores - top_score[..., None]), 0.0)
        denominator = jnp.sum(expo, axis=-1) + jnp.exp(sink_mine[None] - top_score)
        weighted = jnp.einsum(
            "tghk,kgd->tghd",
            expo.astype(jnp.bfloat16),
            all_values,
            preferred_element_type=jnp.float32,
        )
        contexts.append(
            (weighted / denominator[..., None])
            .astype(jnp.bfloat16)
            .reshape(query_block, heads_dev * HD)
        )
    context = jnp.concatenate(contexts, axis=0)
    terms = jnp.dot(
        context,
        lax.all_gather(out_weight, "exp", axis=1, tiled=True),
        preferred_element_type=jnp.float32,
    ).astype(jnp.bfloat16)
    width = terms.shape[1]
    arrived = lax.all_to_all(
        terms.reshape(n_req, tok_dev, width), "req", split_axis=0, concat_axis=0, tiled=True
    )
    attn = jnp.sum(arrived.astype(jnp.float32), axis=0)
    layer_out = (hidden_in[0].astype(jnp.float32) + attn).astype(jnp.bfloat16)
    return (layer_out[None], local_pages[None])


VMEM_LIMIT = 24 * 1024 * 1024
F32 = jnp.float32
BF16 = jnp.bfloat16

PAIR_BIT, NEAR_BIT, FAR_BIT = 2, 1, 4
ORDER = (0, 2, 1, 3)


def vmem():
    return pl.BlockSpec(memory_space=pltpu.VMEM)


def smem():
    return pl.BlockSpec(memory_space=pltpu.SMEM)


def params():
    return pltpu.CompilerParams(vmem_limit_bytes=VMEM_LIMIT)


def cost(flops, nbytes):
    return pl.CostEstimate(flops=int(flops), bytes_accessed=int(nbytes), transcendentals=0)


def swap(values, req_bits, exp_bits):
    if not exp_bits:
        return lax.ppermute(values, "req", [(i, i ^ req_bits) for i in range(lax.axis_size("req"))])
    if not req_bits:
        return lax.ppermute(values, "exp", [(i, i ^ exp_bits) for i in range(lax.axis_size("exp"))])
    rows, cols = lax.axis_size("req"), lax.axis_size("exp")
    pairs = [
        (i * cols + j, (i ^ req_bits) * cols + (j ^ exp_bits)) for i in range(rows) for j in range(cols)
    ]
    return lax.ppermute(values, ("req", "exp"), pairs)


def pack_kernel(q_ref, kv_ref, pool_ref, *outs):
    n_req = len(outs)
    own = lax.axis_index("req")
    tok = q_ref.shape[0]
    q_width = q_ref.shape[1] // n_req
    kv_width = kv_ref.shape[1] // 2
    head_width = kv_width // n_req
    for k, out in enumerate(outs):
        dest = jnp.bitwise_xor(own, k)
        out[:, :q_width] = q_ref[:, pl.ds(pl.multiple_of(dest * q_width, 128), q_width)]
        at = q_width
        blocks = [(kv_ref, 0)]
        blocks += [(pool_ref, i * tok) for i in range(pool_ref.shape[0] // tok)]
        for block, row in blocks:
            for half in range(2):
                col = pl.multiple_of(half * kv_width + dest * head_width, 128)
                out[:, at : at + head_width] = block[row : row + tok, pl.ds(col, head_width)]
                at += head_width


def pack(q, kv, pool, n_req):
    tok = q.shape[0]
    blocks = 1 + pool.shape[0] // tok
    width = (q.shape[1] + blocks * kv.shape[1]) // n_req
    return pl.pallas_call(
        pack_kernel,
        out_shape=[jax.ShapeDtypeStruct((tok, width), BF16)] * n_req,
        in_specs=[vmem()] * 3,
        out_specs=[vmem()] * n_req,
        compiler_params=params(),
        cost_estimate=cost(0, 4 * tok * width * n_req),
        name="pack",
    )(q, kv, pool)


def turn(values, cosine, sine):
    lane = lax.broadcasted_iota(jnp.int32, values.shape, 1)
    other = jnp.where(lane % HD < HD // 2, pltpu.roll(values, 128 - HD // 2, 1), pltpu.roll(values, HD // 2, 1))
    return values * cosine + other * sine


def attention_kernel(
    pages_ref, table_ref, sink_ref, cos_ref, sin_ref, *rest, kv_dev, per_kv, page_size
):
    n_req = len(rest) - 7
    pieces, out_ref = rest[:n_req], rest[n_req]
    q_scr, pool_scr, flat_scr, key_scr, value_scr, bias_scr = rest[n_req + 1 :]
    own = lax.axis_index("req")
    tok = pieces[0].shape[0]
    q_width = kv_dev * per_kv * HD
    head_width = kv_dev * HD
    page_limit = table_ref.shape[1]
    cached = page_limit * page_size
    fresh = tok * n_req
    total = cached + fresh
    pool_rows = pool_scr.shape[1]
    live = pages_ref[0] * page_size
    pairs = per_kv // 2
    for place, k in enumerate(ORDER):
        shard = jnp.bitwise_xor(own, k)
        row = pl.multiple_of(shard * tok, tok)
        cosine = cos_ref[pl.ds(row, tok), :]
        sine = sin_ref[pl.ds(row, tok), :]
        for p in range(kv_dev * pairs):
            col = p * 2 * HD
            turned = turn(pieces[k][:, col : col + 2 * HD].astype(F32), cosine, sine).astype(BF16)
            q_scr[p, place * tok : (place + 1) * tok, :] = turned * jnp.asarray(1.0 / math.sqrt(HD), BF16)
        at = q_width
        key_row = pl.multiple_of(cached + row, tok)
        flat_scr[pl.ds(key_row, tok), :head_width] = turn(
            pieces[k][:, at : at + head_width].astype(F32), cosine, sine
        )
        flat_scr[pl.ds(key_row, tok), head_width:] = pieces[k][
            :, at + head_width : at + 2 * head_width
        ].astype(F32)
        at += 2 * head_width
        for i in range(pool_rows // tok):
            pool_scr[shard, i * tok : (i + 1) * tok, :] = pieces[k][:, at : at + 2 * head_width].astype(F32)
            at += 2 * head_width
        key = lax.broadcasted_iota(jnp.int32, (total, tok), 0)
        query = lax.broadcasted_iota(jnp.int32, (total, tok), 1) + (cached + shard * tok)
        last = jnp.where(key < cached, live - 1, query)
        bias_scr[:, place * tok : (place + 1) * tok] = jnp.where(key > last, NEGATIVE, 0.0)
    per_dev = pool_rows // page_size
    for j in range(page_limit):
        slot = table_ref[0, j]
        source = pl.multiple_of((slot % per_dev) * page_size, page_size)
        flat_scr[j * page_size : (j + 1) * page_size, :] = pool_scr[
            slot // per_dev, pl.ds(source, page_size), :
        ]
    flat = flat_scr[:, :head_width]
    rolled = pltpu.roll(flat, HD, 1)
    low = lax.broadcasted_iota(jnp.int32, flat.shape, 1) < HD
    zero = jnp.zeros_like(flat)
    key_scr[0] = jnp.where(low, flat, zero).astype(BF16)
    key_scr[1] = jnp.where(low, zero, rolled).astype(BF16)
    key_scr[2] = jnp.where(low, rolled, zero).astype(BF16)
    key_scr[3] = jnp.where(low, zero, flat).astype(BF16)
    value_scr[...] = flat_scr[:, head_width:].T.astype(BF16)

    def one_pair(i, carry):
        g = i // pairs
        for a in range(2):
            scores = lax.dot_general(
                key_scr[g * 2 + a], q_scr[i], (((1,), (1,)), ((), ())), preferred_element_type=F32
            )
            scores = scores + bias_scr[...]
            sink = sink_ref[own * (kv_dev * per_kv) + i * 2 + a]
            top = jnp.maximum(jnp.max(scores, axis=0, keepdims=True), sink)
            expo = jnp.exp(scores - top)
            den = jnp.sum(expo, axis=0, keepdims=True) + jnp.exp(sink - top)
            values = value_scr[pl.ds(pl.multiple_of(g * HD, HD), HD), :]
            summed = jnp.dot(values, expo.astype(BF16), preferred_element_type=F32)
            out_ref[pl.ds(pl.multiple_of((i * 2 + a) * HD, HD), HD), :] = (summed / den).astype(BF16)
        return carry

    lax.fori_loop(0, kv_dev * pairs, one_pair, 0)


def attention(pages, table, sinks, cosine, sine, pieces, kv_dev, per_kv, pool_rows, page_size):
    n_req = len(pieces)
    tok = pieces[0].shape[0]
    total = table.shape[1] * page_size + n_req * tok
    head_width = kv_dev * HD
    return pl.pallas_call(
        functools.partial(attention_kernel, kv_dev=kv_dev, per_kv=per_kv, page_size=page_size),
        out_shape=jax.ShapeDtypeStruct((per_kv * head_width, n_req * tok), BF16),
        in_specs=[smem()] * 3 + [vmem()] * (2 + n_req),
        out_specs=vmem(),
        scratch_shapes=[
            pltpu.VMEM((kv_dev * per_kv // 2, n_req * tok, 2 * HD), BF16),
            pltpu.VMEM((n_req, pool_rows, 2 * head_width), F32),
            pltpu.VMEM((total, 2 * head_width), F32),
            pltpu.VMEM((2 * kv_dev, total, head_width), BF16),
            pltpu.VMEM((head_width, total), BF16),
            pltpu.VMEM((total, n_req * tok), F32),
        ],
        compiler_params=params(),
        cost_estimate=cost(4e9, 2**22),
        name="attention",
    )(pages, table, sinks, cosine, sine, *pieces)


def pool_kernel(slots_ref, cos_ref, sin_ref, pool_ref, *rest, page_size):
    pieces, out_ref, fresh_scr = rest[:-2], rest[-2], rest[-1]
    own = lax.axis_index("req")
    tok = pieces[0].shape[0]
    kv_width = pieces[0].shape[1] // 2
    for k, piece in enumerate(pieces):
        row = pl.multiple_of(jnp.bitwise_xor(own, k) * tok, tok)
        cosine = cos_ref[pl.ds(row, tok), :]
        sine = sin_ref[pl.ds(row, tok), :]
        for col in range(0, kv_width, 128):
            turned = turn(piece[:, col : col + 128].astype(F32), cosine, sine).astype(BF16)
            fresh_scr[pl.ds(row, tok), col : col + 128] = turned
        fresh_scr[pl.ds(row, tok), kv_width:] = piece[:, kv_width:]
    out_ref[...] = pool_ref[...]
    slots_dev = out_ref.shape[0]
    for n in range(slots_ref.shape[1]):
        slot = slots_ref[0, n]

        @pl.when(slot // slots_dev == own)
        def _(slot=slot, n=n):
            out_ref[slot % slots_dev] = fresh_scr[n * page_size : (n + 1) * page_size, :]


def write_pool(slots, cosine, sine, pool, pieces):
    tok, width = pieces[0].shape
    return pl.pallas_call(
        functools.partial(pool_kernel, page_size=pool.shape[1]),
        out_shape=jax.ShapeDtypeStruct(pool.shape, BF16),
        in_specs=[smem()] + [vmem()] * (3 + len(pieces)),
        out_specs=vmem(),
        scratch_shapes=[pltpu.VMEM((tok * len(pieces), width), BF16)],
        compiler_params=params(),
        cost_estimate=cost(1e8, 2**21),
        name="write_pool",
    )(slots, cosine, sine, pool, *pieces)


def project_kernel(*refs, n_ctx, chunks):
    contexts = refs[:n_ctx]
    weights = refs[n_ctx:-2]
    send_ref, keep_ref = refs[-2:]
    half = contexts[0].shape[1] // 2
    for i in range(n_ctx):
        at = 0
        for b, count in enumerate(chunks):
            row = 0
            for _ in range(count):
                rows = weights[at].shape[0]
                terms = jnp.dot(weights[at][...], contexts[i][...], preferred_element_type=F32).astype(BF16)
                keep_ref[i, b, row : row + rows, :] = terms[:, :half]
                send_ref[i, b, row : row + rows, :] = terms[:, half:]
                row += rows
                at += 1


def project(contexts, blocks):
    depth, tokens = contexts[0].shape
    cols = sum(chunk.shape[0] for chunk in blocks[0])
    shape = jax.ShapeDtypeStruct((len(contexts), len(blocks), cols, tokens // 2), BF16)
    flat = [chunk for block in blocks for chunk in block]
    work = len(contexts) * len(blocks)
    return pl.pallas_call(
        functools.partial(project_kernel, n_ctx=len(contexts), chunks=tuple(len(b) for b in blocks)),
        out_shape=[shape, shape],
        in_specs=[vmem()] * (len(contexts) + len(flat)),
        out_specs=[vmem()] * 2,
        compiler_params=params(),
        cost_estimate=cost(work * 2 * tokens * depth * cols, 2 * depth * cols * len(blocks)),
        name="project",
    )(*contexts, *flat)


def fold_rows(cols):
    return -(-cols // 32) * 16


def pair_kernel(keep_ref, got_ref, *out_refs):
    n_ctx, blocks, cols, width = keep_ref.shape
    rows = out_refs[0].shape[1]
    tok = width // 2
    low = lax.broadcasted_iota(jnp.int32, (rows, width), 1) < tok
    for i in range(n_ctx):
        for b in range(blocks):
            both = keep_ref[i, b].astype(F32) + got_ref[i, b].astype(F32)
            top = both[:rows]
            rest = jnp.concatenate([both[rows:], jnp.zeros((2 * rows - cols, width), F32)], axis=0)
            out_refs[2 * i][b] = jnp.where(low, top, pltpu.roll(rest, tok, 1)).astype(BF16)
            out_refs[2 * i + 1][b] = jnp.where(low, pltpu.roll(top, tok, 1), rest).astype(BF16)


def pair_sum(keep, got):
    n_ctx, blocks, cols, width = keep.shape
    return pl.pallas_call(
        pair_kernel,
        out_shape=[jax.ShapeDtypeStruct((blocks, fold_rows(cols), width), BF16)] * (2 * n_ctx),
        in_specs=[vmem()] * 2,
        out_specs=[vmem()] * (2 * n_ctx),
        compiler_params=params(),
        cost_estimate=cost(1e6, 6 * keep.size),
        name="pair_sum",
    )(keep, got)


def final_kernel(hidden_ref, *rest, places):
    parts, out_ref, scr = rest[:-2], rest[-2], rest[-1]
    own = lax.axis_index("exp")
    tok, width = hidden_ref.shape
    rows = parts[0].shape[1]
    cols = width // lax.axis_size("exp")
    for (first, second), bits in zip(zip(parts[0::2], parts[1::2]), places):
        for b, bit in enumerate(bits):
            both = first[b].astype(F32) + second[b].astype(F32)
            row = pl.multiple_of(jnp.bitwise_xor(own, bit) * cols, 8)
            scr[pl.ds(row, rows), :] = both
            scr[pl.ds(row + rows, cols - rows), :] = pltpu.roll(both, tok, 1)[: cols - rows]
    attn = scr[...].T[:tok]
    out_ref[...] = (hidden_ref[...].astype(F32) + attn).astype(BF16)


def finish(hidden, parts, places):
    return pl.pallas_call(
        functools.partial(final_kernel, places=places),
        out_shape=jax.ShapeDtypeStruct(hidden.shape, BF16),
        in_specs=[vmem()] * (1 + len(parts)),
        out_specs=vmem(),
        scratch_shapes=[pltpu.VMEM((hidden.shape[1], parts[0].shape[2]), F32)],
        compiler_params=params(),
        cost_estimate=cost(1e6, 8 * hidden.size),
        name="finish",
    )(hidden, *parts)


def paired_plan(
    hidden_in, queries, new_kv, kv_pool, page_table, new_slots, cached_pages, sinks, out_weight
):
    tok = hidden_in.shape[1]
    n_req = lax.axis_size("req")
    head_count = sinks.shape[0]
    kv_width = new_kv.shape[2] // 2
    kv_heads = kv_width // HD
    slots_dev, page_size = kv_pool.shape[1:3]
    pool_rows = slots_dev * page_size
    weight = out_weight.T
    cols = weight.shape[0]
    cut = fold_rows(cols)
    far = [swap(chunk, 0, FAR_BIT) for chunk in (weight[:cut], weight[cut:])]
    near = swap(weight, 0, NEAR_BIT)
    both = [swap(chunk, 0, NEAR_BIT) for chunk in far]

    pieces = pack(queries[0], new_kv[0], kv_pool[0].reshape(pool_rows, 2 * kv_width), n_req)
    pieces = [pieces[0]] + [swap(pieces[k], k, 0) for k in range(1, n_req)]

    position = cached_pages[0] * page_size + jnp.arange(n_req * tok)
    frequency = THETA ** (-2.0 * jnp.arange(HD // 2).astype(F32) / HD)
    angles = position.astype(F32)[:, None] * frequency[None, :]
    cosine, sine = jnp.cos(angles), jnp.sin(angles)
    cosine = jnp.concatenate([cosine] * 4, axis=1)
    sine = jnp.concatenate([-sine, sine, -sine, sine], axis=1)

    ctx = attention(
        cached_pages, page_table, sinks, cosine, sine, pieces, kv_heads // n_req,
        head_count // kv_heads, pool_rows, page_size,
    )
    ctx_mate = swap(ctx, 0, PAIR_BIT)
    fresh = [new_kv[0]] + [swap(new_kv[0], k, 0) for k in range(1, n_req)]
    pool_out = write_pool(new_slots, cosine, sine, kv_pool[0], fresh)

    early = [[weight], [near], far]
    late = [both]
    parts = []
    send, keep = project([ctx], early)
    own_a, over_y = pair_sum(keep, swap(send, 1, 0))
    parts += [own_a, swap(over_y, 2, 0)]
    send, keep = project([ctx_mate], early)
    over_pair, over_both = pair_sum(keep, swap(send, 1, 0))
    parts += [swap(over_pair, 0, PAIR_BIT), swap(over_both, 2, PAIR_BIT)]
    send, keep = project([ctx, ctx_mate], late)
    own_c, over_y, over_pair, over_both = pair_sum(keep, swap(send, 1, 0))
    parts += [own_c, swap(over_y, 2, 0), swap(over_pair, 0, PAIR_BIT), swap(over_both, 2, PAIR_BIT)]
    early_bits = (0, NEAR_BIT, FAR_BIT)
    late_bits = (NEAR_BIT ^ FAR_BIT,)
    places = (
        early_bits,
        tuple(PAIR_BIT ^ b for b in early_bits),
        late_bits,
        tuple(PAIR_BIT ^ b for b in late_bits),
    )
    layer_out = finish(hidden_in[0], parts, places)
    return (layer_out[None], pool_out[None])


def solution(mesh):
    paired = mesh.shape["req"] == 4 and mesh.shape["exp"] == 8
    return jax.shard_map(
        paired_plan if paired else general_plan,
        mesh=mesh,
        in_specs=(
            P("exp", "req", None),
            P("exp", "req", None),
            P("exp", "req", None),
            P("exp", "req", None, None),
            P("exp", None),
            P("exp", None),
            P("exp"),
            P(),
            P("req", "exp"),
        ),
        out_specs=(P("exp", "req", None), P("exp", "req", None, None)),
        check_vma=False,
    )
```

```python
import functools
import math

import jax
import jax.numpy as jnp
from jax import lax
from jax.experimental import pallas as pl
from jax.experimental.pallas import tpu as pltpu
from jax.sharding import PartitionSpec as P

HD = 64


THETA = 150000.0
NEGATIVE = -1e30


def rotate(values, positions):
    half_width = values.shape[-1] // 2
    frequency = THETA ** (-2.0 * jnp.arange(half_width).astype(jnp.float32) / values.shape[-1])
    angles = positions.astype(jnp.float32)[:, None] * frequency[None, :]
    cosine = jnp.cos(angles)[:, None, :]
    sine_part = jnp.sin(angles)[:, None, :]
    lower_half = values[..., :half_width]
    upper_half = values[..., half_width:]
    return jnp.concatenate(
        [
            lower_half * cosine - upper_half * sine_part,
            upper_half * cosine + lower_half * sine_part,
        ],
        axis=-1,
    )


def spread_heads(rows, head_total, kv_heads, dev_count):
    per_dev = head_total // dev_count
    per_kv = head_total // kv_heads
    repeat = max(1, per_kv // per_dev)
    kv_dev = max(1, per_dev // per_kv)
    count = rows.shape[0]
    split = jnp.repeat(rows.reshape(count, 2, kv_heads, HD), repeat, axis=2)
    split = split.reshape(count, 2, dev_count, kv_dev * HD)
    return jnp.transpose(split, (0, 2, 1, 3)).reshape(count, dev_count, 2 * kv_dev * HD)


def general_plan(
    hidden_in, queries, new_kv, kv_pool, page_table, new_slots, cached_pages, sinks, out_weight
):
    tok_dev = hidden_in.shape[1]
    n_req = lax.axis_size("req")
    own_index = lax.axis_index("req")
    fresh_count = tok_dev * n_req
    head_count = sinks.shape[0]
    kv_width = new_kv.shape[2] // 2
    kv_heads = kv_width // HD
    per_kv = head_count // kv_heads
    heads_dev = head_count // n_req
    kv_dev = max(1, heads_dev // per_kv)
    per_dev_group = heads_dev // kv_dev
    head_width = 2 * kv_dev * HD
    slots_dev = kv_pool.shape[1]
    page_size = kv_pool.shape[2]
    slot_total = slots_dev * n_req
    page_limit = page_table.shape[1]
    fresh_pages = new_slots.shape[1]
    page_count = cached_pages[0]
    start_pos = page_count * page_size
    own_pos = start_pos + own_index * tok_dev + jnp.arange(tok_dev)
    q_rot = rotate(queries[0].reshape(tok_dev, head_count, HD).astype(jnp.float32), own_pos).astype(
        jnp.bfloat16
    )
    k_rot = rotate(
        new_kv[0, :, :kv_width].reshape(tok_dev, kv_heads, HD).astype(jnp.float32), own_pos
    ).astype(jnp.bfloat16)
    kv_rot = jnp.concatenate([k_rot.reshape(tok_dev, kv_width), new_kv[0, :, kv_width:]], axis=1)
    slot_all = jnp.arange(slot_total)
    page_index = jnp.arange(page_limit)
    cached_hit = (page_table[0][None, :] == slot_all[:, None]) & (page_index[None, :] < page_count)
    is_cached = jnp.any(cached_hit, axis=1)
    cached_base = jnp.sum(jnp.where(cached_hit, page_index[None, :], 0), axis=1) * page_size
    fresh_hit = new_slots[0][None, :] == slot_all[:, None]
    is_fresh = jnp.any(fresh_hit, axis=1)
    fresh_base = (
        start_pos
        + jnp.sum(jnp.where(fresh_hit, jnp.arange(fresh_pages)[None, :], 0), axis=1) * page_size
    )
    key_pos = (
        jnp.where(is_fresh, fresh_base, cached_base)[:, None] + jnp.arange(page_size)[None, :]
    ).reshape(-1)
    key_live = jnp.repeat(is_cached | is_fresh, page_size)
    all_fresh = lax.all_gather(kv_rot, "req", axis=0, tiled=True)
    own_hit = lax.dynamic_slice_in_dim(fresh_hit, own_index * slots_dev, slots_dev, 0)
    own_fresh = lax.dynamic_slice_in_dim(is_fresh, own_index * slots_dev, slots_dev, 0)
    appended = jnp.dot(
        own_hit.astype(jnp.bfloat16),
        all_fresh.reshape(fresh_pages, page_size * 2 * kv_width),
        preferred_element_type=jnp.float32,
    )
    appended = appended.astype(jnp.bfloat16).reshape(slots_dev, page_size, 2 * kv_width)
    local_pages = jnp.where(own_fresh[:, None, None], appended, kv_pool[0])
    head_pool = lax.all_to_all(
        spread_heads(
            local_pages.reshape(slots_dev * page_size, 2 * kv_width), head_count, kv_heads, n_req
        ),
        "req",
        split_axis=1,
        concat_axis=0,
        tiled=True,
    )
    head_pool = head_pool.reshape(slot_total * page_size, head_width)
    q_here = lax.all_to_all(
        q_rot.reshape(tok_dev, n_req, heads_dev * HD),
        "req",
        split_axis=1,
        concat_axis=0,
        tiled=True,
    )
    q_here = q_here.reshape(fresh_count, heads_dev * HD)
    key_total = slot_total * page_size
    all_keys = head_pool[:, : kv_dev * HD].reshape(key_total, kv_dev, HD)
    all_values = head_pool[:, kv_dev * HD :].reshape(key_total, kv_dev, HD)
    sink_mine = lax.dynamic_slice_in_dim(sinks, own_index * heads_dev, heads_dev, 0).reshape(
        kv_dev, per_dev_group
    )
    scale = 1.0 / math.sqrt(HD)
    query_block = math.gcd(fresh_count, 128)
    contexts = []
    for block_start in range(0, fresh_count, query_block):
        block_queries = q_here[block_start : block_start + query_block].reshape(
            query_block, kv_dev, per_dev_group, HD
        )
        query_pos = start_pos + block_start + jnp.arange(query_block)
        visible = key_live[None, :] & (key_pos[None, :] <= query_pos[:, None])
        scores = (
            jnp.einsum(
                "tghd,kgd->tghk", block_queries, all_keys, preferred_element_type=jnp.float32
            )
            * scale
        )
        scores = jnp.where(visible[:, None, None, :], scores, NEGATIVE)
        top_score = jnp.maximum(jnp.max(scores, axis=-1), sink_mine[None])
        expo = jnp.where(visible[:, None, None, :], jnp.exp(scores - top_score[..., None]), 0.0)
        denominator = jnp.sum(expo, axis=-1) + jnp.exp(sink_mine[None] - top_score)
        weighted = jnp.einsum(
            "tghk,kgd->tghd",
            expo.astype(jnp.bfloat16),
            all_values,
            preferred_element_type=jnp.float32,
        )
        contexts.append(
            (weighted / denominator[..., None])
            .astype(jnp.bfloat16)
            .reshape(query_block, heads_dev * HD)
        )
    context = jnp.concatenate(contexts, axis=0)
    terms = jnp.dot(
        context,
        lax.all_gather(out_weight, "exp", axis=1, tiled=True),
        preferred_element_type=jnp.float32,
    ).astype(jnp.bfloat16)
    width = terms.shape[1]
    arrived = lax.all_to_all(
        terms.reshape(n_req, tok_dev, width), "req", split_axis=0, concat_axis=0, tiled=True
    )
    attn = jnp.sum(arrived.astype(jnp.float32), axis=0)
    layer_out = (hidden_in[0].astype(jnp.float32) + attn).astype(jnp.bfloat16)
    return (layer_out[None], local_pages[None])


VMEM_LIMIT = 24 * 1024 * 1024
F32 = jnp.float32
BF16 = jnp.bfloat16

PAIR_BIT, NEAR_BIT, FAR_BIT = 2, 1, 6
OUTER, INNER = (0, 1, 6, 7), (2, 3, 4, 5)
ORDER = (0, 2, 1, 3)


def vmem():
    return pl.BlockSpec(memory_space=pltpu.VMEM)


def smem():
    return pl.BlockSpec(memory_space=pltpu.SMEM)


def params():
    return pltpu.CompilerParams(vmem_limit_bytes=VMEM_LIMIT)


def cost(flops, nbytes):
    return pl.CostEstimate(flops=int(flops), bytes_accessed=int(nbytes), transcendentals=0)


def swap(values, req_bits, exp_bits, among=None):
    if not exp_bits:
        return lax.ppermute(values, "req", [(i, i ^ req_bits) for i in range(lax.axis_size("req"))])
    if not req_bits:
        among = range(lax.axis_size("exp")) if among is None else among
        return lax.ppermute(values, "exp", [(i, i ^ exp_bits) for i in among])
    rows, cols = lax.axis_size("req"), lax.axis_size("exp")
    pairs = [
        (i * cols + j, (i ^ req_bits) * cols + (j ^ exp_bits)) for i in range(rows) for j in range(cols)
    ]
    return lax.ppermute(values, ("req", "exp"), pairs)


def pack_kernel(q_ref, kv_ref, pool_ref, *rest):
    outs, sems = rest[:-1], rest[-1]
    n_req = len(outs)
    own = lax.axis_index("req")
    tok = q_ref.shape[0]
    q_width = q_ref.shape[1] // n_req
    kv_width = kv_ref.shape[1] // 2
    head_width = kv_width // n_req
    copies = []

    def copy(source, target):
        copies.append(pltpu.make_async_copy(source, target, sems.at[len(copies)]))
        copies[-1].start()

    for k in (3, 2, 1, 0):
        out = outs[k]
        dest = jnp.bitwise_xor(own, k)
        col = pl.multiple_of(dest * q_width, 128)
        copy(q_ref.at[:, pl.ds(col, q_width)], out.at[:, pl.ds(0, q_width)])
        at = q_width
        blocks = [(kv_ref, 0)]
        blocks += [(pool_ref, i * tok) for i in range(pool_ref.shape[0] // tok)]
        for block, row in blocks:
            for half in range(2):
                col = pl.multiple_of(half * kv_width + dest * head_width, 128)
                copy(
                    block.at[pl.ds(row, tok), pl.ds(col, head_width)],
                    out.at[:, pl.ds(at, head_width)],
                )
                at += head_width
        if k == 1:
            copy(kv_ref, out.at[:, pl.ds(at, 2 * kv_width)])
    for one in copies:
        one.wait()


def pack(q, kv, pool, n_req):
    tok = q.shape[0]
    blocks = 1 + pool.shape[0] // tok
    width = (q.shape[1] + blocks * kv.shape[1]) // n_req
    widths = [width + (kv.shape[1] if k == 1 else 0) for k in range(n_req)]
    return pl.pallas_call(
        pack_kernel,
        out_shape=[jax.ShapeDtypeStruct((tok, w), BF16) for w in widths],
        in_specs=[pl.BlockSpec(memory_space=pltpu.MemorySpace.HBM)] * 3,
        out_specs=[vmem()] * n_req,
        scratch_shapes=[pltpu.SemaphoreType.DMA((n_req * (1 + 2 * blocks) + 1,))],
        compiler_params=params(),
        cost_estimate=cost(0, 4 * tok * width * n_req),
        name="pack",
    )(q, kv, pool)


def turn(values, cosine, sine):
    lane = lax.broadcasted_iota(jnp.int32, values.shape, 1)
    other = jnp.where(lane % HD < HD // 2, pltpu.roll(values, 128 - HD // 2, 1), pltpu.roll(values, HD // 2, 1))
    return values * cosine + other * sine


def attention_kernel(
    pages_ref, table_ref, sink_ref, cos_ref, sin_ref, *rest, kv_dev, per_kv, page_size
):
    n_req = len(rest) - 7
    pieces, out_ref = rest[:n_req], rest[n_req]
    q_scr, pool_scr, flat_scr, key_scr, value_scr, bias_scr = rest[n_req + 1 :]
    own = lax.axis_index("req")
    tok = pieces[0].shape[0]
    q_width = kv_dev * per_kv * HD
    head_width = kv_dev * HD
    page_limit = table_ref.shape[1]
    cached = page_limit * page_size
    fresh = tok * n_req
    total = cached + fresh
    pool_rows = pool_scr.shape[1]
    live = pages_ref[0] * page_size
    pairs = per_kv // 2
    for place, k in enumerate(ORDER):
        shard = jnp.bitwise_xor(own, k)
        row = pl.multiple_of(shard * tok, tok)
        cosine = cos_ref[pl.ds(row, tok), :]
        sine = sin_ref[pl.ds(row, tok), :]
        for p in range(kv_dev * pairs):
            col = p * 2 * HD
            turned = turn(pieces[k][:, col : col + 2 * HD].astype(F32), cosine, sine).astype(BF16)
            q_scr[p, place * tok : (place + 1) * tok, :] = turned * jnp.asarray(1.0 / math.sqrt(HD), BF16)
        at = q_width
        key_row = pl.multiple_of(cached + row, tok)
        flat_scr[pl.ds(key_row, tok), :head_width] = turn(
            pieces[k][:, at : at + head_width].astype(F32), cosine, sine
        )
        flat_scr[pl.ds(key_row, tok), head_width:] = pieces[k][
            :, at + head_width : at + 2 * head_width
        ].astype(F32)
        at += 2 * head_width
        for i in range(pool_rows // tok):
            pool_scr[shard, i * tok : (i + 1) * tok, :] = pieces[k][:, at : at + 2 * head_width].astype(F32)
            at += 2 * head_width
        key = lax.broadcasted_iota(jnp.int32, (total, tok), 0)
        query = lax.broadcasted_iota(jnp.int32, (total, tok), 1) + (cached + shard * tok)
        last = jnp.where(key < cached, live - 1, query)
        bias_scr[:, place * tok : (place + 1) * tok] = jnp.where(key > last, NEGATIVE, 0.0)
    per_dev = pool_rows // page_size
    for j in range(page_limit):
        slot = table_ref[0, j]
        source = pl.multiple_of((slot % per_dev) * page_size, page_size)
        flat_scr[j * page_size : (j + 1) * page_size, :] = pool_scr[
            slot // per_dev, pl.ds(source, page_size), :
        ]
    flat = flat_scr[:, :head_width]
    rolled = pltpu.roll(flat, HD, 1)
    low = lax.broadcasted_iota(jnp.int32, flat.shape, 1) < HD
    zero = jnp.zeros_like(flat)
    key_scr[0] = jnp.where(low, flat, zero).astype(BF16)
    key_scr[1] = jnp.where(low, zero, rolled).astype(BF16)
    key_scr[2] = jnp.where(low, rolled, zero).astype(BF16)
    key_scr[3] = jnp.where(low, zero, flat).astype(BF16)
    value_scr[...] = flat_scr[:, head_width:].T.astype(BF16)

    def one_pair(i, carry):
        g = i // pairs
        for a in range(2):
            scores = lax.dot_general(
                key_scr[g * 2 + a], q_scr[i], (((1,), (1,)), ((), ())), preferred_element_type=F32
            )
            scores = scores + bias_scr[...]
            sink = sink_ref[own * (kv_dev * per_kv) + i * 2 + a]
            top = jnp.maximum(jnp.max(scores, axis=0, keepdims=True), sink)
            expo = jnp.exp(scores - top)
            den = jnp.sum(expo, axis=0, keepdims=True) + jnp.exp(sink - top)
            values = value_scr[pl.ds(pl.multiple_of(g * HD, HD), HD), :]
            summed = jnp.dot(values, expo.astype(BF16), preferred_element_type=F32)
            out_ref[pl.ds(pl.multiple_of((i * 2 + a) * HD, HD), HD), :] = (summed / den).astype(BF16)
        return carry

    lax.fori_loop(0, kv_dev * pairs, one_pair, 0)


def attention(pages, table, sinks, cosine, sine, pieces, kv_dev, per_kv, pool_rows, page_size):
    n_req = len(pieces)
    tok = pieces[0].shape[0]
    total = table.shape[1] * page_size + n_req * tok
    head_width = kv_dev * HD
    return pl.pallas_call(
        functools.partial(attention_kernel, kv_dev=kv_dev, per_kv=per_kv, page_size=page_size),
        out_shape=jax.ShapeDtypeStruct((per_kv * head_width, n_req * tok), BF16),
        in_specs=[smem()] * 3 + [vmem()] * (2 + n_req),
        out_specs=vmem(),
        scratch_shapes=[
            pltpu.VMEM((kv_dev * per_kv // 2, n_req * tok, 2 * HD), BF16),
            pltpu.VMEM((n_req, pool_rows, 2 * head_width), F32),
            pltpu.VMEM((total, 2 * head_width), F32),
            pltpu.VMEM((2 * kv_dev, total, head_width), BF16),
            pltpu.VMEM((head_width, total), BF16),
            pltpu.VMEM((total, n_req * tok), F32),
        ],
        compiler_params=params(),
        cost_estimate=cost(4e9, 2**22),
        name="attention",
    )(pages, table, sinks, cosine, sine, *pieces)


def pool_kernel(slots_ref, cos_ref, sin_ref, pool_ref, *rest, page_size):
    pairs, out_ref, fresh_scr = rest[:-2], rest[-2], rest[-1]
    own = lax.axis_index("req")
    tok = pairs[0].shape[0] // 2
    kv_width = pairs[0].shape[1] // 2
    for k in range(2 * len(pairs)):
        piece = pairs[k // 2][k % 2 * tok : (k % 2 + 1) * tok, :]
        row = pl.multiple_of(jnp.bitwise_xor(own, k) * tok, tok)
        cosine = cos_ref[pl.ds(row, tok), :]
        sine = sin_ref[pl.ds(row, tok), :]
        for col in range(0, kv_width, 128):
            turned = turn(piece[:, col : col + 128].astype(F32), cosine, sine).astype(BF16)
            fresh_scr[pl.ds(row, tok), col : col + 128] = turned
        fresh_scr[pl.ds(row, tok), kv_width:] = piece[:, kv_width:]
    out_ref[...] = pool_ref[...]
    slots_dev = out_ref.shape[0]
    for n in range(slots_ref.shape[1]):
        slot = slots_ref[0, n]

        @pl.when(slot // slots_dev == own)
        def _(slot=slot, n=n):
            out_ref[slot % slots_dev] = fresh_scr[n * page_size : (n + 1) * page_size, :]


def write_pool(slots, cosine, sine, pool, pairs):
    rows, width = pairs[0].shape
    return pl.pallas_call(
        functools.partial(pool_kernel, page_size=pool.shape[1]),
        out_shape=jax.ShapeDtypeStruct(pool.shape, BF16),
        in_specs=[smem()] + [vmem()] * (3 + len(pairs)),
        out_specs=vmem(),
        scratch_shapes=[pltpu.VMEM((rows * len(pairs), width), BF16)],
        compiler_params=params(),
        cost_estimate=cost(1e8, 2**21),
        name="write_pool",
    )(slots, cosine, sine, pool, *pairs)


def project_kernel(*refs, n_ctx, counts):
    contexts = refs[:n_ctx]
    weights = refs[n_ctx:-2]
    send_ref, keep_ref = refs[-2:]
    half = contexts[0].shape[1] // 2
    at = 0
    for b, count in enumerate(counts):
        whole, pieces = weights[at], weights[at + 1 : at + count]
        at += count
        row = 0
        for piece in pieces or (whole,):
            rows = slice(row, row + piece.shape[0])
            block = whole[rows, :] + piece[...] if pieces else whole[...]
            for i in range(n_ctx):
                terms = jnp.dot(block, contexts[i][...], preferred_element_type=F32).astype(BF16)
                keep_ref[i, b, rows, :] = terms[:, :half]
                send_ref[i, b, rows, :] = terms[:, half:]
            row += piece.shape[0]


def project(contexts, blocks):
    depth, tokens = contexts[0].shape
    cols = blocks[0][0].shape[0]
    shape = jax.ShapeDtypeStruct((len(contexts), len(blocks), cols, tokens // 2), BF16)
    flat = [chunk for block in blocks for chunk in block]
    work = len(contexts) * len(blocks)
    return pl.pallas_call(
        functools.partial(project_kernel, n_ctx=len(contexts), counts=tuple(len(b) for b in blocks)),
        out_shape=[shape, shape],
        in_specs=[vmem()] * (len(contexts) + len(flat)),
        out_specs=[vmem()] * 2,
        compiler_params=params(),
        cost_estimate=cost(work * 2 * tokens * depth * cols, 2 * depth * cols * len(blocks)),
        name="project",
    )(*contexts, *flat)


def fold_rows(cols):
    return -(-cols // 32) * 16


def pair_kernel(keep_ref, got_ref, *out_refs):
    n_ctx, blocks, cols, width = keep_ref.shape
    rows = out_refs[0].shape[1]
    tok = width // 2
    low = lax.broadcasted_iota(jnp.int32, (rows, width), 1) < tok
    for i in range(n_ctx):
        for b in range(blocks):
            both = keep_ref[i, b].astype(F32) + got_ref[i, b].astype(F32)
            top = both[:rows]
            rest = jnp.concatenate([both[rows:], jnp.zeros((2 * rows - cols, width), F32)], axis=0)
            out_refs[2 * i][b] = jnp.where(low, top, pltpu.roll(rest, tok, 1)).astype(BF16)
            out_refs[2 * i + 1][b] = jnp.where(low, pltpu.roll(top, tok, 1), rest).astype(BF16)


def pair_sum(keep, got):
    n_ctx, blocks, cols, width = keep.shape
    return pl.pallas_call(
        pair_kernel,
        out_shape=[jax.ShapeDtypeStruct((blocks, fold_rows(cols), width), BF16)] * (2 * n_ctx),
        in_specs=[vmem()] * 2,
        out_specs=[vmem()] * (2 * n_ctx),
        compiler_params=params(),
        cost_estimate=cost(1e6, 6 * keep.size),
        name="pair_sum",
    )(keep, got)


def final_kernel(hidden_ref, *rest, places):
    parts, out_ref, scr = rest[:-2], rest[-2], rest[-1]
    own = lax.axis_index("exp")
    tok, width = hidden_ref.shape
    rows = parts[0].shape[1]
    cols = width // lax.axis_size("exp")
    for (first, second), bits in zip(zip(parts[0::2], parts[1::2]), places):
        for b, bit in enumerate(bits):
            both = first[b].astype(F32) + second[b].astype(F32)
            row = pl.multiple_of(jnp.bitwise_xor(own, bit) * cols, 8)
            scr[pl.ds(row, rows), :] = both
            scr[pl.ds(row + rows, cols - rows), :] = pltpu.roll(both, tok, 1)[: cols - rows]
    attn = scr[...].T[:tok]
    out_ref[...] = (hidden_ref[...].astype(F32) + attn).astype(BF16)


def finish(hidden, parts, places):
    return pl.pallas_call(
        functools.partial(final_kernel, places=places),
        out_shape=jax.ShapeDtypeStruct(hidden.shape, BF16),
        in_specs=[vmem()] * (1 + len(parts)),
        out_specs=vmem(),
        scratch_shapes=[pltpu.VMEM((hidden.shape[1], parts[0].shape[2]), F32)],
        compiler_params=params(),
        cost_estimate=cost(1e6, 8 * hidden.size),
        name="finish",
    )(hidden, *parts)


def paired_plan(
    hidden_in, queries, new_kv, kv_pool, page_table, new_slots, cached_pages, sinks, out_weight
):
    tok = hidden_in.shape[1]
    n_req = lax.axis_size("req")
    head_count = sinks.shape[0]
    kv_width = new_kv.shape[2] // 2
    kv_heads = kv_width // HD
    slots_dev, page_size = kv_pool.shape[1:3]
    pool_rows = slots_dev * page_size
    weight = out_weight.T
    cols = weight.shape[0]
    cut = fold_rows(cols)
    outer = swap(weight, 0, FAR_BIT, OUTER)
    near = swap(weight, 0, NEAR_BIT)

    pieces = pack(queries[0], new_kv[0], kv_pool[0].reshape(pool_rows, 2 * kv_width), n_req)
    pieces = [pieces[0]] + [swap(pieces[k], k, 0) for k in range(1, n_req)]
    pieces, weight_late = lax.optimization_barrier((pieces, weight))
    inner = [swap(chunk, 0, FAR_BIT, INNER) for chunk in (weight_late[:cut], weight_late[cut:])]

    position = cached_pages[0] * page_size + jnp.arange(n_req * tok)
    frequency = THETA ** (-2.0 * jnp.arange(HD // 2).astype(F32) / HD)
    angles = position.astype(F32)[:, None] * frequency[None, :]
    cosine, sine = jnp.cos(angles), jnp.sin(angles)
    cosine = jnp.concatenate([cosine] * 4, axis=1)
    sine = jnp.concatenate([-sine, sine, -sine, sine], axis=1)

    ctx = attention(
        cached_pages, page_table, sinks, cosine, sine, pieces, kv_heads // n_req,
        head_count // kv_heads, pool_rows, page_size,
    )
    chip_rows = jnp.concatenate([new_kv[0], pieces[1][:, -2 * kv_width :]], axis=0)
    ctx, outer, near, chip_rows = lax.optimization_barrier((ctx, outer, near, chip_rows))
    ctx_mate = swap(ctx, 0, PAIR_BIT)
    outer_both = swap(outer, 0, NEAR_BIT, OUTER)
    inner_both = [swap(chunk, 0, NEAR_BIT, INNER) for chunk in inner]
    far = [outer, *inner]
    both = [outer_both, *inner_both]
    pool_out = write_pool(new_slots, cosine, sine, kv_pool[0], [chip_rows, swap(chip_rows, 2, 0)])

    ctx, pool_out = lax.optimization_barrier((ctx, pool_out))
    early = [[weight], [near], far]
    late = [both]
    parts = []
    send, keep = project([ctx], early)
    own_a, over_y = pair_sum(keep, swap(send, 1, 0))
    parts += [own_a, swap(over_y, 2, 0)]
    send, keep = project([ctx_mate], early)
    over_pair, over_both = pair_sum(keep, swap(send, 1, 0))
    parts += [swap(over_pair, 0, PAIR_BIT), swap(over_both, 2, PAIR_BIT)]
    send, keep = project([ctx, ctx_mate], late)
    own_c, over_y, over_pair, over_both = pair_sum(keep, swap(send, 1, 0))
    parts += [own_c, swap(over_y, 2, 0), swap(over_pair, 0, PAIR_BIT), swap(over_both, 2, PAIR_BIT)]
    early_bits = (0, NEAR_BIT, FAR_BIT)
    late_bits = (NEAR_BIT ^ FAR_BIT,)
    places = (
        early_bits,
        tuple(PAIR_BIT ^ b for b in early_bits),
        late_bits,
        tuple(PAIR_BIT ^ b for b in late_bits),
    )
    layer_out = finish(hidden_in[0], parts, places)
    return (layer_out[None], pool_out[None])


def solution(mesh):
    paired = mesh.shape["req"] == 4 and mesh.shape["exp"] == 8
    return jax.shard_map(
        paired_plan if paired else general_plan,
        mesh=mesh,
        in_specs=(
            P("exp", "req", None),
            P("exp", "req", None),
            P("exp", "req", None),
            P("exp", "req", None, None),
            P("exp", None),
            P("exp", None),
            P("exp"),
            P(),
            P("req", "exp"),
        ),
        out_specs=(P("exp", "req", None), P("exp", "req", None, None)),
        check_vma=False,
    )
```

```python
import functools
import math

import jax
import jax.numpy as jnp
from jax import lax
from jax.experimental import pallas as pl
from jax.experimental.pallas import tpu as pltpu
from jax.sharding import PartitionSpec as P

HD = 64


THETA = 150000.0
NEGATIVE = -1e30


def rotate(values, positions):
    half_width = values.shape[-1] // 2
    frequency = THETA ** (-2.0 * jnp.arange(half_width).astype(jnp.float32) / values.shape[-1])
    angles = positions.astype(jnp.float32)[:, None] * frequency[None, :]
    cosine = jnp.cos(angles)[:, None, :]
    sine_part = jnp.sin(angles)[:, None, :]
    lower_half = values[..., :half_width]
    upper_half = values[..., half_width:]
    return jnp.concatenate(
        [
            lower_half * cosine - upper_half * sine_part,
            upper_half * cosine + lower_half * sine_part,
        ],
        axis=-1,
    )


def spread_heads(rows, head_total, kv_heads, dev_count):
    per_dev = head_total // dev_count
    per_kv = head_total // kv_heads
    repeat = max(1, per_kv // per_dev)
    kv_dev = max(1, per_dev // per_kv)
    count = rows.shape[0]
    split = jnp.repeat(rows.reshape(count, 2, kv_heads, HD), repeat, axis=2)
    split = split.reshape(count, 2, dev_count, kv_dev * HD)
    return jnp.transpose(split, (0, 2, 1, 3)).reshape(count, dev_count, 2 * kv_dev * HD)


def general_plan(
    hidden_in, queries, new_kv, kv_pool, page_table, new_slots, cached_pages, sinks, out_weight
):
    tok_dev = hidden_in.shape[1]
    n_req = lax.axis_size("req")
    own_index = lax.axis_index("req")
    fresh_count = tok_dev * n_req
    head_count = sinks.shape[0]
    kv_width = new_kv.shape[2] // 2
    kv_heads = kv_width // HD
    per_kv = head_count // kv_heads
    heads_dev = head_count // n_req
    kv_dev = max(1, heads_dev // per_kv)
    per_dev_group = heads_dev // kv_dev
    head_width = 2 * kv_dev * HD
    slots_dev = kv_pool.shape[1]
    page_size = kv_pool.shape[2]
    slot_total = slots_dev * n_req
    page_limit = page_table.shape[1]
    fresh_pages = new_slots.shape[1]
    page_count = cached_pages[0]
    start_pos = page_count * page_size
    own_pos = start_pos + own_index * tok_dev + jnp.arange(tok_dev)
    q_rot = rotate(queries[0].reshape(tok_dev, head_count, HD).astype(jnp.float32), own_pos).astype(
        jnp.bfloat16
    )
    k_rot = rotate(
        new_kv[0, :, :kv_width].reshape(tok_dev, kv_heads, HD).astype(jnp.float32), own_pos
    ).astype(jnp.bfloat16)
    kv_rot = jnp.concatenate([k_rot.reshape(tok_dev, kv_width), new_kv[0, :, kv_width:]], axis=1)
    slot_all = jnp.arange(slot_total)
    page_index = jnp.arange(page_limit)
    cached_hit = (page_table[0][None, :] == slot_all[:, None]) & (page_index[None, :] < page_count)
    is_cached = jnp.any(cached_hit, axis=1)
    cached_base = jnp.sum(jnp.where(cached_hit, page_index[None, :], 0), axis=1) * page_size
    fresh_hit = new_slots[0][None, :] == slot_all[:, None]
    is_fresh = jnp.any(fresh_hit, axis=1)
    fresh_base = (
        start_pos
        + jnp.sum(jnp.where(fresh_hit, jnp.arange(fresh_pages)[None, :], 0), axis=1) * page_size
    )
    key_pos = (
        jnp.where(is_fresh, fresh_base, cached_base)[:, None] + jnp.arange(page_size)[None, :]
    ).reshape(-1)
    key_live = jnp.repeat(is_cached | is_fresh, page_size)
    all_fresh = lax.all_gather(kv_rot, "req", axis=0, tiled=True)
    own_hit = lax.dynamic_slice_in_dim(fresh_hit, own_index * slots_dev, slots_dev, 0)
    own_fresh = lax.dynamic_slice_in_dim(is_fresh, own_index * slots_dev, slots_dev, 0)
    appended = jnp.dot(
        own_hit.astype(jnp.bfloat16),
        all_fresh.reshape(fresh_pages, page_size * 2 * kv_width),
        preferred_element_type=jnp.float32,
    )
    appended = appended.astype(jnp.bfloat16).reshape(slots_dev, page_size, 2 * kv_width)
    local_pages = jnp.where(own_fresh[:, None, None], appended, kv_pool[0])
    head_pool = lax.all_to_all(
        spread_heads(
            local_pages.reshape(slots_dev * page_size, 2 * kv_width), head_count, kv_heads, n_req
        ),
        "req",
        split_axis=1,
        concat_axis=0,
        tiled=True,
    )
    head_pool = head_pool.reshape(slot_total * page_size, head_width)
    q_here = lax.all_to_all(
        q_rot.reshape(tok_dev, n_req, heads_dev * HD),
        "req",
        split_axis=1,
        concat_axis=0,
        tiled=True,
    )
    q_here = q_here.reshape(fresh_count, heads_dev * HD)
    key_total = slot_total * page_size
    all_keys = head_pool[:, : kv_dev * HD].reshape(key_total, kv_dev, HD)
    all_values = head_pool[:, kv_dev * HD :].reshape(key_total, kv_dev, HD)
    sink_mine = lax.dynamic_slice_in_dim(sinks, own_index * heads_dev, heads_dev, 0).reshape(
        kv_dev, per_dev_group
    )
    scale = 1.0 / math.sqrt(HD)
    query_block = math.gcd(fresh_count, 128)
    contexts = []
    for block_start in range(0, fresh_count, query_block):
        block_queries = q_here[block_start : block_start + query_block].reshape(
            query_block, kv_dev, per_dev_group, HD
        )
        query_pos = start_pos + block_start + jnp.arange(query_block)
        visible = key_live[None, :] & (key_pos[None, :] <= query_pos[:, None])
        scores = (
            jnp.einsum(
                "tghd,kgd->tghk", block_queries, all_keys, preferred_element_type=jnp.float32
            )
            * scale
        )
        scores = jnp.where(visible[:, None, None, :], scores, NEGATIVE)
        top_score = jnp.maximum(jnp.max(scores, axis=-1), sink_mine[None])
        expo = jnp.where(visible[:, None, None, :], jnp.exp(scores - top_score[..., None]), 0.0)
        denominator = jnp.sum(expo, axis=-1) + jnp.exp(sink_mine[None] - top_score)
        weighted = jnp.einsum(
            "tghk,kgd->tghd",
            expo.astype(jnp.bfloat16),
            all_values,
            preferred_element_type=jnp.float32,
        )
        contexts.append(
            (weighted / denominator[..., None])
            .astype(jnp.bfloat16)
            .reshape(query_block, heads_dev * HD)
        )
    context = jnp.concatenate(contexts, axis=0)
    terms = jnp.dot(
        context,
        lax.all_gather(out_weight, "exp", axis=1, tiled=True),
        preferred_element_type=jnp.float32,
    ).astype(jnp.bfloat16)
    width = terms.shape[1]
    arrived = lax.all_to_all(
        terms.reshape(n_req, tok_dev, width), "req", split_axis=0, concat_axis=0, tiled=True
    )
    attn = jnp.sum(arrived.astype(jnp.float32), axis=0)
    layer_out = (hidden_in[0].astype(jnp.float32) + attn).astype(jnp.bfloat16)
    return (layer_out[None], local_pages[None])


VMEM_LIMIT = 24 * 1024 * 1024
FREE = pl.CostEstimate(flops=0, bytes_accessed=0, transcendentals=0)
F32 = jnp.float32
BF16 = jnp.bfloat16

PAIR_BIT, NEAR_BIT, FAR_BIT = 2, 1, 6
ORDER = (0, 2, 1, 3)


def vmem():
    return pl.BlockSpec(memory_space=pltpu.VMEM)


def smem():
    return pl.BlockSpec(memory_space=pltpu.SMEM)


def params():
    return pltpu.CompilerParams(vmem_limit_bytes=VMEM_LIMIT)


def swap(values, req_bits, exp_bits):
    if not exp_bits:
        return lax.ppermute(values, "req", [(i, i ^ req_bits) for i in range(lax.axis_size("req"))])
    if not req_bits:
        return lax.ppermute(values, "exp", [(i, i ^ exp_bits) for i in range(lax.axis_size("exp"))])
    rows, cols = lax.axis_size("req"), lax.axis_size("exp")
    pairs = [
        (i * cols + j, (i ^ req_bits) * cols + (j ^ exp_bits)) for i in range(rows) for j in range(cols)
    ]
    return lax.ppermute(values, ("req", "exp"), pairs)


def is_inner(index):
    return (index & 2) * 2 != (index & 4)


def swap_blocks(values, inner_bits, outer_bits):
    pairs = [(i, i ^ (inner_bits if is_inner(i) else outer_bits)) for i in range(lax.axis_size("exp"))]
    return lax.ppermute(values, "exp", pairs)


def pack_kernel(q_ref, kv_ref, pool_ref, *rest):
    outs, sems = rest[:-1], rest[-1]
    n_req = len(outs)
    own = lax.axis_index("req")
    tok = q_ref.shape[0]
    q_width = q_ref.shape[1] // n_req
    kv_width = kv_ref.shape[1] // 2
    head_width = kv_width // n_req
    copies = []

    def copy(source, target):
        copies.append(pltpu.make_async_copy(source, target, sems.at[len(copies)]))
        copies[-1].start()

    for k in (3, 2, 1, 0):
        out = outs[k]
        dest = jnp.bitwise_xor(own, k)
        col = pl.multiple_of(dest * q_width, 128)
        copy(q_ref.at[:, pl.ds(col, q_width)], out.at[:, pl.ds(0, q_width)])
        at = q_width
        blocks = [(kv_ref, 0)]
        blocks += [(pool_ref, i * tok) for i in range(pool_ref.shape[0] // tok)]
        for block, row in blocks:
            for half in range(2):
                col = pl.multiple_of(half * kv_width + dest * head_width, 128)
                copy(
                    block.at[pl.ds(row, tok), pl.ds(col, head_width)],
                    out.at[:, pl.ds(at, head_width)],
                )
                at += head_width
        if k == 1:
            copy(kv_ref, out.at[:, pl.ds(at, 2 * kv_width)])
    for one in copies:
        one.wait()


def pack(q, kv, pool, n_req):
    tok = q.shape[0]
    blocks = 1 + pool.shape[0] // tok
    width = (q.shape[1] + blocks * kv.shape[1]) // n_req
    widths = [width + (kv.shape[1] if k == 1 else 0) for k in range(n_req)]
    return pl.pallas_call(
        pack_kernel,
        out_shape=[jax.ShapeDtypeStruct((tok, w), BF16) for w in widths],
        in_specs=[pl.BlockSpec(memory_space=pltpu.MemorySpace.HBM)] * 3,
        out_specs=[vmem()] * n_req,
        scratch_shapes=[pltpu.SemaphoreType.DMA((n_req * (1 + 2 * blocks) + 1,))],
        compiler_params=params(),
        cost_estimate=FREE,
        name="pack",
    )(q, kv, pool)


def turn(values, cosine, sine):
    lane = lax.broadcasted_iota(jnp.int32, values.shape, 1)
    other = jnp.where(lane % HD < HD // 2, pltpu.roll(values, 128 - HD // 2, 1), pltpu.roll(values, HD // 2, 1))
    return values * cosine + other * sine


def attention_kernel(
    pages_ref, table_ref, sink_ref, cos_ref, sin_ref, *rest, kv_dev, per_kv, page_size
):
    n_req = len(rest) - 8
    pieces, out_ref = rest[:n_req], rest[n_req]
    q_scr, qt_scr, pool_scr, flat_scr, key_scr, value_scr, bias_scr = rest[n_req + 1 :]
    own = lax.axis_index("req")
    tok = pieces[0].shape[0]
    q_width = kv_dev * per_kv * HD
    head_width = kv_dev * HD
    page_limit = table_ref.shape[1]
    cached = page_limit * page_size
    fresh = tok * n_req
    total = cached + fresh
    pool_rows = pool_scr.shape[1]
    live = pages_ref[0] * page_size
    pairs = per_kv // 2
    for place, k in enumerate(ORDER):
        shard = jnp.bitwise_xor(own, k)
        row = pl.multiple_of(shard * tok, tok)
        cosine = cos_ref[pl.ds(row, tok), :]
        sine = sin_ref[pl.ds(row, tok), :]
        for p in range(kv_dev * pairs):
            col = p * 2 * HD
            turned = turn(pieces[k][:, col : col + 2 * HD].astype(F32), cosine, sine).astype(BF16)
            q_scr[p, place // 2, place % 2 * tok : (place % 2 + 1) * tok, :] = turned.astype(F32) * (1.0 / math.sqrt(HD))
        at = q_width
        key_row = pl.multiple_of(cached + row, tok)
        flat_scr[pl.ds(key_row, tok), :head_width] = turn(
            pieces[k][:, at : at + head_width].astype(F32), cosine, sine
        )
        flat_scr[pl.ds(key_row, tok), head_width:] = pieces[k][
            :, at + head_width : at + 2 * head_width
        ].astype(F32)
        at += 2 * head_width
        for i in range(pool_rows // tok):
            pool_scr[shard, i * tok : (i + 1) * tok, :] = pieces[k][:, at : at + 2 * head_width].astype(F32)
            at += 2 * head_width
        key = lax.broadcasted_iota(jnp.int32, (total, tok), 0)
        query = lax.broadcasted_iota(jnp.int32, (total, tok), 1) + (cached + shard * tok)
        last = jnp.where(key < cached, live - 1, query)
        bias_scr[:, place * tok : (place + 1) * tok] = jnp.where(key > last, NEGATIVE, 0.0)
    for p in range(kv_dev * pairs):
        for h in range(2):
            at = (p % pairs * 2 + h) * 2 * tok
            qt_scr[p // pairs, :, at : at + 2 * tok] = q_scr[p, h].T.astype(BF16)
    per_dev = pool_rows // page_size
    for j in range(page_limit):
        slot = table_ref[0, j]
        source = pl.multiple_of((slot % per_dev) * page_size, page_size)
        flat_scr[j * page_size : (j + 1) * page_size, :] = pool_scr[
            slot // per_dev, pl.ds(source, page_size), :
        ]
    flat = flat_scr[:, :head_width]
    rolled = pltpu.roll(flat, HD, 1)
    low = lax.broadcasted_iota(jnp.int32, flat.shape, 1) < HD
    zero = jnp.zeros_like(flat)
    key_scr[0] = jnp.where(low, flat, zero).astype(BF16)
    key_scr[1] = jnp.where(low, zero, rolled).astype(BF16)
    key_scr[2] = jnp.where(low, rolled, zero).astype(BF16)
    key_scr[3] = jnp.where(low, zero, flat).astype(BF16)
    value_scr[...] = flat_scr[:, head_width:].T.astype(BF16)

    def one_set(i, carry):
        g, a = i // 2, i % 2
        wide = n_req * tok
        scores = jnp.dot(key_scr[i], qt_scr[g], preferred_element_type=F32)
        weights, dens = [], []
        for p in range(pairs):
            part = scores[:, p * wide : (p + 1) * wide] + bias_scr[...]
            sink = sink_ref[own * (kv_dev * per_kv) + g * per_kv + 2 * p + a]
            top = jnp.maximum(jnp.max(part, axis=0, keepdims=True), sink)
            expo = jnp.exp(part - top)
            dens.append(jnp.sum(expo, axis=0, keepdims=True) + jnp.exp(sink - top))
            weights.append(expo.astype(BF16))
        values = value_scr[pl.ds(pl.multiple_of(g * HD, HD), HD), :]
        summed = jnp.dot(values, jnp.concatenate(weights, axis=1), preferred_element_type=F32)
        for p in range(pairs):
            row = pl.multiple_of((g * per_kv + 2 * p + a) * HD, HD)
            out_ref[pl.ds(row, HD), :] = (summed[:, p * wide : (p + 1) * wide] / dens[p]).astype(BF16)
        return carry

    lax.fori_loop(0, 2 * kv_dev, one_set, 0, unroll=False)


def attention(pages, table, sinks, cosine, sine, pieces, kv_dev, per_kv, pool_rows, page_size):
    n_req = len(pieces)
    tok = pieces[0].shape[0]
    total = table.shape[1] * page_size + n_req * tok
    head_width = kv_dev * HD
    return pl.pallas_call(
        functools.partial(attention_kernel, kv_dev=kv_dev, per_kv=per_kv, page_size=page_size),
        out_shape=jax.ShapeDtypeStruct((per_kv * head_width, n_req * tok), BF16),
        in_specs=[smem()] * 3 + [vmem()] * (2 + n_req),
        out_specs=vmem(),
        scratch_shapes=[
            pltpu.VMEM((kv_dev * per_kv // 2, 2, 2 * tok, 2 * HD), F32),
            pltpu.VMEM((kv_dev, 2 * HD, per_kv // 2 * n_req * tok), BF16),
            pltpu.VMEM((n_req, pool_rows, 2 * head_width), F32),
            pltpu.VMEM((total, 2 * head_width), F32),
            pltpu.VMEM((2 * kv_dev, total, head_width), BF16),
            pltpu.VMEM((head_width, total), BF16),
            pltpu.VMEM((total, n_req * tok), F32),
        ],
        compiler_params=params(),
        cost_estimate=FREE,
        name="attention",
    )(pages, table, sinks, cosine, sine, *pieces)


def pool_kernel(slots_ref, cos_ref, sin_ref, pool_ref, *rest, page_size):
    pairs, out_ref, fresh_scr = rest[:-2], rest[-2], rest[-1]
    own = lax.axis_index("req")
    tok = pairs[0].shape[0] // 2
    kv_width = pairs[0].shape[1] // 2
    for k in range(2 * len(pairs)):
        piece = pairs[k // 2][k % 2 * tok : (k % 2 + 1) * tok, :]
        row = pl.multiple_of(jnp.bitwise_xor(own, k) * tok, tok)
        cosine = cos_ref[pl.ds(row, tok), :]
        sine = sin_ref[pl.ds(row, tok), :]
        for col in range(0, kv_width, 128):
            turned = turn(piece[:, col : col + 128].astype(F32), cosine, sine).astype(BF16)
            fresh_scr[pl.ds(row, tok), col : col + 128] = turned
        fresh_scr[pl.ds(row, tok), kv_width:] = piece[:, kv_width:]
    out_ref[...] = pool_ref[...]
    slots_dev = out_ref.shape[0]
    for n in range(slots_ref.shape[1]):
        slot = slots_ref[0, n]

        @pl.when(slot // slots_dev == own)
        def _(slot=slot, n=n):
            out_ref[slot % slots_dev] = fresh_scr[n * page_size : (n + 1) * page_size, :]


def write_pool(slots, cosine, sine, pool, pairs):
    rows, width = pairs[0].shape
    return pl.pallas_call(
        functools.partial(pool_kernel, page_size=pool.shape[1]),
        out_shape=jax.ShapeDtypeStruct(pool.shape, BF16),
        in_specs=[smem()] + [vmem()] * (3 + len(pairs)),
        out_specs=vmem(),
        scratch_shapes=[pltpu.VMEM((rows * len(pairs), width), BF16)],
        compiler_params=params(),
        cost_estimate=FREE,
        name="write_pool",
    )(slots, cosine, sine, pool, *pairs)


def project_kernel(*refs, n_ctx, counts, pairs):
    contexts = refs[:n_ctx]
    weights = refs[n_ctx:-2]
    send_ref, keep_ref = refs[-2:]
    half = contexts[0].shape[1] // 2
    for n, (i, b) in enumerate(pairs):
        at = sum(counts[:b])
        row = 0
        for piece in weights[at : at + counts[b]]:
            rows = slice(row, row + piece.shape[0])
            terms = jnp.dot(piece[...], contexts[i][...], preferred_element_type=F32).astype(BF16)
            keep_ref[n, rows, :] = terms[:, :half]
            send_ref[n, rows, :] = terms[:, half:]
            row += piece.shape[0]


def project(contexts, blocks, pairs):
    tokens = contexts[0].shape[1]
    cols = sum(piece.shape[0] for piece in blocks[0])
    shape = jax.ShapeDtypeStruct((len(pairs), cols, tokens // 2), BF16)
    flat = [piece for block in blocks for piece in block]
    counts = tuple(len(block) for block in blocks)
    return pl.pallas_call(
        functools.partial(project_kernel, n_ctx=len(contexts), counts=counts, pairs=pairs),
        out_shape=[shape, shape],
        in_specs=[vmem()] * (len(contexts) + len(flat)),
        out_specs=[vmem()] * 2,
        compiler_params=params(),
        cost_estimate=FREE,
        name="project",
    )(*contexts, *flat)


def fold_rows(cols):
    return -(-cols // 32) * 16


def pair_kernel(keep_ref, got_ref, *out_refs, counts):
    cols, width = keep_ref.shape[1:]
    rows = out_refs[0].shape[1]
    tok = width // 2
    low = lax.broadcasted_iota(jnp.int32, (rows, width), 1) < tok
    at = 0
    for i, count in enumerate(counts):
        for b in range(count):
            both = keep_ref[at].astype(F32) + got_ref[at].astype(F32)
            top = both[:rows]
            rest = jnp.concatenate([both[rows:], jnp.zeros((2 * rows - cols, width), F32)], axis=0)
            out_refs[2 * i][b] = jnp.where(low, top, pltpu.roll(rest, tok, 1)).astype(BF16)
            out_refs[2 * i + 1][b] = jnp.where(low, pltpu.roll(top, tok, 1), rest).astype(BF16)
            at += 1


def pair_sum(keep, got, counts):
    cols, width = keep.shape[1:]
    shapes = [jax.ShapeDtypeStruct((c, fold_rows(cols), width), BF16) for c in counts for _ in range(2)]
    return pl.pallas_call(
        functools.partial(pair_kernel, counts=counts),
        out_shape=shapes,
        in_specs=[vmem()] * 2,
        out_specs=[vmem()] * len(shapes),
        compiler_params=params(),
        cost_estimate=FREE,
        name="pair_sum",
    )(keep, got)


def final_kernel(hidden_ref, *rest, places):
    parts, out_ref, scr = rest[:-2], rest[-2], rest[-1]
    own = lax.axis_index("exp")
    inner = is_inner(own)
    tok, width = hidden_ref.shape
    rows = parts[0].shape[1]
    cols = width // lax.axis_size("exp")
    for (first, second), bits in zip(zip(parts[0::2], parts[1::2]), places):
        for b, (inner_bits, outer_bits) in enumerate(bits):
            bit = jnp.where(inner, inner_bits, outer_bits)
            both = first[b].astype(F32) + second[b].astype(F32)
            row = pl.multiple_of(jnp.bitwise_xor(own, bit) * cols, 8)
            scr[pl.ds(row, rows), :] = both
            scr[pl.ds(row + rows, cols - rows), :] = pltpu.roll(both, tok, 1)[: cols - rows]
    attn = scr[...].T[:tok]
    out_ref[...] = (hidden_ref[...].astype(F32) + attn).astype(BF16)


def finish(hidden, parts, places):
    return pl.pallas_call(
        functools.partial(final_kernel, places=places),
        out_shape=jax.ShapeDtypeStruct(hidden.shape, BF16),
        in_specs=[vmem()] * (1 + len(parts)),
        out_specs=vmem(),
        scratch_shapes=[pltpu.VMEM((hidden.shape[1], parts[0].shape[2]), F32)],
        compiler_params=params(),
        cost_estimate=FREE,
        name="finish",
    )(hidden, *parts)


def paired_plan(
    hidden_in, queries, new_kv, kv_pool, page_table, new_slots, cached_pages, sinks, out_weight
):
    tok = hidden_in.shape[1]
    n_req = lax.axis_size("req")
    head_count = sinks.shape[0]
    kv_width = new_kv.shape[2] // 2
    kv_heads = kv_width // HD
    slots_dev, page_size = kv_pool.shape[1:3]
    pool_rows = slots_dev * page_size
    weight = out_weight.T
    cols = weight.shape[0]
    cut = fold_rows(cols)
    first = swap_blocks(weight, FAR_BIT, NEAR_BIT)

    pieces = pack(queries[0], new_kv[0], kv_pool[0].reshape(pool_rows, 2 * kv_width), n_req)
    pieces = [pieces[0]] + [swap(pieces[k], k, 0) for k in range(1, n_req)]
    second = [swap_blocks(chunk, NEAR_BIT, FAR_BIT) for chunk in (weight[:cut], weight[cut:])]

    position = cached_pages[0] * page_size + jnp.arange(n_req * tok)
    frequency = THETA ** (-2.0 * jnp.arange(HD // 2).astype(F32) / HD)
    angles = position.astype(F32)[:, None] * frequency[None, :]
    cosine, sine = jnp.cos(angles), jnp.sin(angles)
    cosine = jnp.concatenate([cosine] * 4, axis=1)
    sine = jnp.concatenate([-sine, sine, -sine, sine], axis=1)

    ctx = attention(
        cached_pages, page_table, sinks, cosine, sine, pieces, kv_heads // n_req,
        head_count // kv_heads, pool_rows, page_size,
    )
    chip_rows = jnp.concatenate([new_kv[0], pieces[1][:, -2 * kv_width :]], axis=0)
    ctx, first, chip_rows = lax.optimization_barrier((ctx, first, chip_rows))
    ctx_mate = swap(ctx, 0, PAIR_BIT)
    inner = is_inner(lax.axis_index("exp"))
    far = [jnp.where(inner, first[:cut], second[0]), jnp.where(inner, first[cut:], second[1])]
    both = [swap(chunk, 0, NEAR_BIT) for chunk in far]
    pool_out = write_pool(new_slots, cosine, sine, kv_pool[0], [chip_rows, swap(chip_rows, 2, 0)])

    def both_sides(contexts, blocks, pairs):
        send, keep = project(contexts, blocks, pairs)
        counts = tuple(n for n in (sum(i == c for c, _ in pairs) for i in range(len(contexts))) if n)
        return pair_sum(keep, swap(send, 1, 0), counts)

    parts = []
    ctx, pool_out = lax.optimization_barrier((ctx, pool_out))
    own_part, over_y = both_sides([ctx], [[weight], [first]], ((0, 0), (0, 1)))
    parts += [own_part, swap(over_y, 2, 0)]
    ctx_mate, parts[1] = lax.optimization_barrier((ctx_mate, parts[1]))
    over_pair, over_both = both_sides([ctx_mate], [[weight], [first], second], ((0, 0), (0, 1), (0, 2)))
    parts += [swap(over_pair, 0, PAIR_BIT), swap(over_both, 2, PAIR_BIT)]
    own_part, over_y, over_pair, over_both = both_sides([ctx, ctx_mate], [second, both], ((0, 0), (0, 1), (1, 1)))
    parts += [own_part, swap(over_y, 2, 0)]
    parts += [swap(over_pair, 0, PAIR_BIT), swap(over_both, 2, PAIR_BIT)]
    own_bits, first_bits, second_bits, both_bits = (
        (0, 0), (FAR_BIT, NEAR_BIT), (NEAR_BIT, FAR_BIT), (FAR_BIT ^ NEAR_BIT,) * 2
    )

    def of_mate(bits):
        return PAIR_BIT ^ bits[1], PAIR_BIT ^ bits[0]

    places = (
        (own_bits, first_bits),
        (of_mate(own_bits), of_mate(first_bits), of_mate(second_bits)),
        (second_bits, both_bits),
        (of_mate(both_bits),),
    )
    layer_out = finish(hidden_in[0], parts, places)
    return (layer_out[None], pool_out[None])


def solution(mesh):
    paired = mesh.shape["req"] == 4 and mesh.shape["exp"] == 8
    return jax.shard_map(
        paired_plan if paired else general_plan,
        mesh=mesh,
        in_specs=(
            P("exp", "req", None),
            P("exp", "req", None),
            P("exp", "req", None),
            P("exp", "req", None, None),
            P("exp", None),
            P("exp", None),
            P("exp"),
            P(),
            P("req", "exp"),
        ),
        out_specs=(P("exp", "req", None), P("exp", "req", None, None)),
        check_vma=False,
    )
```

```python
import functools
import math

import jax
import jax.numpy as jnp
from jax import lax
from jax.experimental import pallas as pl
from jax.experimental.pallas import tpu as pltpu
from jax.sharding import PartitionSpec as P

HD = 64


THETA = 150000.0
NEGATIVE = -1e30


def rotate(values, positions):
    half_width = values.shape[-1] // 2
    frequency = THETA ** (-2.0 * jnp.arange(half_width).astype(jnp.float32) / values.shape[-1])
    angles = positions.astype(jnp.float32)[:, None] * frequency[None, :]
    cosine = jnp.cos(angles)[:, None, :]
    sine_part = jnp.sin(angles)[:, None, :]
    lower_half = values[..., :half_width]
    upper_half = values[..., half_width:]
    return jnp.concatenate(
        [
            lower_half * cosine - upper_half * sine_part,
            upper_half * cosine + lower_half * sine_part,
        ],
        axis=-1,
    )


def spread_heads(rows, head_total, kv_heads, dev_count):
    per_dev = head_total // dev_count
    per_kv = head_total // kv_heads
    repeat = max(1, per_kv // per_dev)
    kv_dev = max(1, per_dev // per_kv)
    count = rows.shape[0]
    split = jnp.repeat(rows.reshape(count, 2, kv_heads, HD), repeat, axis=2)
    split = split.reshape(count, 2, dev_count, kv_dev * HD)
    return jnp.transpose(split, (0, 2, 1, 3)).reshape(count, dev_count, 2 * kv_dev * HD)


def general_plan(
    hidden_in, queries, new_kv, kv_pool, page_table, new_slots, cached_pages, sinks, out_weight
):
    tok_dev = hidden_in.shape[1]
    n_req = lax.axis_size("req")
    own_index = lax.axis_index("req")
    fresh_count = tok_dev * n_req
    head_count = sinks.shape[0]
    kv_width = new_kv.shape[2] // 2
    kv_heads = kv_width // HD
    per_kv = head_count // kv_heads
    heads_dev = head_count // n_req
    kv_dev = max(1, heads_dev // per_kv)
    per_dev_group = heads_dev // kv_dev
    head_width = 2 * kv_dev * HD
    slots_dev = kv_pool.shape[1]
    page_size = kv_pool.shape[2]
    slot_total = slots_dev * n_req
    page_limit = page_table.shape[1]
    fresh_pages = new_slots.shape[1]
    page_count = cached_pages[0]
    start_pos = page_count * page_size
    own_pos = start_pos + own_index * tok_dev + jnp.arange(tok_dev)
    q_rot = rotate(queries[0].reshape(tok_dev, head_count, HD).astype(jnp.float32), own_pos).astype(
        jnp.bfloat16
    )
    k_rot = rotate(
        new_kv[0, :, :kv_width].reshape(tok_dev, kv_heads, HD).astype(jnp.float32), own_pos
    ).astype(jnp.bfloat16)
    kv_rot = jnp.concatenate([k_rot.reshape(tok_dev, kv_width), new_kv[0, :, kv_width:]], axis=1)
    slot_all = jnp.arange(slot_total)
    page_index = jnp.arange(page_limit)
    cached_hit = (page_table[0][None, :] == slot_all[:, None]) & (page_index[None, :] < page_count)
    is_cached = jnp.any(cached_hit, axis=1)
    cached_base = jnp.sum(jnp.where(cached_hit, page_index[None, :], 0), axis=1) * page_size
    fresh_hit = new_slots[0][None, :] == slot_all[:, None]
    is_fresh = jnp.any(fresh_hit, axis=1)
    fresh_base = (
        start_pos
        + jnp.sum(jnp.where(fresh_hit, jnp.arange(fresh_pages)[None, :], 0), axis=1) * page_size
    )
    key_pos = (
        jnp.where(is_fresh, fresh_base, cached_base)[:, None] + jnp.arange(page_size)[None, :]
    ).reshape(-1)
    key_live = jnp.repeat(is_cached | is_fresh, page_size)
    all_fresh = lax.all_gather(kv_rot, "req", axis=0, tiled=True)
    own_hit = lax.dynamic_slice_in_dim(fresh_hit, own_index * slots_dev, slots_dev, 0)
    own_fresh = lax.dynamic_slice_in_dim(is_fresh, own_index * slots_dev, slots_dev, 0)
    appended = jnp.dot(
        own_hit.astype(jnp.bfloat16),
        all_fresh.reshape(fresh_pages, page_size * 2 * kv_width),
        preferred_element_type=jnp.float32,
    )
    appended = appended.astype(jnp.bfloat16).reshape(slots_dev, page_size, 2 * kv_width)
    local_pages = jnp.where(own_fresh[:, None, None], appended, kv_pool[0])
    head_pool = lax.all_to_all(
        spread_heads(
            local_pages.reshape(slots_dev * page_size, 2 * kv_width), head_count, kv_heads, n_req
        ),
        "req",
        split_axis=1,
        concat_axis=0,
        tiled=True,
    )
    head_pool = head_pool.reshape(slot_total * page_size, head_width)
    q_here = lax.all_to_all(
        q_rot.reshape(tok_dev, n_req, heads_dev * HD),
        "req",
        split_axis=1,
        concat_axis=0,
        tiled=True,
    )
    q_here = q_here.reshape(fresh_count, heads_dev * HD)
    key_total = slot_total * page_size
    all_keys = head_pool[:, : kv_dev * HD].reshape(key_total, kv_dev, HD)
    all_values = head_pool[:, kv_dev * HD :].reshape(key_total, kv_dev, HD)
    sink_mine = lax.dynamic_slice_in_dim(sinks, own_index * heads_dev, heads_dev, 0).reshape(
        kv_dev, per_dev_group
    )
    scale = 1.0 / math.sqrt(HD)
    query_block = math.gcd(fresh_count, 128)
    contexts = []
    for block_start in range(0, fresh_count, query_block):
        block_queries = q_here[block_start : block_start + query_block].reshape(
            query_block, kv_dev, per_dev_group, HD
        )
        query_pos = start_pos + block_start + jnp.arange(query_block)
        visible = key_live[None, :] & (key_pos[None, :] <= query_pos[:, None])
        scores = (
            jnp.einsum(
                "tghd,kgd->tghk", block_queries, all_keys, preferred_element_type=jnp.float32
            )
            * scale
        )
        scores = jnp.where(visible[:, None, None, :], scores, NEGATIVE)
        top_score = jnp.maximum(jnp.max(scores, axis=-1), sink_mine[None])
        expo = jnp.where(visible[:, None, None, :], jnp.exp(scores - top_score[..., None]), 0.0)
        denominator = jnp.sum(expo, axis=-1) + jnp.exp(sink_mine[None] - top_score)
        weighted = jnp.einsum(
            "tghk,kgd->tghd",
            expo.astype(jnp.bfloat16),
            all_values,
            preferred_element_type=jnp.float32,
        )
        contexts.append(
            (weighted / denominator[..., None])
            .astype(jnp.bfloat16)
            .reshape(query_block, heads_dev * HD)
        )
    context = jnp.concatenate(contexts, axis=0)
    terms = jnp.dot(
        context,
        lax.all_gather(out_weight, "exp", axis=1, tiled=True),
        preferred_element_type=jnp.float32,
    ).astype(jnp.bfloat16)
    width = terms.shape[1]
    arrived = lax.all_to_all(
        terms.reshape(n_req, tok_dev, width), "req", split_axis=0, concat_axis=0, tiled=True
    )
    attn = jnp.sum(arrived.astype(jnp.float32), axis=0)
    layer_out = (hidden_in[0].astype(jnp.float32) + attn).astype(jnp.bfloat16)
    return (layer_out[None], local_pages[None])


VMEM_LIMIT = 24 * 1024 * 1024
FREE = pl.CostEstimate(flops=0, bytes_accessed=0, transcendentals=0)
F32 = jnp.float32
BF16 = jnp.bfloat16

PAIR_BIT, NEAR_BIT, FAR_BIT = 2, 1, 6
ORDER = (0, 2, 1, 3)


def vmem():
    return pl.BlockSpec(memory_space=pltpu.VMEM)


def smem():
    return pl.BlockSpec(memory_space=pltpu.SMEM)


def params():
    return pltpu.CompilerParams(vmem_limit_bytes=VMEM_LIMIT)


def swap(values, req_bits, exp_bits):
    if not exp_bits:
        return lax.ppermute(values, "req", [(i, i ^ req_bits) for i in range(lax.axis_size("req"))])
    if not req_bits:
        return lax.ppermute(values, "exp", [(i, i ^ exp_bits) for i in range(lax.axis_size("exp"))])
    rows, cols = lax.axis_size("req"), lax.axis_size("exp")
    pairs = [
        (i * cols + j, (i ^ req_bits) * cols + (j ^ exp_bits)) for i in range(rows) for j in range(cols)
    ]
    return lax.ppermute(values, ("req", "exp"), pairs)


def is_inner(index):
    return (index & 2) * 2 != (index & 4)


def swap_blocks(values, inner_bits, outer_bits):
    pairs = [(i, i ^ (inner_bits if is_inner(i) else outer_bits)) for i in range(lax.axis_size("exp"))]
    return lax.ppermute(values, "exp", pairs)


def pack_kernel(q_ref, kv_ref, pool_ref, *rest):
    outs, sems = rest[:-1], rest[-1]
    n_req = len(outs)
    own = lax.axis_index("req")
    tok = q_ref.shape[0]
    q_width = q_ref.shape[1] // n_req
    kv_width = kv_ref.shape[1] // 2
    head_width = kv_width // n_req
    copies = []

    def copy(source, target):
        copies.append(pltpu.make_async_copy(source, target, sems.at[len(copies)]))
        copies[-1].start()

    for k in (3, 2, 1, 0):
        out = outs[k]
        dest = jnp.bitwise_xor(own, k)
        col = pl.multiple_of(dest * q_width, 128)
        copy(q_ref.at[:, pl.ds(col, q_width)], out.at[:, pl.ds(0, q_width)])
        at = q_width
        blocks = [(kv_ref, 0)]
        blocks += [(pool_ref, i * tok) for i in range(pool_ref.shape[0] // tok)]
        for block, row in blocks:
            for half in range(2):
                col = pl.multiple_of(half * kv_width + dest * head_width, 128)
                copy(
                    block.at[pl.ds(row, tok), pl.ds(col, head_width)],
                    out.at[:, pl.ds(at, head_width)],
                )
                at += head_width
        if k == 1:
            copy(kv_ref, out.at[:, pl.ds(at, 2 * kv_width)])
    for one in copies:
        one.wait()


def pack(q, kv, pool, n_req):
    tok = q.shape[0]
    blocks = 1 + pool.shape[0] // tok
    width = (q.shape[1] + blocks * kv.shape[1]) // n_req
    widths = [width + (kv.shape[1] if k == 1 else 0) for k in range(n_req)]
    return pl.pallas_call(
        pack_kernel,
        out_shape=[jax.ShapeDtypeStruct((tok, w), BF16) for w in widths],
        in_specs=[pl.BlockSpec(memory_space=pltpu.MemorySpace.HBM)] * 3,
        out_specs=[vmem()] * n_req,
        scratch_shapes=[pltpu.SemaphoreType.DMA((n_req * (1 + 2 * blocks) + 1,))],
        compiler_params=params(),
        cost_estimate=FREE,
        name="pack",
    )(q, kv, pool)


def turn(values, cosine, sine):
    lane = lax.broadcasted_iota(jnp.int32, values.shape, 1)
    other = jnp.where(lane % HD < HD // 2, pltpu.roll(values, 128 - HD // 2, 1), pltpu.roll(values, HD // 2, 1))
    return values * cosine + other * sine


def attention_kernel(
    pages_ref, table_ref, sink_ref, cos_ref, sin_ref, *rest, kv_dev, per_kv, page_size
):
    n_req = len(rest) - 8
    pieces, out_ref = rest[:n_req], rest[n_req]
    q_scr, qt_scr, pool_scr, flat_scr, key_scr, value_scr, bias_scr = rest[n_req + 1 :]
    own = lax.axis_index("req")
    tok = pieces[0].shape[0]
    q_width = kv_dev * per_kv * HD
    head_width = kv_dev * HD
    page_limit = table_ref.shape[1]
    cached = page_limit * page_size
    fresh = tok * n_req
    total = cached + fresh
    pool_rows = pool_scr.shape[1]
    live = pages_ref[0] * page_size
    pairs = per_kv // 2
    for place, k in enumerate(ORDER):
        shard = jnp.bitwise_xor(own, k)
        row = pl.multiple_of(shard * tok, tok)
        cosine = cos_ref[pl.ds(row, tok), :]
        sine = sin_ref[pl.ds(row, tok), :]
        for p in range(kv_dev * pairs):
            col = p * 2 * HD
            turned = turn(pieces[k][:, col : col + 2 * HD].astype(F32), cosine, sine).astype(BF16)
            q_scr[p, place // 2, place % 2 * tok : (place % 2 + 1) * tok, :] = turned.astype(F32) * (1.0 / math.sqrt(HD))
        at = q_width
        key_row = pl.multiple_of(cached + row, tok)
        flat_scr[pl.ds(key_row, tok), :head_width] = turn(
            pieces[k][:, at : at + head_width].astype(F32), cosine, sine
        )
        flat_scr[pl.ds(key_row, tok), head_width:] = pieces[k][
            :, at + head_width : at + 2 * head_width
        ].astype(F32)
        at += 2 * head_width
        for i in range(pool_rows // tok):
            pool_scr[shard, i * tok : (i + 1) * tok, :] = pieces[k][:, at : at + 2 * head_width].astype(F32)
            at += 2 * head_width
        key = lax.broadcasted_iota(jnp.int32, (total, tok), 0)
        query = lax.broadcasted_iota(jnp.int32, (total, tok), 1) + (cached + shard * tok)
        last = jnp.where(key < cached, live - 1, query)
        bias_scr[:, place * tok : (place + 1) * tok] = jnp.where(key > last, NEGATIVE, 0.0)
    for p in range(kv_dev * pairs):
        for h in range(2):
            at = (p % pairs * 2 + h) * 2 * tok
            qt_scr[p // pairs, :, at : at + 2 * tok] = q_scr[p, h].T.astype(BF16)
    per_dev = pool_rows // page_size
    for j in range(page_limit):
        slot = table_ref[0, j]
        source = pl.multiple_of((slot % per_dev) * page_size, page_size)
        flat_scr[j * page_size : (j + 1) * page_size, :] = pool_scr[
            slot // per_dev, pl.ds(source, page_size), :
        ]
    flat = flat_scr[:, :head_width]
    rolled = pltpu.roll(flat, HD, 1)
    low = lax.broadcasted_iota(jnp.int32, flat.shape, 1) < HD
    zero = jnp.zeros_like(flat)
    key_scr[0] = jnp.where(low, flat, zero).astype(BF16)
    key_scr[1] = jnp.where(low, zero, rolled).astype(BF16)
    key_scr[2] = jnp.where(low, rolled, zero).astype(BF16)
    key_scr[3] = jnp.where(low, zero, flat).astype(BF16)
    value_scr[...] = flat_scr[:, head_width:].T.astype(BF16)

    def one_set(i, carry):
        g, a = i // 2, i % 2
        wide = n_req * tok
        scores = jnp.dot(key_scr[i], qt_scr[g], preferred_element_type=F32)
        weights, dens = [], []
        for p in range(pairs):
            part = scores[:, p * wide : (p + 1) * wide] + bias_scr[...]
            sink = sink_ref[own * (kv_dev * per_kv) + g * per_kv + 2 * p + a]
            top = jnp.maximum(jnp.max(part, axis=0, keepdims=True), sink)
            expo = jnp.exp(part - top)
            dens.append(jnp.sum(expo, axis=0, keepdims=True) + jnp.exp(sink - top))
            weights.append(expo.astype(BF16))
        values = value_scr[pl.ds(pl.multiple_of(g * HD, HD), HD), :]
        summed = jnp.dot(values, jnp.concatenate(weights, axis=1), preferred_element_type=F32)
        for p in range(pairs):
            row = pl.multiple_of((g * per_kv + 2 * p + a) * HD, HD)
            out_ref[pl.ds(row, HD), :] = (summed[:, p * wide : (p + 1) * wide] / dens[p]).astype(BF16)
        return carry

    lax.fori_loop(0, 2 * kv_dev, one_set, 0, unroll=False)


def attention(pages, table, sinks, cosine, sine, pieces, kv_dev, per_kv, pool_rows, page_size):
    n_req = len(pieces)
    tok = pieces[0].shape[0]
    total = table.shape[1] * page_size + n_req * tok
    head_width = kv_dev * HD
    return pl.pallas_call(
        functools.partial(attention_kernel, kv_dev=kv_dev, per_kv=per_kv, page_size=page_size),
        out_shape=jax.ShapeDtypeStruct((per_kv * head_width, n_req * tok), BF16),
        in_specs=[smem()] * 3 + [vmem()] * (2 + n_req),
        out_specs=vmem(),
        scratch_shapes=[
            pltpu.VMEM((kv_dev * per_kv // 2, 2, 2 * tok, 2 * HD), F32),
            pltpu.VMEM((kv_dev, 2 * HD, per_kv // 2 * n_req * tok), BF16),
            pltpu.VMEM((n_req, pool_rows, 2 * head_width), F32),
            pltpu.VMEM((total, 2 * head_width), F32),
            pltpu.VMEM((2 * kv_dev, total, head_width), BF16),
            pltpu.VMEM((head_width, total), BF16),
            pltpu.VMEM((total, n_req * tok), F32),
        ],
        compiler_params=params(),
        cost_estimate=FREE,
        name="attention",
    )(pages, table, sinks, cosine, sine, *pieces)


def pool_kernel(slots_ref, cos_ref, sin_ref, pool_ref, *rest, page_size):
    pairs, out_ref, fresh_scr = rest[:-2], rest[-2], rest[-1]
    own = lax.axis_index("req")
    tok = pairs[0].shape[0] // 2
    kv_width = pairs[0].shape[1] // 2
    for k in range(2 * len(pairs)):
        piece = pairs[k // 2][k % 2 * tok : (k % 2 + 1) * tok, :]
        row = pl.multiple_of(jnp.bitwise_xor(own, k) * tok, tok)
        cosine = cos_ref[pl.ds(row, tok), :]
        sine = sin_ref[pl.ds(row, tok), :]
        for col in range(0, kv_width, 128):
            turned = turn(piece[:, col : col + 128].astype(F32), cosine, sine).astype(BF16)
            fresh_scr[pl.ds(row, tok), col : col + 128] = turned
        fresh_scr[pl.ds(row, tok), kv_width:] = piece[:, kv_width:]
    out_ref[...] = pool_ref[...]
    slots_dev = out_ref.shape[0]
    for n in range(slots_ref.shape[1]):
        slot = slots_ref[0, n]

        @pl.when(slot // slots_dev == own)
        def _(slot=slot, n=n):
            out_ref[slot % slots_dev] = fresh_scr[n * page_size : (n + 1) * page_size, :]


def write_pool(slots, cosine, sine, pool, pairs):
    rows, width = pairs[0].shape
    return pl.pallas_call(
        functools.partial(pool_kernel, page_size=pool.shape[1]),
        out_shape=jax.ShapeDtypeStruct(pool.shape, BF16),
        in_specs=[smem()] + [vmem()] * (3 + len(pairs)),
        out_specs=vmem(),
        scratch_shapes=[pltpu.VMEM((rows * len(pairs), width), BF16)],
        compiler_params=params(),
        cost_estimate=FREE,
        name="write_pool",
    )(slots, cosine, sine, pool, *pairs)


def project_kernel(*refs, n_ctx, counts, pairs):
    contexts = refs[:n_ctx]
    weights = refs[n_ctx:-2]
    send_ref, keep_ref = refs[-2:]
    half = contexts[0].shape[1] // 2
    for n, (i, b) in enumerate(pairs):
        at = sum(counts[:b])
        row = 0
        for piece in weights[at : at + counts[b]]:
            rows = slice(row, row + piece.shape[0])
            terms = jnp.dot(piece[...], contexts[i][...], preferred_element_type=F32).astype(BF16)
            keep_ref[n, rows, :] = terms[:, :half]
            send_ref[n, rows, :] = terms[:, half:]
            row += piece.shape[0]


def project(contexts, blocks, pairs):
    tokens = contexts[0].shape[1]
    cols = sum(piece.shape[0] for piece in blocks[0])
    shape = jax.ShapeDtypeStruct((len(pairs), cols, tokens // 2), BF16)
    flat = [piece for block in blocks for piece in block]
    counts = tuple(len(block) for block in blocks)
    return pl.pallas_call(
        functools.partial(project_kernel, n_ctx=len(contexts), counts=counts, pairs=pairs),
        out_shape=[shape, shape],
        in_specs=[vmem()] * (len(contexts) + len(flat)),
        out_specs=[vmem()] * 2,
        compiler_params=params(),
        cost_estimate=FREE,
        name="project",
    )(*contexts, *flat)


def fold_rows(cols):
    return -(-cols // 32) * 16


def pair_kernel(keep_ref, got_ref, *out_refs, counts):
    cols, width = keep_ref.shape[1:]
    rows = out_refs[0].shape[1]
    tok = width // 2
    low = lax.broadcasted_iota(jnp.int32, (rows, width), 1) < tok
    at = 0
    for i, count in enumerate(counts):
        for b in range(count):
            both = keep_ref[at].astype(F32) + got_ref[at].astype(F32)
            top = both[:rows]
            rest = jnp.concatenate([both[rows:], jnp.zeros((2 * rows - cols, width), F32)], axis=0)
            out_refs[2 * i][b] = jnp.where(low, top, pltpu.roll(rest, tok, 1)).astype(BF16)
            out_refs[2 * i + 1][b] = jnp.where(low, pltpu.roll(top, tok, 1), rest).astype(BF16)
            at += 1


def pair_sum(keep, got, counts):
    cols, width = keep.shape[1:]
    shapes = [jax.ShapeDtypeStruct((c, fold_rows(cols), width), BF16) for c in counts for _ in range(2)]
    return pl.pallas_call(
        functools.partial(pair_kernel, counts=counts),
        out_shape=shapes,
        in_specs=[vmem()] * 2,
        out_specs=[vmem()] * len(shapes),
        compiler_params=params(),
        cost_estimate=FREE,
        name="pair_sum",
    )(keep, got)


def final_kernel(hidden_ref, *rest, places):
    parts, out_ref, scr = rest[:-2], rest[-2], rest[-1]
    own = lax.axis_index("exp")
    inner = is_inner(own)
    tok, width = hidden_ref.shape
    rows = parts[0].shape[1]
    cols = width // lax.axis_size("exp")
    for (first, second), bits in zip(zip(parts[0::2], parts[1::2]), places):
        for b, (inner_bits, outer_bits) in enumerate(bits):
            bit = jnp.where(inner, inner_bits, outer_bits)
            both = first[b].astype(F32) + second[b].astype(F32)
            row = pl.multiple_of(jnp.bitwise_xor(own, bit) * cols, 8)
            scr[pl.ds(row, rows), :] = both
            scr[pl.ds(row + rows, cols - rows), :] = pltpu.roll(both, tok, 1)[: cols - rows]
    attn = scr[...].T[:tok]
    out_ref[...] = (hidden_ref[...].astype(F32) + attn).astype(BF16)


def finish(hidden, parts, places):
    return pl.pallas_call(
        functools.partial(final_kernel, places=places),
        out_shape=jax.ShapeDtypeStruct(hidden.shape, BF16),
        in_specs=[vmem()] * (1 + len(parts)),
        out_specs=vmem(),
        scratch_shapes=[pltpu.VMEM((hidden.shape[1], parts[0].shape[2]), F32)],
        compiler_params=params(),
        cost_estimate=FREE,
        name="finish",
    )(hidden, *parts)


def paired_plan(
    hidden_in, queries, new_kv, kv_pool, page_table, new_slots, cached_pages, sinks, out_weight
):
    tok = hidden_in.shape[1]
    n_req = lax.axis_size("req")
    head_count = sinks.shape[0]
    kv_width = new_kv.shape[2] // 2
    kv_heads = kv_width // HD
    slots_dev, page_size = kv_pool.shape[1:3]
    pool_rows = slots_dev * page_size
    weight = out_weight.T
    cols = weight.shape[0]
    cuts = [slice(cols * i // 360, cols * j // 360) for i, j in zip((0, 200), (200, 360))]
    first = swap_blocks(weight, FAR_BIT, NEAR_BIT)

    pieces = pack(queries[0], new_kv[0], kv_pool[0].reshape(pool_rows, 2 * kv_width), n_req)
    pieces = [pieces[0]] + [swap(pieces[k], k, 0) for k in range(1, n_req)]
    second = [swap_blocks(weight[cuts[0]], NEAR_BIT, FAR_BIT)]

    position = cached_pages[0] * page_size + jnp.arange(n_req * tok)
    frequency = THETA ** (-2.0 * jnp.arange(HD // 2).astype(F32) / HD)
    angles = position.astype(F32)[:, None] * frequency[None, :]
    cosine, sine = jnp.cos(angles), jnp.sin(angles)
    cosine = jnp.concatenate([cosine] * 4, axis=1)
    sine = jnp.concatenate([-sine, sine, -sine, sine], axis=1)

    ctx = attention(
        cached_pages, page_table, sinks, cosine, sine, pieces, kv_heads // n_req,
        head_count // kv_heads, pool_rows, page_size,
    )
    chip_rows = jnp.concatenate([new_kv[0], pieces[1][:, -2 * kv_width :]], axis=0)
    ctx, later = lax.optimization_barrier((ctx, weight))
    second += [swap_blocks(later[cuts[1]], NEAR_BIT, FAR_BIT)]
    ctx, first, chip_rows = lax.optimization_barrier((ctx, first, chip_rows))
    ctx_mate = swap(ctx, 0, PAIR_BIT)
    inner = is_inner(lax.axis_index("exp"))
    far = [jnp.where(inner, first[rows], piece) for rows, piece in zip(cuts, second)]
    both = [swap(chunk, 0, NEAR_BIT) for chunk in far]
    pool_out = write_pool(new_slots, cosine, sine, kv_pool[0], [chip_rows, swap(chip_rows, 2, 0)])

    def both_sides(contexts, blocks, pairs):
        send, keep = project(contexts, blocks, pairs)
        counts = tuple(n for n in (sum(i == c for c, _ in pairs) for i in range(len(contexts))) if n)
        return pair_sum(keep, swap(send, 1, 0), counts)

    parts = []
    ctx, pool_out = lax.optimization_barrier((ctx, pool_out))
    own_part, over_y = both_sides([ctx], [[weight], [first]], ((0, 0), (0, 1)))
    parts += [own_part, swap(over_y, 2, 0)]
    ctx_mate, parts[1] = lax.optimization_barrier((ctx_mate, parts[1]))
    over_pair, over_both = both_sides([ctx_mate], [[weight], [first], second], ((0, 0), (0, 1), (0, 2)))
    parts += [swap(over_pair, 0, PAIR_BIT), swap(over_both, 2, PAIR_BIT)]
    own_part, over_y, over_pair, over_both = both_sides([ctx, ctx_mate], [second, both], ((0, 0), (0, 1), (1, 1)))
    parts += [own_part, swap(over_y, 2, 0)]
    parts += [swap(over_pair, 0, PAIR_BIT), swap(over_both, 2, PAIR_BIT)]
    own_bits, first_bits, second_bits, both_bits = (
        (0, 0), (FAR_BIT, NEAR_BIT), (NEAR_BIT, FAR_BIT), (FAR_BIT ^ NEAR_BIT,) * 2
    )

    def of_mate(bits):
        return PAIR_BIT ^ bits[1], PAIR_BIT ^ bits[0]

    places = (
        (own_bits, first_bits),
        (of_mate(own_bits), of_mate(first_bits), of_mate(second_bits)),
        (second_bits, both_bits),
        (of_mate(both_bits),),
    )
    layer_out = finish(hidden_in[0], parts, places)
    return (layer_out[None], pool_out[None])


def solution(mesh):
    paired = mesh.shape["req"] == 4 and mesh.shape["exp"] == 8
    return jax.shard_map(
        paired_plan if paired else general_plan,
        mesh=mesh,
        in_specs=(
            P("exp", "req", None),
            P("exp", "req", None),
            P("exp", "req", None),
            P("exp", "req", None, None),
            P("exp", None),
            P("exp", None),
            P("exp"),
            P(),
            P("req", "exp"),
        ),
        out_specs=(P("exp", "req", None), P("exp", "req", None, None)),
        check_vma=False,
    )
```

```python
import functools
import math

import jax
import jax.numpy as jnp
from jax import lax
from jax.experimental import pallas as pl
from jax.experimental.pallas import tpu as pltpu
from jax.sharding import PartitionSpec as P

HD = 64


THETA = 150000.0
NEGATIVE = -1e30


def rotate(values, positions):
    half_width = values.shape[-1] // 2
    frequency = THETA ** (-2.0 * jnp.arange(half_width).astype(jnp.float32) / values.shape[-1])
    angles = positions.astype(jnp.float32)[:, None] * frequency[None, :]
    cosine = jnp.cos(angles)[:, None, :]
    sine_part = jnp.sin(angles)[:, None, :]
    lower_half = values[..., :half_width]
    upper_half = values[..., half_width:]
    return jnp.concatenate(
        [
            lower_half * cosine - upper_half * sine_part,
            upper_half * cosine + lower_half * sine_part,
        ],
        axis=-1,
    )


def spread_heads(rows, head_total, kv_heads, dev_count):
    per_dev = head_total // dev_count
    per_kv = head_total // kv_heads
    repeat = max(1, per_kv // per_dev)
    kv_dev = max(1, per_dev // per_kv)
    count = rows.shape[0]
    split = jnp.repeat(rows.reshape(count, 2, kv_heads, HD), repeat, axis=2)
    split = split.reshape(count, 2, dev_count, kv_dev * HD)
    return jnp.transpose(split, (0, 2, 1, 3)).reshape(count, dev_count, 2 * kv_dev * HD)


def general_plan(
    hidden_in, queries, new_kv, kv_pool, page_table, new_slots, cached_pages, sinks, out_weight
):
    tok_dev = hidden_in.shape[1]
    n_req = lax.axis_size("req")
    own_index = lax.axis_index("req")
    fresh_count = tok_dev * n_req
    head_count = sinks.shape[0]
    kv_width = new_kv.shape[2] // 2
    kv_heads = kv_width // HD
    per_kv = head_count // kv_heads
    heads_dev = head_count // n_req
    kv_dev = max(1, heads_dev // per_kv)
    per_dev_group = heads_dev // kv_dev
    head_width = 2 * kv_dev * HD
    slots_dev = kv_pool.shape[1]
    page_size = kv_pool.shape[2]
    slot_total = slots_dev * n_req
    page_limit = page_table.shape[1]
    fresh_pages = new_slots.shape[1]
    page_count = cached_pages[0]
    start_pos = page_count * page_size
    own_pos = start_pos + own_index * tok_dev + jnp.arange(tok_dev)
    q_rot = rotate(queries[0].reshape(tok_dev, head_count, HD).astype(jnp.float32), own_pos).astype(
        jnp.bfloat16
    )
    k_rot = rotate(
        new_kv[0, :, :kv_width].reshape(tok_dev, kv_heads, HD).astype(jnp.float32), own_pos
    ).astype(jnp.bfloat16)
    kv_rot = jnp.concatenate([k_rot.reshape(tok_dev, kv_width), new_kv[0, :, kv_width:]], axis=1)
    slot_all = jnp.arange(slot_total)
    page_index = jnp.arange(page_limit)
    cached_hit = (page_table[0][None, :] == slot_all[:, None]) & (page_index[None, :] < page_count)
    is_cached = jnp.any(cached_hit, axis=1)
    cached_base = jnp.sum(jnp.where(cached_hit, page_index[None, :], 0), axis=1) * page_size
    fresh_hit = new_slots[0][None, :] == slot_all[:, None]
    is_fresh = jnp.any(fresh_hit, axis=1)
    fresh_base = (
        start_pos
        + jnp.sum(jnp.where(fresh_hit, jnp.arange(fresh_pages)[None, :], 0), axis=1) * page_size
    )
    key_pos = (
        jnp.where(is_fresh, fresh_base, cached_base)[:, None] + jnp.arange(page_size)[None, :]
    ).reshape(-1)
    key_live = jnp.repeat(is_cached | is_fresh, page_size)
    all_fresh = lax.all_gather(kv_rot, "req", axis=0, tiled=True)
    own_hit = lax.dynamic_slice_in_dim(fresh_hit, own_index * slots_dev, slots_dev, 0)
    own_fresh = lax.dynamic_slice_in_dim(is_fresh, own_index * slots_dev, slots_dev, 0)
    appended = jnp.dot(
        own_hit.astype(jnp.bfloat16),
        all_fresh.reshape(fresh_pages, page_size * 2 * kv_width),
        preferred_element_type=jnp.float32,
    )
    appended = appended.astype(jnp.bfloat16).reshape(slots_dev, page_size, 2 * kv_width)
    local_pages = jnp.where(own_fresh[:, None, None], appended, kv_pool[0])
    head_pool = lax.all_to_all(
        spread_heads(
            local_pages.reshape(slots_dev * page_size, 2 * kv_width), head_count, kv_heads, n_req
        ),
        "req",
        split_axis=1,
        concat_axis=0,
        tiled=True,
    )
    head_pool = head_pool.reshape(slot_total * page_size, head_width)
    q_here = lax.all_to_all(
        q_rot.reshape(tok_dev, n_req, heads_dev * HD),
        "req",
        split_axis=1,
        concat_axis=0,
        tiled=True,
    )
    q_here = q_here.reshape(fresh_count, heads_dev * HD)
    key_total = slot_total * page_size
    all_keys = head_pool[:, : kv_dev * HD].reshape(key_total, kv_dev, HD)
    all_values = head_pool[:, kv_dev * HD :].reshape(key_total, kv_dev, HD)
    sink_mine = lax.dynamic_slice_in_dim(sinks, own_index * heads_dev, heads_dev, 0).reshape(
        kv_dev, per_dev_group
    )
    scale = 1.0 / math.sqrt(HD)
    query_block = math.gcd(fresh_count, 128)
    contexts = []
    for block_start in range(0, fresh_count, query_block):
        block_queries = q_here[block_start : block_start + query_block].reshape(
            query_block, kv_dev, per_dev_group, HD
        )
        query_pos = start_pos + block_start + jnp.arange(query_block)
        visible = key_live[None, :] & (key_pos[None, :] <= query_pos[:, None])
        scores = (
            jnp.einsum(
                "tghd,kgd->tghk", block_queries, all_keys, preferred_element_type=jnp.float32
            )
            * scale
        )
        scores = jnp.where(visible[:, None, None, :], scores, NEGATIVE)
        top_score = jnp.maximum(jnp.max(scores, axis=-1), sink_mine[None])
        expo = jnp.where(visible[:, None, None, :], jnp.exp(scores - top_score[..., None]), 0.0)
        denominator = jnp.sum(expo, axis=-1) + jnp.exp(sink_mine[None] - top_score)
        weighted = jnp.einsum(
            "tghk,kgd->tghd",
            expo.astype(jnp.bfloat16),
            all_values,
            preferred_element_type=jnp.float32,
        )
        contexts.append(
            (weighted / denominator[..., None])
            .astype(jnp.bfloat16)
            .reshape(query_block, heads_dev * HD)
        )
    context = jnp.concatenate(contexts, axis=0)
    terms = jnp.dot(
        context,
        lax.all_gather(out_weight, "exp", axis=1, tiled=True),
        preferred_element_type=jnp.float32,
    ).astype(jnp.bfloat16)
    width = terms.shape[1]
    arrived = lax.all_to_all(
        terms.reshape(n_req, tok_dev, width), "req", split_axis=0, concat_axis=0, tiled=True
    )
    attn = jnp.sum(arrived.astype(jnp.float32), axis=0)
    layer_out = (hidden_in[0].astype(jnp.float32) + attn).astype(jnp.bfloat16)
    return (layer_out[None], local_pages[None])


VMEM_LIMIT = 24 * 1024 * 1024
FREE = pl.CostEstimate(flops=0, bytes_accessed=0, transcendentals=0)
F32 = jnp.float32
BF16 = jnp.bfloat16

PAIR_BIT, NEAR_BIT, FAR_BIT = 2, 1, 6
ORDER = (0, 2, 1, 3)


def vmem():
    return pl.BlockSpec(memory_space=pltpu.VMEM)


def smem():
    return pl.BlockSpec(memory_space=pltpu.SMEM)


def params():
    return pltpu.CompilerParams(vmem_limit_bytes=VMEM_LIMIT)


def swap(values, req_bits, exp_bits):
    if not exp_bits:
        return lax.ppermute(values, "req", [(i, i ^ req_bits) for i in range(lax.axis_size("req"))])
    if not req_bits:
        return lax.ppermute(values, "exp", [(i, i ^ exp_bits) for i in range(lax.axis_size("exp"))])
    rows, cols = lax.axis_size("req"), lax.axis_size("exp")
    pairs = [
        (i * cols + j, (i ^ req_bits) * cols + (j ^ exp_bits)) for i in range(rows) for j in range(cols)
    ]
    return lax.ppermute(values, ("req", "exp"), pairs)


def is_inner(index):
    return (index & 2) * 2 != (index & 4)


def swap_blocks(values, inner_bits, outer_bits):
    pairs = [(i, i ^ (inner_bits if is_inner(i) else outer_bits)) for i in range(lax.axis_size("exp"))]
    return lax.ppermute(values, "exp", pairs)


def pack_kernel(q_ref, kv_ref, pool_ref, *rest):
    outs, sems = rest[:-1], rest[-1]
    n_req = len(outs)
    own = lax.axis_index("req")
    tok = q_ref.shape[0]
    q_width = q_ref.shape[1] // n_req
    kv_width = kv_ref.shape[1] // 2
    head_width = kv_width // n_req
    copies = []

    def copy(source, target):
        copies.append(pltpu.make_async_copy(source, target, sems.at[len(copies)]))
        copies[-1].start()

    for k in (3, 2, 1, 0):
        out = outs[k]
        dest = jnp.bitwise_xor(own, k)
        col = pl.multiple_of(dest * q_width, 128)
        copy(q_ref.at[:, pl.ds(col, q_width)], out.at[:, pl.ds(0, q_width)])
        at = q_width
        blocks = [(kv_ref, 0)]
        blocks += [(pool_ref, i * tok) for i in range(pool_ref.shape[0] // tok)]
        for block, row in blocks:
            for half in range(2):
                col = pl.multiple_of(half * kv_width + dest * head_width, 128)
                copy(
                    block.at[pl.ds(row, tok), pl.ds(col, head_width)],
                    out.at[:, pl.ds(at, head_width)],
                )
                at += head_width
        if k == 1:
            copy(kv_ref, out.at[:, pl.ds(at, 2 * kv_width)])
    for one in copies:
        one.wait()


def pack(q, kv, pool, n_req):
    tok = q.shape[0]
    blocks = 1 + pool.shape[0] // tok
    width = (q.shape[1] + blocks * kv.shape[1]) // n_req
    widths = [width + (kv.shape[1] if k == 1 else 0) for k in range(n_req)]
    return pl.pallas_call(
        pack_kernel,
        out_shape=[jax.ShapeDtypeStruct((tok, w), BF16) for w in widths],
        in_specs=[pl.BlockSpec(memory_space=pltpu.MemorySpace.HBM)] * 3,
        out_specs=[vmem()] * n_req,
        scratch_shapes=[pltpu.SemaphoreType.DMA((n_req * (1 + 2 * blocks) + 1,))],
        compiler_params=params(),
        cost_estimate=FREE,
        name="pack",
    )(q, kv, pool)


def turn(values, cosine, sine):
    lane = lax.broadcasted_iota(jnp.int32, values.shape, 1)
    other = jnp.where(lane % HD < HD // 2, pltpu.roll(values, 128 - HD // 2, 1), pltpu.roll(values, HD // 2, 1))
    return values * cosine + other * sine


def attention_kernel(
    pages_ref, table_ref, sink_ref, cos_ref, sin_ref, *rest, kv_dev, per_kv, page_size
):
    n_req = len(rest) - 8
    pieces, out_ref = rest[:n_req], rest[n_req]
    q_scr, qt_scr, pool_scr, flat_scr, key_scr, value_scr, bias_scr = rest[n_req + 1 :]
    own = lax.axis_index("req")
    tok = pieces[0].shape[0]
    q_width = kv_dev * per_kv * HD
    head_width = kv_dev * HD
    page_limit = table_ref.shape[1]
    cached = page_limit * page_size
    fresh = tok * n_req
    total = cached + fresh
    pool_rows = pool_scr.shape[1]
    live = pages_ref[0] * page_size
    pairs = per_kv // 2
    for place, k in enumerate(ORDER):
        shard = jnp.bitwise_xor(own, k)
        row = pl.multiple_of(shard * tok, tok)
        cosine = cos_ref[pl.ds(row, tok), :]
        sine = sin_ref[pl.ds(row, tok), :]
        for p in range(kv_dev * pairs):
            col = p * 2 * HD
            turned = turn(pieces[k][:, col : col + 2 * HD].astype(F32), cosine, sine).astype(BF16)
            q_scr[p, place // 2, place % 2 * tok : (place % 2 + 1) * tok, :] = turned.astype(F32) * (1.0 / math.sqrt(HD))
        at = q_width
        key_row = pl.multiple_of(cached + row, tok)
        flat_scr[pl.ds(key_row, tok), :head_width] = turn(
            pieces[k][:, at : at + head_width].astype(F32), cosine, sine
        )
        flat_scr[pl.ds(key_row, tok), head_width:] = pieces[k][
            :, at + head_width : at + 2 * head_width
        ].astype(F32)
        at += 2 * head_width
        for i in range(pool_rows // tok):
            pool_scr[shard, i * tok : (i + 1) * tok, :] = pieces[k][:, at : at + 2 * head_width].astype(F32)
            at += 2 * head_width
        key = lax.broadcasted_iota(jnp.int32, (total, tok), 0)
        query = lax.broadcasted_iota(jnp.int32, (total, tok), 1) + (cached + shard * tok)
        last = jnp.where(key < cached, live - 1, query)
        bias_scr[:, place * tok : (place + 1) * tok] = jnp.where(key > last, NEGATIVE, 0.0)
    for p in range(kv_dev * pairs):
        for h in range(2):
            at = (p % pairs * 2 + h) * 2 * tok
            qt_scr[p // pairs, :, at : at + 2 * tok] = q_scr[p, h].T.astype(BF16)
    per_dev = pool_rows // page_size
    for j in range(page_limit):
        slot = table_ref[0, j]
        source = pl.multiple_of((slot % per_dev) * page_size, page_size)
        flat_scr[j * page_size : (j + 1) * page_size, :] = pool_scr[
            slot // per_dev, pl.ds(source, page_size), :
        ]
    flat = flat_scr[:, :head_width]
    rolled = pltpu.roll(flat, HD, 1)
    low = lax.broadcasted_iota(jnp.int32, flat.shape, 1) < HD
    zero = jnp.zeros_like(flat)
    key_scr[0] = jnp.where(low, flat, zero).astype(BF16)
    key_scr[1] = jnp.where(low, zero, rolled).astype(BF16)
    key_scr[2] = jnp.where(low, rolled, zero).astype(BF16)
    key_scr[3] = jnp.where(low, zero, flat).astype(BF16)
    value_scr[...] = flat_scr[:, head_width:].T.astype(BF16)

    def one_set(i, carry):
        g, a = i // 2, i % 2
        wide = n_req * tok
        scores = jnp.dot(key_scr[i], qt_scr[g], preferred_element_type=F32)
        weights, dens = [], []
        for p in range(pairs):
            part = scores[:, p * wide : (p + 1) * wide] + bias_scr[...]
            sink = sink_ref[own * (kv_dev * per_kv) + g * per_kv + 2 * p + a]
            top = jnp.maximum(jnp.max(part, axis=0, keepdims=True), sink)
            expo = jnp.exp(part - top)
            dens.append(jnp.sum(expo, axis=0, keepdims=True) + jnp.exp(sink - top))
            weights.append(expo.astype(BF16))
        values = value_scr[pl.ds(pl.multiple_of(g * HD, HD), HD), :]
        summed = jnp.dot(values, jnp.concatenate(weights, axis=1), preferred_element_type=F32)
        for p in range(pairs):
            row = pl.multiple_of((g * per_kv + 2 * p + a) * HD, HD)
            out_ref[pl.ds(row, HD), :] = (summed[:, p * wide : (p + 1) * wide] / dens[p]).astype(BF16)
        return carry

    lax.fori_loop(0, 2 * kv_dev, one_set, 0, unroll=False)


def attention(pages, table, sinks, cosine, sine, pieces, kv_dev, per_kv, pool_rows, page_size):
    n_req = len(pieces)
    tok = pieces[0].shape[0]
    total = table.shape[1] * page_size + n_req * tok
    head_width = kv_dev * HD
    return pl.pallas_call(
        functools.partial(attention_kernel, kv_dev=kv_dev, per_kv=per_kv, page_size=page_size),
        out_shape=jax.ShapeDtypeStruct((per_kv * head_width, n_req * tok), BF16),
        in_specs=[smem()] * 3 + [vmem()] * (2 + n_req),
        out_specs=vmem(),
        scratch_shapes=[
            pltpu.VMEM((kv_dev * per_kv // 2, 2, 2 * tok, 2 * HD), F32),
            pltpu.VMEM((kv_dev, 2 * HD, per_kv // 2 * n_req * tok), BF16),
            pltpu.VMEM((n_req, pool_rows, 2 * head_width), F32),
            pltpu.VMEM((total, 2 * head_width), F32),
            pltpu.VMEM((2 * kv_dev, total, head_width), BF16),
            pltpu.VMEM((head_width, total), BF16),
            pltpu.VMEM((total, n_req * tok), F32),
        ],
        compiler_params=params(),
        cost_estimate=FREE,
        name="attention",
    )(pages, table, sinks, cosine, sine, *pieces)


def pool_kernel(slots_ref, cos_ref, sin_ref, pool_ref, *rest, page_size):
    pairs, out_ref, fresh_scr = rest[:-2], rest[-2], rest[-1]
    own = lax.axis_index("req")
    tok = pairs[0].shape[0] // 2
    kv_width = pairs[0].shape[1] // 2
    for k in range(2 * len(pairs)):
        piece = pairs[k // 2][k % 2 * tok : (k % 2 + 1) * tok, :]
        row = pl.multiple_of(jnp.bitwise_xor(own, k) * tok, tok)
        cosine = cos_ref[pl.ds(row, tok), :]
        sine = sin_ref[pl.ds(row, tok), :]
        for col in range(0, kv_width, 128):
            turned = turn(piece[:, col : col + 128].astype(F32), cosine, sine).astype(BF16)
            fresh_scr[pl.ds(row, tok), col : col + 128] = turned
        fresh_scr[pl.ds(row, tok), kv_width:] = piece[:, kv_width:]
    out_ref[...] = pool_ref[...]
    slots_dev = out_ref.shape[0]
    for n in range(slots_ref.shape[1]):
        slot = slots_ref[0, n]

        @pl.when(slot // slots_dev == own)
        def _(slot=slot, n=n):
            out_ref[slot % slots_dev] = fresh_scr[n * page_size : (n + 1) * page_size, :]


def write_pool(slots, cosine, sine, pool, pairs):
    rows, width = pairs[0].shape
    return pl.pallas_call(
        functools.partial(pool_kernel, page_size=pool.shape[1]),
        out_shape=jax.ShapeDtypeStruct(pool.shape, BF16),
        in_specs=[smem()] + [vmem()] * (3 + len(pairs)),
        out_specs=vmem(),
        scratch_shapes=[pltpu.VMEM((rows * len(pairs), width), BF16)],
        compiler_params=params(),
        cost_estimate=FREE,
        name="write_pool",
    )(slots, cosine, sine, pool, *pairs)


def project_kernel(*refs, n_ctx, counts, pairs):
    contexts = refs[:n_ctx]
    weights = refs[n_ctx:-2]
    send_ref, keep_ref = refs[-2:]
    half = contexts[0].shape[1] // 2
    for n, (i, b) in enumerate(pairs):
        at = sum(counts[:b])
        row = 0
        for piece in weights[at : at + counts[b]]:
            rows = slice(row, row + piece.shape[0])
            terms = jnp.dot(piece[...], contexts[i][...], preferred_element_type=F32).astype(BF16)
            keep_ref[n, rows, :] = terms[:, :half]
            send_ref[n, rows, :] = terms[:, half:]
            row += piece.shape[0]


def project(contexts, blocks, pairs):
    tokens = contexts[0].shape[1]
    cols = sum(piece.shape[0] for piece in blocks[0])
    shape = jax.ShapeDtypeStruct((len(pairs), cols, tokens // 2), BF16)
    flat = [piece for block in blocks for piece in block]
    counts = tuple(len(block) for block in blocks)
    return pl.pallas_call(
        functools.partial(project_kernel, n_ctx=len(contexts), counts=counts, pairs=pairs),
        out_shape=[shape, shape],
        in_specs=[vmem()] * (len(contexts) + len(flat)),
        out_specs=[vmem()] * 2,
        compiler_params=params(),
        cost_estimate=FREE,
        name="project",
    )(*contexts, *flat)


def fold_rows(cols):
    return -(-cols // 32) * 16


def pair_kernel(keep_ref, got_ref, *out_refs, counts):
    cols, width = keep_ref.shape[1:]
    rows = out_refs[0].shape[1]
    tok = width // 2
    low = lax.broadcasted_iota(jnp.int32, (rows, width), 1) < tok
    at = 0
    for i, count in enumerate(counts):
        for b in range(count):
            both = keep_ref[at].astype(F32) + got_ref[at].astype(F32)
            top = both[:rows]
            rest = jnp.concatenate([both[rows:], jnp.zeros((2 * rows - cols, width), F32)], axis=0)
            out_refs[2 * i][b] = jnp.where(low, top, pltpu.roll(rest, tok, 1)).astype(BF16)
            out_refs[2 * i + 1][b] = jnp.where(low, pltpu.roll(top, tok, 1), rest).astype(BF16)
            at += 1


def pair_sum(keep, got, counts):
    cols, width = keep.shape[1:]
    shapes = [jax.ShapeDtypeStruct((c, fold_rows(cols), width), BF16) for c in counts for _ in range(2)]
    return pl.pallas_call(
        functools.partial(pair_kernel, counts=counts),
        out_shape=shapes,
        in_specs=[vmem()] * 2,
        out_specs=[vmem()] * len(shapes),
        compiler_params=params(),
        cost_estimate=FREE,
        name="pair_sum",
    )(keep, got)


def final_kernel(hidden_ref, *rest, places):
    parts, out_ref, scr = rest[:-2], rest[-2], rest[-1]
    own = lax.axis_index("exp")
    inner = is_inner(own)
    tok, width = hidden_ref.shape
    rows = parts[0].shape[1]
    cols = width // lax.axis_size("exp")
    for (first, second), bits in zip(zip(parts[0::2], parts[1::2]), places):
        for b, (inner_bits, outer_bits) in enumerate(bits):
            bit = jnp.where(inner, inner_bits, outer_bits)
            both = first[b].astype(F32) + second[b].astype(F32)
            row = pl.multiple_of(jnp.bitwise_xor(own, bit) * cols, 8)
            scr[pl.ds(row, rows), :] = both
            scr[pl.ds(row + rows, cols - rows), :] = pltpu.roll(both, tok, 1)[: cols - rows]
    attn = scr[...].T[:tok]
    out_ref[...] = (hidden_ref[...].astype(F32) + attn).astype(BF16)


def finish(hidden, parts, places):
    return pl.pallas_call(
        functools.partial(final_kernel, places=places),
        out_shape=jax.ShapeDtypeStruct(hidden.shape, BF16),
        in_specs=[vmem()] * (1 + len(parts)),
        out_specs=vmem(),
        scratch_shapes=[pltpu.VMEM((hidden.shape[1], parts[0].shape[2]), F32)],
        compiler_params=params(),
        cost_estimate=FREE,
        name="finish",
    )(hidden, *parts)


def paired_plan(
    hidden_in, queries, new_kv, kv_pool, page_table, new_slots, cached_pages, sinks, out_weight
):
    tok = hidden_in.shape[1]
    n_req = lax.axis_size("req")
    head_count = sinks.shape[0]
    kv_width = new_kv.shape[2] // 2
    kv_heads = kv_width // HD
    slots_dev, page_size = kv_pool.shape[1:3]
    pool_rows = slots_dev * page_size
    weight = out_weight.T
    cols = weight.shape[0]
    cuts = [slice(cols * i // 360, cols * j // 360) for i, j in zip((0, 200), (200, 360))]
    first = swap_blocks(weight, NEAR_BIT, FAR_BIT)

    pieces = pack(queries[0], new_kv[0], kv_pool[0].reshape(pool_rows, 2 * kv_width), n_req)
    pieces = [pieces[0]] + [swap(pieces[k], k, 0) for k in range(1, n_req)]
    second = [swap_blocks(weight[cuts[0]], FAR_BIT, NEAR_BIT)]
    second += [swap_blocks(weight[cuts[1]], FAR_BIT, NEAR_BIT)]

    position = cached_pages[0] * page_size + jnp.arange(n_req * tok)
    frequency = THETA ** (-2.0 * jnp.arange(HD // 2).astype(F32) / HD)
    angles = position.astype(F32)[:, None] * frequency[None, :]
    cosine, sine = jnp.cos(angles), jnp.sin(angles)
    cosine = jnp.concatenate([cosine] * 4, axis=1)
    sine = jnp.concatenate([-sine, sine, -sine, sine], axis=1)

    ctx = attention(
        cached_pages, page_table, sinks, cosine, sine, pieces, kv_heads // n_req,
        head_count // kv_heads, pool_rows, page_size,
    )
    chip_rows = jnp.concatenate([new_kv[0], pieces[1][:, -2 * kv_width :]], axis=0)
    ctx, first, chip_rows = lax.optimization_barrier((ctx, first, chip_rows))
    ctx_mate = swap(ctx, 0, PAIR_BIT)
    inner = is_inner(lax.axis_index("exp"))
    far = [jnp.where(inner, piece, first[rows]) for rows, piece in zip(cuts, second)]
    both = [swap(chunk, 0, NEAR_BIT) for chunk in far]
    fresh = swap(chip_rows, 2, 0)
    pool_out = write_pool(new_slots, cosine, sine, kv_pool[0], [chip_rows, fresh])

    def both_sides(contexts, blocks, pairs):
        send, keep = project(contexts, blocks, pairs)
        counts = tuple(n for n in (sum(i == c for c, _ in pairs) for i in range(len(contexts))) if n)
        return pair_sum(keep, swap(send, 1, 0), counts)

    parts = []
    ctx, pool_out = lax.optimization_barrier((ctx, pool_out))
    own_part, over_y = both_sides([ctx], [[weight], [first]], ((0, 0), (0, 1)))
    parts += [own_part, swap(over_y, 2, 0)]
    ctx_mate, parts[1] = lax.optimization_barrier((ctx_mate, parts[1]))
    over_pair, over_both = both_sides([ctx_mate], [[weight], [first], second], ((0, 0), (0, 1), (0, 2)))
    parts += [swap(over_pair, 0, PAIR_BIT), swap(over_both, 2, PAIR_BIT)]
    own_part, over_y, over_pair, over_both = both_sides([ctx, ctx_mate], [second, both], ((0, 0), (0, 1), (1, 1)))
    parts += [own_part, swap(over_y, 2, 0)]
    parts += [swap(over_pair, 0, PAIR_BIT), swap(over_both, 2, PAIR_BIT)]
    own_bits, first_bits, second_bits, both_bits = (
        (0, 0), (NEAR_BIT, FAR_BIT), (FAR_BIT, NEAR_BIT), (FAR_BIT ^ NEAR_BIT,) * 2
    )

    def of_mate(bits):
        return PAIR_BIT ^ bits[1], PAIR_BIT ^ bits[0]

    places = (
        (own_bits, first_bits),
        (of_mate(own_bits), of_mate(first_bits), of_mate(second_bits)),
        (second_bits, both_bits),
        (of_mate(both_bits),),
    )
    layer_out = finish(hidden_in[0], parts, places)
    return (layer_out[None], pool_out[None])


def solution(mesh):
    paired = mesh.shape["req"] == 4 and mesh.shape["exp"] == 8
    return jax.shard_map(
        paired_plan if paired else general_plan,
        mesh=mesh,
        in_specs=(
            P("exp", "req", None),
            P("exp", "req", None),
            P("exp", "req", None),
            P("exp", "req", None, None),
            P("exp", None),
            P("exp", None),
            P("exp"),
            P(),
            P("req", "exp"),
        ),
        out_specs=(P("exp", "req", None), P("exp", "req", None, None)),
        check_vma=False,
    )
```

```python
import functools
import math

import jax
import jax.numpy as jnp
from jax import lax
from jax.experimental import pallas as pl
from jax.experimental.pallas import tpu as pltpu
from jax.sharding import PartitionSpec as P

HD = 64


THETA = 150000.0
NEGATIVE = -1e30


def rotate(values, positions):
    half_width = values.shape[-1] // 2
    frequency = THETA ** (-2.0 * jnp.arange(half_width).astype(jnp.float32) / values.shape[-1])
    angles = positions.astype(jnp.float32)[:, None] * frequency[None, :]
    cosine = jnp.cos(angles)[:, None, :]
    sine_part = jnp.sin(angles)[:, None, :]
    lower_half = values[..., :half_width]
    upper_half = values[..., half_width:]
    return jnp.concatenate(
        [
            lower_half * cosine - upper_half * sine_part,
            upper_half * cosine + lower_half * sine_part,
        ],
        axis=-1,
    )


def spread_heads(rows, head_total, kv_heads, dev_count):
    per_dev = head_total // dev_count
    per_kv = head_total // kv_heads
    repeat = max(1, per_kv // per_dev)
    kv_dev = max(1, per_dev // per_kv)
    count = rows.shape[0]
    split = jnp.repeat(rows.reshape(count, 2, kv_heads, HD), repeat, axis=2)
    split = split.reshape(count, 2, dev_count, kv_dev * HD)
    return jnp.transpose(split, (0, 2, 1, 3)).reshape(count, dev_count, 2 * kv_dev * HD)


def general_plan(
    hidden_in, queries, new_kv, kv_pool, page_table, new_slots, cached_pages, sinks, out_weight
):
    tok_dev = hidden_in.shape[1]
    n_req = lax.axis_size("req")
    own_index = lax.axis_index("req")
    fresh_count = tok_dev * n_req
    head_count = sinks.shape[0]
    kv_width = new_kv.shape[2] // 2
    kv_heads = kv_width // HD
    per_kv = head_count // kv_heads
    heads_dev = head_count // n_req
    kv_dev = max(1, heads_dev // per_kv)
    per_dev_group = heads_dev // kv_dev
    head_width = 2 * kv_dev * HD
    slots_dev = kv_pool.shape[1]
    page_size = kv_pool.shape[2]
    slot_total = slots_dev * n_req
    page_limit = page_table.shape[1]
    fresh_pages = new_slots.shape[1]
    page_count = cached_pages[0]
    start_pos = page_count * page_size
    own_pos = start_pos + own_index * tok_dev + jnp.arange(tok_dev)
    q_rot = rotate(queries[0].reshape(tok_dev, head_count, HD).astype(jnp.float32), own_pos).astype(
        jnp.bfloat16
    )
    k_rot = rotate(
        new_kv[0, :, :kv_width].reshape(tok_dev, kv_heads, HD).astype(jnp.float32), own_pos
    ).astype(jnp.bfloat16)
    kv_rot = jnp.concatenate([k_rot.reshape(tok_dev, kv_width), new_kv[0, :, kv_width:]], axis=1)
    slot_all = jnp.arange(slot_total)
    page_index = jnp.arange(page_limit)
    cached_hit = (page_table[0][None, :] == slot_all[:, None]) & (page_index[None, :] < page_count)
    is_cached = jnp.any(cached_hit, axis=1)
    cached_base = jnp.sum(jnp.where(cached_hit, page_index[None, :], 0), axis=1) * page_size
    fresh_hit = new_slots[0][None, :] == slot_all[:, None]
    is_fresh = jnp.any(fresh_hit, axis=1)
    fresh_base = (
        start_pos
        + jnp.sum(jnp.where(fresh_hit, jnp.arange(fresh_pages)[None, :], 0), axis=1) * page_size
    )
    key_pos = (
        jnp.where(is_fresh, fresh_base, cached_base)[:, None] + jnp.arange(page_size)[None, :]
    ).reshape(-1)
    key_live = jnp.repeat(is_cached | is_fresh, page_size)
    all_fresh = lax.all_gather(kv_rot, "req", axis=0, tiled=True)
    own_hit = lax.dynamic_slice_in_dim(fresh_hit, own_index * slots_dev, slots_dev, 0)
    own_fresh = lax.dynamic_slice_in_dim(is_fresh, own_index * slots_dev, slots_dev, 0)
    appended = jnp.dot(
        own_hit.astype(jnp.bfloat16),
        all_fresh.reshape(fresh_pages, page_size * 2 * kv_width),
        preferred_element_type=jnp.float32,
    )
    appended = appended.astype(jnp.bfloat16).reshape(slots_dev, page_size, 2 * kv_width)
    local_pages = jnp.where(own_fresh[:, None, None], appended, kv_pool[0])
    head_pool = lax.all_to_all(
        spread_heads(
            local_pages.reshape(slots_dev * page_size, 2 * kv_width), head_count, kv_heads, n_req
        ),
        "req",
        split_axis=1,
        concat_axis=0,
        tiled=True,
    )
    head_pool = head_pool.reshape(slot_total * page_size, head_width)
    q_here = lax.all_to_all(
        q_rot.reshape(tok_dev, n_req, heads_dev * HD),
        "req",
        split_axis=1,
        concat_axis=0,
        tiled=True,
    )
    q_here = q_here.reshape(fresh_count, heads_dev * HD)
    key_total = slot_total * page_size
    all_keys = head_pool[:, : kv_dev * HD].reshape(key_total, kv_dev, HD)
    all_values = head_pool[:, kv_dev * HD :].reshape(key_total, kv_dev, HD)
    sink_mine = lax.dynamic_slice_in_dim(sinks, own_index * heads_dev, heads_dev, 0).reshape(
        kv_dev, per_dev_group
    )
    scale = 1.0 / math.sqrt(HD)
    query_block = math.gcd(fresh_count, 128)
    contexts = []
    for block_start in range(0, fresh_count, query_block):
        block_queries = q_here[block_start : block_start + query_block].reshape(
            query_block, kv_dev, per_dev_group, HD
        )
        query_pos = start_pos + block_start + jnp.arange(query_block)
        visible = key_live[None, :] & (key_pos[None, :] <= query_pos[:, None])
        scores = (
            jnp.einsum(
                "tghd,kgd->tghk", block_queries, all_keys, preferred_element_type=jnp.float32
            )
            * scale
        )
        scores = jnp.where(visible[:, None, None, :], scores, NEGATIVE)
        top_score = jnp.maximum(jnp.max(scores, axis=-1), sink_mine[None])
        expo = jnp.where(visible[:, None, None, :], jnp.exp(scores - top_score[..., None]), 0.0)
        denominator = jnp.sum(expo, axis=-1) + jnp.exp(sink_mine[None] - top_score)
        weighted = jnp.einsum(
            "tghk,kgd->tghd",
            expo.astype(jnp.bfloat16),
            all_values,
            preferred_element_type=jnp.float32,
        )
        contexts.append(
            (weighted / denominator[..., None])
            .astype(jnp.bfloat16)
            .reshape(query_block, heads_dev * HD)
        )
    context = jnp.concatenate(contexts, axis=0)
    terms = jnp.dot(
        context,
        lax.all_gather(out_weight, "exp", axis=1, tiled=True),
        preferred_element_type=jnp.float32,
    ).astype(jnp.bfloat16)
    width = terms.shape[1]
    arrived = lax.all_to_all(
        terms.reshape(n_req, tok_dev, width), "req", split_axis=0, concat_axis=0, tiled=True
    )
    attn = jnp.sum(arrived.astype(jnp.float32), axis=0)
    layer_out = (hidden_in[0].astype(jnp.float32) + attn).astype(jnp.bfloat16)
    return (layer_out[None], local_pages[None])


VMEM_LIMIT = 24 * 1024 * 1024
FREE = pl.CostEstimate(flops=0, bytes_accessed=0, transcendentals=0)
F32 = jnp.float32
BF16 = jnp.bfloat16

PAIR_BIT, NEAR_BIT, FAR_BIT = 2, 1, 6
ORDER = (0, 2, 1, 3)


def vmem():
    return pl.BlockSpec(memory_space=pltpu.VMEM)


def smem():
    return pl.BlockSpec(memory_space=pltpu.SMEM)


def params():
    return pltpu.CompilerParams(vmem_limit_bytes=VMEM_LIMIT)


def swap(values, req_bits, exp_bits):
    if not exp_bits:
        return lax.ppermute(values, "req", [(i, i ^ req_bits) for i in range(lax.axis_size("req"))])
    if not req_bits:
        return lax.ppermute(values, "exp", [(i, i ^ exp_bits) for i in range(lax.axis_size("exp"))])
    rows, cols = lax.axis_size("req"), lax.axis_size("exp")
    pairs = [
        (i * cols + j, (i ^ req_bits) * cols + (j ^ exp_bits)) for i in range(rows) for j in range(cols)
    ]
    return lax.ppermute(values, ("req", "exp"), pairs)


def is_inner(index):
    return (index & 2) * 2 != (index & 4)


def swap_blocks(values, inner_bits, outer_bits):
    pairs = [(i, i ^ (inner_bits if is_inner(i) else outer_bits)) for i in range(lax.axis_size("exp"))]
    return lax.ppermute(values, "exp", pairs)


def pack_kernel(q_ref, kv_ref, pool_ref, *rest):
    outs, sems = rest[:-1], rest[-1]
    n_req = len(outs)
    own = lax.axis_index("req")
    tok = q_ref.shape[0]
    q_width = q_ref.shape[1] // n_req
    kv_width = kv_ref.shape[1] // 2
    head_width = kv_width // n_req
    copies = []

    def copy(source, target):
        copies.append(pltpu.make_async_copy(source, target, sems.at[len(copies)]))
        copies[-1].start()

    for k in (3, 2, 1, 0):
        out = outs[k]
        dest = jnp.bitwise_xor(own, k)
        col = pl.multiple_of(dest * q_width, 128)
        copy(q_ref.at[:, pl.ds(col, q_width)], out.at[:, pl.ds(0, q_width)])
        at = q_width
        blocks = [(kv_ref, 0)]
        blocks += [(pool_ref, i * tok) for i in range(pool_ref.shape[0] // tok)]
        for block, row in blocks:
            for half in range(2):
                col = pl.multiple_of(half * kv_width + dest * head_width, 128)
                copy(
                    block.at[pl.ds(row, tok), pl.ds(col, head_width)],
                    out.at[:, pl.ds(at, head_width)],
                )
                at += head_width
        if k == 1:
            copy(kv_ref, out.at[:, pl.ds(at, 2 * kv_width)])
    for one in copies:
        one.wait()


def pack(q, kv, pool, n_req):
    tok = q.shape[0]
    blocks = 1 + pool.shape[0] // tok
    width = (q.shape[1] + blocks * kv.shape[1]) // n_req
    widths = [width + (kv.shape[1] if k == 1 else 0) for k in range(n_req)]
    return pl.pallas_call(
        pack_kernel,
        out_shape=[jax.ShapeDtypeStruct((tok, w), BF16) for w in widths],
        in_specs=[pl.BlockSpec(memory_space=pltpu.MemorySpace.HBM)] * 3,
        out_specs=[vmem()] * n_req,
        scratch_shapes=[pltpu.SemaphoreType.DMA((n_req * (1 + 2 * blocks) + 1,))],
        compiler_params=params(),
        cost_estimate=FREE,
        name="pack",
    )(q, kv, pool)


def turn(values, cosine, sine):
    lane = lax.broadcasted_iota(jnp.int32, values.shape, 1)
    other = jnp.where(lane % HD < HD // 2, pltpu.roll(values, 128 - HD // 2, 1), pltpu.roll(values, HD // 2, 1))
    return values * cosine + other * sine


def attention_kernel(
    pages_ref, table_ref, sink_ref, cos_ref, sin_ref, *rest, kv_dev, per_kv, page_size
):
    n_req = len(rest) - 8
    pieces, out_ref = rest[:n_req], rest[n_req]
    q_scr, qt_scr, pool_scr, flat_scr, key_scr, value_scr, bias_scr = rest[n_req + 1 :]
    own = lax.axis_index("req")
    tok = pieces[0].shape[0]
    q_width = kv_dev * per_kv * HD
    head_width = kv_dev * HD
    page_limit = table_ref.shape[1]
    cached = page_limit * page_size
    fresh = tok * n_req
    total = cached + fresh
    pool_rows = pool_scr.shape[1]
    live = pages_ref[0] * page_size
    pairs = per_kv // 2
    for place, k in enumerate(ORDER):
        shard = jnp.bitwise_xor(own, k)
        row = pl.multiple_of(shard * tok, tok)
        cosine = cos_ref[pl.ds(row, tok), :]
        sine = sin_ref[pl.ds(row, tok), :]
        for p in range(kv_dev * pairs):
            col = p * 2 * HD
            turned = turn(pieces[k][:, col : col + 2 * HD].astype(F32), cosine, sine).astype(BF16)
            q_scr[p, place // 2, place % 2 * tok : (place % 2 + 1) * tok, :] = turned.astype(F32) * (1.0 / math.sqrt(HD))
        at = q_width
        key_row = pl.multiple_of(cached + row, tok)
        flat_scr[pl.ds(key_row, tok), :head_width] = turn(
            pieces[k][:, at : at + head_width].astype(F32), cosine, sine
        )
        flat_scr[pl.ds(key_row, tok), head_width:] = pieces[k][
            :, at + head_width : at + 2 * head_width
        ].astype(F32)
        at += 2 * head_width
        for i in range(pool_rows // tok):
            pool_scr[shard, i * tok : (i + 1) * tok, :] = pieces[k][:, at : at + 2 * head_width].astype(F32)
            at += 2 * head_width
        key = lax.broadcasted_iota(jnp.int32, (total, tok), 0)
        query = lax.broadcasted_iota(jnp.int32, (total, tok), 1) + (cached + shard * tok)
        last = jnp.where(key < cached, live - 1, query)
        bias_scr[:, place * tok : (place + 1) * tok] = jnp.where(key > last, NEGATIVE, 0.0)
    for p in range(kv_dev * pairs):
        for h in range(2):
            at = (p % pairs * 2 + h) * 2 * tok
            qt_scr[p // pairs, :, at : at + 2 * tok] = q_scr[p, h].T.astype(BF16)
    per_dev = pool_rows // page_size
    for j in range(page_limit):
        slot = table_ref[0, j]
        source = pl.multiple_of((slot % per_dev) * page_size, page_size)
        flat_scr[j * page_size : (j + 1) * page_size, :] = pool_scr[
            slot // per_dev, pl.ds(source, page_size), :
        ]
    flat = flat_scr[:, :head_width]
    rolled = pltpu.roll(flat, HD, 1)
    low = lax.broadcasted_iota(jnp.int32, flat.shape, 1) < HD
    zero = jnp.zeros_like(flat)
    key_scr[0] = jnp.where(low, flat, zero).astype(BF16)
    key_scr[1] = jnp.where(low, zero, rolled).astype(BF16)
    key_scr[2] = jnp.where(low, rolled, zero).astype(BF16)
    key_scr[3] = jnp.where(low, zero, flat).astype(BF16)
    value_scr[...] = flat_scr[:, head_width:].T.astype(BF16)

    def one_set(i, carry):
        g, a = i // 2, i % 2
        wide = n_req * tok
        scores = jnp.dot(key_scr[i], qt_scr[g], preferred_element_type=F32)
        weights, dens = [], []
        for p in range(pairs):
            part = scores[:, p * wide : (p + 1) * wide] + bias_scr[...]
            sink = sink_ref[own * (kv_dev * per_kv) + g * per_kv + 2 * p + a]
            top = jnp.maximum(jnp.max(part, axis=0, keepdims=True), sink)
            expo = jnp.exp(part - top)
            dens.append(jnp.sum(expo, axis=0, keepdims=True) + jnp.exp(sink - top))
            weights.append(expo.astype(BF16))
        values = value_scr[pl.ds(pl.multiple_of(g * HD, HD), HD), :]
        summed = jnp.dot(values, jnp.concatenate(weights, axis=1), preferred_element_type=F32)
        for p in range(pairs):
            row = pl.multiple_of((g * per_kv + 2 * p + a) * HD, HD)
            out_ref[pl.ds(row, HD), :] = (summed[:, p * wide : (p + 1) * wide] / dens[p]).astype(BF16)
        return carry

    lax.fori_loop(0, 2 * kv_dev, one_set, 0, unroll=True)


def attention(pages, table, sinks, cosine, sine, pieces, kv_dev, per_kv, pool_rows, page_size):
    n_req = len(pieces)
    tok = pieces[0].shape[0]
    total = table.shape[1] * page_size + n_req * tok
    head_width = kv_dev * HD
    return pl.pallas_call(
        functools.partial(attention_kernel, kv_dev=kv_dev, per_kv=per_kv, page_size=page_size),
        out_shape=jax.ShapeDtypeStruct((per_kv * head_width, n_req * tok), BF16),
        in_specs=[smem()] * 3 + [vmem()] * (2 + n_req),
        out_specs=vmem(),
        scratch_shapes=[
            pltpu.VMEM((kv_dev * per_kv // 2, 2, 2 * tok, 2 * HD), F32),
            pltpu.VMEM((kv_dev, 2 * HD, per_kv // 2 * n_req * tok), BF16),
            pltpu.VMEM((n_req, pool_rows, 2 * head_width), F32),
            pltpu.VMEM((total, 2 * head_width), F32),
            pltpu.VMEM((2 * kv_dev, total, head_width), BF16),
            pltpu.VMEM((head_width, total), BF16),
            pltpu.VMEM((total, n_req * tok), F32),
        ],
        compiler_params=params(),
        cost_estimate=FREE,
        name="attention",
    )(pages, table, sinks, cosine, sine, *pieces)


def pool_kernel(slots_ref, cos_ref, sin_ref, pool_ref, *rest, page_size):
    pairs, out_ref, fresh_scr = rest[:-2], rest[-2], rest[-1]
    own = lax.axis_index("req")
    tok = pairs[0].shape[0] // 2
    kv_width = pairs[0].shape[1] // 2
    for k in range(2 * len(pairs)):
        piece = pairs[k // 2][k % 2 * tok : (k % 2 + 1) * tok, :]
        row = pl.multiple_of(jnp.bitwise_xor(own, k) * tok, tok)
        cosine = cos_ref[pl.ds(row, tok), :]
        sine = sin_ref[pl.ds(row, tok), :]
        for col in range(0, kv_width, 128):
            turned = turn(piece[:, col : col + 128].astype(F32), cosine, sine).astype(BF16)
            fresh_scr[pl.ds(row, tok), col : col + 128] = turned
        fresh_scr[pl.ds(row, tok), kv_width:] = piece[:, kv_width:]
    out_ref[...] = pool_ref[...]
    slots_dev = out_ref.shape[0]
    for n in range(slots_ref.shape[1]):
        slot = slots_ref[0, n]

        @pl.when(slot // slots_dev == own)
        def _(slot=slot, n=n):
            out_ref[slot % slots_dev] = fresh_scr[n * page_size : (n + 1) * page_size, :]


def write_pool(slots, cosine, sine, pool, pairs):
    rows, width = pairs[0].shape
    return pl.pallas_call(
        functools.partial(pool_kernel, page_size=pool.shape[1]),
        out_shape=jax.ShapeDtypeStruct(pool.shape, BF16),
        in_specs=[smem()] + [vmem()] * (3 + len(pairs)),
        out_specs=vmem(),
        scratch_shapes=[pltpu.VMEM((rows * len(pairs), width), BF16)],
        compiler_params=params(),
        cost_estimate=FREE,
        name="write_pool",
    )(slots, cosine, sine, pool, *pairs)


def project_kernel(*refs, n_ctx, counts, pairs):
    contexts = refs[:n_ctx]
    weights = refs[n_ctx:-2]
    send_ref, keep_ref = refs[-2:]
    half = contexts[0].shape[1] // 2
    for n, (i, b) in enumerate(pairs):
        at = sum(counts[:b])
        row = 0
        for piece in weights[at : at + counts[b]]:
            rows = slice(row, row + piece.shape[0])
            terms = jnp.dot(piece[...], contexts[i][...], preferred_element_type=F32).astype(BF16)
            keep_ref[n, rows, :] = terms[:, :half]
            send_ref[n, rows, :] = terms[:, half:]
            row += piece.shape[0]


def project(contexts, blocks, pairs):
    tokens = contexts[0].shape[1]
    cols = sum(piece.shape[0] for piece in blocks[0])
    shape = jax.ShapeDtypeStruct((len(pairs), cols, tokens // 2), BF16)
    flat = [piece for block in blocks for piece in block]
    counts = tuple(len(block) for block in blocks)
    return pl.pallas_call(
        functools.partial(project_kernel, n_ctx=len(contexts), counts=counts, pairs=pairs),
        out_shape=[shape, shape],
        in_specs=[vmem()] * (len(contexts) + len(flat)),
        out_specs=[vmem()] * 2,
        compiler_params=params(),
        cost_estimate=FREE,
        name="project",
    )(*contexts, *flat)


def fold_rows(cols):
    return -(-cols // 32) * 16


def pair_kernel(keep_ref, got_ref, *out_refs, counts):
    cols, width = keep_ref.shape[1:]
    rows = out_refs[0].shape[1]
    tok = width // 2
    low = lax.broadcasted_iota(jnp.int32, (rows, width), 1) < tok
    at = 0
    for i, count in enumerate(counts):
        for b in range(count):
            both = keep_ref[at].astype(F32) + got_ref[at].astype(F32)
            top = both[:rows]
            rest = jnp.concatenate([both[rows:], jnp.zeros((2 * rows - cols, width), F32)], axis=0)
            out_refs[2 * i][b] = jnp.where(low, top, pltpu.roll(rest, tok, 1)).astype(out_refs[2 * i].dtype)
            out_refs[2 * i + 1][b] = jnp.where(low, pltpu.roll(top, tok, 1), rest).astype(BF16)
            at += 1


def pair_sum(keep, got, counts, own_first):
    cols, width = keep.shape[1:]
    shapes = [jax.ShapeDtypeStruct((c, fold_rows(cols), width), BF16) for c in counts for _ in range(2)]
    if own_first:
        shapes[0] = jax.ShapeDtypeStruct(shapes[0].shape, F32)
    return pl.pallas_call(
        functools.partial(pair_kernel, counts=counts),
        out_shape=shapes,
        in_specs=[vmem()] * 2,
        out_specs=[vmem()] * len(shapes),
        compiler_params=params(),
        cost_estimate=FREE,
        name="pair_sum",
    )(keep, got)


def final_kernel(hidden_ref, *rest, places):
    parts, out_ref, scr = rest[:-2], rest[-2], rest[-1]
    own = lax.axis_index("exp")
    inner = is_inner(own)
    tok, width = hidden_ref.shape
    rows = parts[0].shape[1]
    cols = width // lax.axis_size("exp")
    for (first, second), bits in zip(zip(parts[0::2], parts[1::2]), places):
        for b, (inner_bits, outer_bits) in enumerate(bits):
            bit = jnp.where(inner, inner_bits, outer_bits)
            both = first[b].astype(F32) + second[b].astype(F32)
            row = pl.multiple_of(jnp.bitwise_xor(own, bit) * cols, 8)
            scr[pl.ds(row, rows), :] = both
            scr[pl.ds(row + rows, cols - rows), :] = pltpu.roll(both, tok, 1)[: cols - rows]
    attn = scr[...].T[:tok]
    out_ref[...] = (hidden_ref[...].astype(F32) + attn).astype(BF16)


def finish(hidden, parts, places):
    return pl.pallas_call(
        functools.partial(final_kernel, places=places),
        out_shape=jax.ShapeDtypeStruct(hidden.shape, BF16),
        in_specs=[vmem()] * (1 + len(parts)),
        out_specs=vmem(),
        scratch_shapes=[pltpu.VMEM((hidden.shape[1], parts[0].shape[2]), F32)],
        compiler_params=params(),
        cost_estimate=FREE,
        name="finish",
    )(hidden, *parts)


def paired_plan(
    hidden_in, queries, new_kv, kv_pool, page_table, new_slots, cached_pages, sinks, out_weight
):
    tok = hidden_in.shape[1]
    n_req = lax.axis_size("req")
    head_count = sinks.shape[0]
    kv_width = new_kv.shape[2] // 2
    kv_heads = kv_width // HD
    slots_dev, page_size = kv_pool.shape[1:3]
    pool_rows = slots_dev * page_size
    weight = out_weight.T
    cols = weight.shape[0]
    cut = cols * 5 // 9
    cuts = (slice(0, cut), slice(cut, cols))
    first = swap_blocks(weight, NEAR_BIT, FAR_BIT)

    pieces = pack(queries[0], new_kv[0], kv_pool[0].reshape(pool_rows, 2 * kv_width), n_req)
    pieces = [pieces[0]] + [swap(pieces[k], k, 0) for k in range(1, n_req)]
    second = [swap_blocks(weight[cuts[0]], FAR_BIT, NEAR_BIT)]
    second += [swap_blocks(weight[cuts[1]], FAR_BIT, NEAR_BIT)]

    position = cached_pages[0] * page_size + jnp.arange(n_req * tok)
    frequency = THETA ** (-2.0 * jnp.arange(HD // 2).astype(F32) / HD)
    angles = position.astype(F32)[:, None] * frequency[None, :]
    cosine, sine = jnp.cos(angles), jnp.sin(angles)
    cosine = jnp.concatenate([cosine] * 4, axis=1)
    sine = jnp.concatenate([-sine, sine, -sine, sine], axis=1)

    ctx = attention(
        cached_pages, page_table, sinks, cosine, sine, pieces, kv_heads // n_req,
        head_count // kv_heads, pool_rows, page_size,
    )
    chip_rows = jnp.concatenate([new_kv[0], pieces[1][:, -2 * kv_width :]], axis=0)
    ctx, first, chip_rows = lax.optimization_barrier((ctx, first, chip_rows))
    ctx_mate = swap(ctx, 0, PAIR_BIT)
    inner = is_inner(lax.axis_index("exp"))
    far = [jnp.where(inner, piece, first[rows]) for rows, piece in zip(cuts, second)]
    both = [swap(chunk, 0, NEAR_BIT) for chunk in far]
    fresh = swap(chip_rows, 2, 0)

    def both_sides(contexts, blocks, pairs, own_first):
        send, keep = project(contexts, blocks, pairs)
        counts = tuple(n for n in (sum(i == c for c, _ in pairs) for i in range(len(contexts))) if n)
        return pair_sum(keep, swap(send, 1, 0), counts, own_first)

    parts = []
    ctx, fresh = lax.optimization_barrier((ctx, fresh))
    own_part, over_y = both_sides([ctx], [[weight], [first]], ((0, 0), (0, 1)), True)
    parts += [own_part, swap(over_y, 2, 0)]
    pool_out = write_pool(new_slots, cosine, sine, kv_pool[0], [chip_rows, fresh])
    ctx_mate, pool_out = lax.optimization_barrier((ctx_mate, pool_out))
    ctx_mate, parts[1] = lax.optimization_barrier((ctx_mate, parts[1]))
    over_pair, over_both = both_sides([ctx_mate], [[weight], [first], second], ((0, 0), (0, 1), (0, 2)), False)
    parts += [swap(over_pair, 0, PAIR_BIT), swap(over_both, 2, PAIR_BIT)]
    own_part, over_y, over_pair, over_both = both_sides([ctx, ctx_mate], [second, both], ((0, 0), (0, 1), (1, 1)), True)
    parts += [own_part, swap(over_y, 2, 0)]
    parts += [swap(over_pair, 0, PAIR_BIT), swap(over_both, 2, PAIR_BIT)]
    own_bits, first_bits, second_bits, both_bits = (
        (0, 0), (NEAR_BIT, FAR_BIT), (FAR_BIT, NEAR_BIT), (FAR_BIT ^ NEAR_BIT,) * 2
    )

    def of_mate(bits):
        return PAIR_BIT ^ bits[1], PAIR_BIT ^ bits[0]

    places = (
        (own_bits, first_bits),
        (of_mate(own_bits), of_mate(first_bits), of_mate(second_bits)),
        (second_bits, both_bits),
        (of_mate(both_bits),),
    )
    layer_out = finish(hidden_in[0], parts, places)
    return (layer_out[None], pool_out[None])


def solution(mesh):
    paired = mesh.shape["req"] == 4 and mesh.shape["exp"] == 8
    return jax.shard_map(
        paired_plan if paired else general_plan,
        mesh=mesh,
        in_specs=(
            P("exp", "req", None),
            P("exp", "req", None),
            P("exp", "req", None),
            P("exp", "req", None, None),
            P("exp", None),
            P("exp", None),
            P("exp"),
            P(),
            P("req", "exp"),
        ),
        out_specs=(P("exp", "req", None), P("exp", "req", None, None)),
        check_vma=False,
    )
```

```python
import functools
import math

import jax
import jax.numpy as jnp
from jax import lax
from jax.experimental import pallas as pl
from jax.experimental.pallas import tpu as pltpu
from jax.sharding import PartitionSpec as P

HD = 64


THETA = 150000.0
NEGATIVE = -1e30


def rotate(values, positions):
    half_width = values.shape[-1] // 2
    frequency = THETA ** (-2.0 * jnp.arange(half_width).astype(jnp.float32) / values.shape[-1])
    angles = positions.astype(jnp.float32)[:, None] * frequency[None, :]
    cosine = jnp.cos(angles)[:, None, :]
    sine_part = jnp.sin(angles)[:, None, :]
    lower_half = values[..., :half_width]
    upper_half = values[..., half_width:]
    return jnp.concatenate(
        [
            lower_half * cosine - upper_half * sine_part,
            upper_half * cosine + lower_half * sine_part,
        ],
        axis=-1,
    )


def spread_heads(rows, head_total, kv_heads, dev_count):
    per_dev = head_total // dev_count
    per_kv = head_total // kv_heads
    repeat = max(1, per_kv // per_dev)
    kv_dev = max(1, per_dev // per_kv)
    count = rows.shape[0]
    split = jnp.repeat(rows.reshape(count, 2, kv_heads, HD), repeat, axis=2)
    split = split.reshape(count, 2, dev_count, kv_dev * HD)
    return jnp.transpose(split, (0, 2, 1, 3)).reshape(count, dev_count, 2 * kv_dev * HD)


def general_plan(
    hidden_in, queries, new_kv, kv_pool, page_table, new_slots, cached_pages, sinks, out_weight
):
    tok_dev = hidden_in.shape[1]
    n_req = lax.axis_size("req")
    own_index = lax.axis_index("req")
    fresh_count = tok_dev * n_req
    head_count = sinks.shape[0]
    kv_width = new_kv.shape[2] // 2
    kv_heads = kv_width // HD
    per_kv = head_count // kv_heads
    heads_dev = head_count // n_req
    kv_dev = max(1, heads_dev // per_kv)
    per_dev_group = heads_dev // kv_dev
    head_width = 2 * kv_dev * HD
    slots_dev = kv_pool.shape[1]
    page_size = kv_pool.shape[2]
    slot_total = slots_dev * n_req
    page_limit = page_table.shape[1]
    fresh_pages = new_slots.shape[1]
    page_count = cached_pages[0]
    start_pos = page_count * page_size
    own_pos = start_pos + own_index * tok_dev + jnp.arange(tok_dev)
    q_rot = rotate(queries[0].reshape(tok_dev, head_count, HD).astype(jnp.float32), own_pos).astype(
        jnp.bfloat16
    )
    k_rot = rotate(
        new_kv[0, :, :kv_width].reshape(tok_dev, kv_heads, HD).astype(jnp.float32), own_pos
    ).astype(jnp.bfloat16)
    kv_rot = jnp.concatenate([k_rot.reshape(tok_dev, kv_width), new_kv[0, :, kv_width:]], axis=1)
    slot_all = jnp.arange(slot_total)
    page_index = jnp.arange(page_limit)
    cached_hit = (page_table[0][None, :] == slot_all[:, None]) & (page_index[None, :] < page_count)
    is_cached = jnp.any(cached_hit, axis=1)
    cached_base = jnp.sum(jnp.where(cached_hit, page_index[None, :], 0), axis=1) * page_size
    fresh_hit = new_slots[0][None, :] == slot_all[:, None]
    is_fresh = jnp.any(fresh_hit, axis=1)
    fresh_base = (
        start_pos
        + jnp.sum(jnp.where(fresh_hit, jnp.arange(fresh_pages)[None, :], 0), axis=1) * page_size
    )
    key_pos = (
        jnp.where(is_fresh, fresh_base, cached_base)[:, None] + jnp.arange(page_size)[None, :]
    ).reshape(-1)
    key_live = jnp.repeat(is_cached | is_fresh, page_size)
    all_fresh = lax.all_gather(kv_rot, "req", axis=0, tiled=True)
    own_hit = lax.dynamic_slice_in_dim(fresh_hit, own_index * slots_dev, slots_dev, 0)
    own_fresh = lax.dynamic_slice_in_dim(is_fresh, own_index * slots_dev, slots_dev, 0)
    appended = jnp.dot(
        own_hit.astype(jnp.bfloat16),
        all_fresh.reshape(fresh_pages, page_size * 2 * kv_width),
        preferred_element_type=jnp.float32,
    )
    appended = appended.astype(jnp.bfloat16).reshape(slots_dev, page_size, 2 * kv_width)
    local_pages = jnp.where(own_fresh[:, None, None], appended, kv_pool[0])
    head_pool = lax.all_to_all(
        spread_heads(
            local_pages.reshape(slots_dev * page_size, 2 * kv_width), head_count, kv_heads, n_req
        ),
        "req",
        split_axis=1,
        concat_axis=0,
        tiled=True,
    )
    head_pool = head_pool.reshape(slot_total * page_size, head_width)
    q_here = lax.all_to_all(
        q_rot.reshape(tok_dev, n_req, heads_dev * HD),
        "req",
        split_axis=1,
        concat_axis=0,
        tiled=True,
    )
    q_here = q_here.reshape(fresh_count, heads_dev * HD)
    key_total = slot_total * page_size
    all_keys = head_pool[:, : kv_dev * HD].reshape(key_total, kv_dev, HD)
    all_values = head_pool[:, kv_dev * HD :].reshape(key_total, kv_dev, HD)
    sink_mine = lax.dynamic_slice_in_dim(sinks, own_index * heads_dev, heads_dev, 0).reshape(
        kv_dev, per_dev_group
    )
    scale = 1.0 / math.sqrt(HD)
    query_block = math.gcd(fresh_count, 128)
    contexts = []
    for block_start in range(0, fresh_count, query_block):
        block_queries = q_here[block_start : block_start + query_block].reshape(
            query_block, kv_dev, per_dev_group, HD
        )
        query_pos = start_pos + block_start + jnp.arange(query_block)
        visible = key_live[None, :] & (key_pos[None, :] <= query_pos[:, None])
        scores = (
            jnp.einsum(
                "tghd,kgd->tghk", block_queries, all_keys, preferred_element_type=jnp.float32
            )
            * scale
        )
        scores = jnp.where(visible[:, None, None, :], scores, NEGATIVE)
        top_score = jnp.maximum(jnp.max(scores, axis=-1), sink_mine[None])
        expo = jnp.where(visible[:, None, None, :], jnp.exp(scores - top_score[..., None]), 0.0)
        denominator = jnp.sum(expo, axis=-1) + jnp.exp(sink_mine[None] - top_score)
        weighted = jnp.einsum(
            "tghk,kgd->tghd",
            expo.astype(jnp.bfloat16),
            all_values,
            preferred_element_type=jnp.float32,
        )
        contexts.append(
            (weighted / denominator[..., None])
            .astype(jnp.bfloat16)
            .reshape(query_block, heads_dev * HD)
        )
    context = jnp.concatenate(contexts, axis=0)
    terms = jnp.dot(
        context,
        lax.all_gather(out_weight, "exp", axis=1, tiled=True),
        preferred_element_type=jnp.float32,
    ).astype(jnp.bfloat16)
    width = terms.shape[1]
    arrived = lax.all_to_all(
        terms.reshape(n_req, tok_dev, width), "req", split_axis=0, concat_axis=0, tiled=True
    )
    attn = jnp.sum(arrived.astype(jnp.float32), axis=0)
    layer_out = (hidden_in[0].astype(jnp.float32) + attn).astype(jnp.bfloat16)
    return (layer_out[None], local_pages[None])


VMEM_LIMIT = 24 * 1024 * 1024
FREE = pl.CostEstimate(flops=0, bytes_accessed=0, transcendentals=0)
F32 = jnp.float32
BF16 = jnp.bfloat16

PAIR_BIT, NEAR_BIT, FAR_BIT = 2, 1, 6
ORDER = (0, 2, 1, 3)


def vmem():
    return pl.BlockSpec(memory_space=pltpu.VMEM)


def smem():
    return pl.BlockSpec(memory_space=pltpu.SMEM)


def params():
    return pltpu.CompilerParams(vmem_limit_bytes=VMEM_LIMIT)


def swap(values, req_bits, exp_bits):
    if not exp_bits:
        return lax.ppermute(values, "req", [(i, i ^ req_bits) for i in range(lax.axis_size("req"))])
    if not req_bits:
        return lax.ppermute(values, "exp", [(i, i ^ exp_bits) for i in range(lax.axis_size("exp"))])
    rows, cols = lax.axis_size("req"), lax.axis_size("exp")
    pairs = [
        (i * cols + j, (i ^ req_bits) * cols + (j ^ exp_bits)) for i in range(rows) for j in range(cols)
    ]
    return lax.ppermute(values, ("req", "exp"), pairs)


def is_inner(index):
    return (index & 2) * 2 != (index & 4)


def swap_blocks(values, inner_bits, outer_bits):
    pairs = [(i, i ^ (inner_bits if is_inner(i) else outer_bits)) for i in range(lax.axis_size("exp"))]
    return lax.ppermute(values, "exp", pairs)


def pack_kernel(q_ref, kv_ref, pool_ref, *rest):
    outs, sems = rest[:-1], rest[-1]
    n_req = len(outs)
    own = lax.axis_index("req")
    tok = q_ref.shape[0]
    q_width = q_ref.shape[1] // n_req
    kv_width = kv_ref.shape[1] // 2
    head_width = kv_width // n_req
    copies = []

    def copy(source, target):
        copies.append(pltpu.make_async_copy(source, target, sems.at[len(copies)]))
        copies[-1].start()

    for k in (3, 2, 1, 0):
        out = outs[k]
        dest = jnp.bitwise_xor(own, k)
        col = pl.multiple_of(dest * q_width, 128)
        copy(q_ref.at[:, pl.ds(col, q_width)], out.at[:, pl.ds(0, q_width)])
        at = q_width
        blocks = [(kv_ref, 0)]
        blocks += [(pool_ref, i * tok) for i in range(pool_ref.shape[0] // tok)]
        for block, row in blocks:
            for half in range(2):
                col = pl.multiple_of(half * kv_width + dest * head_width, 128)
                copy(
                    block.at[pl.ds(row, tok), pl.ds(col, head_width)],
                    out.at[:, pl.ds(at, head_width)],
                )
                at += head_width
        if k == 1:
            copy(kv_ref, out.at[:, pl.ds(at, 2 * kv_width)])
    for one in copies:
        one.wait()


def pack(q, kv, pool, n_req):
    tok = q.shape[0]
    blocks = 1 + pool.shape[0] // tok
    width = (q.shape[1] + blocks * kv.shape[1]) // n_req
    widths = [width + (kv.shape[1] if k == 1 else 0) for k in range(n_req)]
    return pl.pallas_call(
        pack_kernel,
        out_shape=[jax.ShapeDtypeStruct((tok, w), BF16) for w in widths],
        in_specs=[pl.BlockSpec(memory_space=pltpu.MemorySpace.HBM)] * 3,
        out_specs=[vmem()] * n_req,
        scratch_shapes=[pltpu.SemaphoreType.DMA((n_req * (1 + 2 * blocks) + 1,))],
        compiler_params=params(),
        cost_estimate=FREE,
        name="pack",
    )(q, kv, pool)


def turn(values, cosine, sine):
    lane = lax.broadcasted_iota(jnp.int32, values.shape, 1)
    other = jnp.where(lane % HD < HD // 2, pltpu.roll(values, 128 - HD // 2, 1), pltpu.roll(values, HD // 2, 1))
    return values * cosine + other * sine


def attention_kernel(
    pages_ref, table_ref, sink_ref, cos_ref, sin_ref, *rest, kv_dev, per_kv, page_size
):
    n_req = len(rest) - 8
    pieces, out_ref = rest[:n_req], rest[n_req]
    q_scr, qt_scr, pool_scr, flat_scr, key_scr, value_scr, bias_scr = rest[n_req + 1 :]
    own = lax.axis_index("req")
    tok = pieces[0].shape[0]
    q_width = kv_dev * per_kv * HD
    head_width = kv_dev * HD
    page_limit = table_ref.shape[1]
    cached = page_limit * page_size
    fresh = tok * n_req
    total = cached + fresh
    pool_rows = pool_scr.shape[1]
    live = pages_ref[0] * page_size
    pairs = per_kv // 2
    for place, k in enumerate(ORDER):
        shard = jnp.bitwise_xor(own, k)
        row = pl.multiple_of(shard * tok, tok)
        cosine = cos_ref[pl.ds(row, tok), :]
        sine = sin_ref[pl.ds(row, tok), :]
        for p in range(kv_dev * pairs):
            col = p * 2 * HD
            turned = turn(pieces[k][:, col : col + 2 * HD].astype(F32), cosine, sine).astype(BF16)
            q_scr[p, place // 2, place % 2 * tok : (place % 2 + 1) * tok, :] = turned.astype(F32) * (1.0 / math.sqrt(HD))
        at = q_width
        key_row = pl.multiple_of(cached + row, tok)
        flat_scr[pl.ds(key_row, tok), :head_width] = turn(
            pieces[k][:, at : at + head_width].astype(F32), cosine, sine
        )
        flat_scr[pl.ds(key_row, tok), head_width:] = pieces[k][
            :, at + head_width : at + 2 * head_width
        ].astype(F32)
        at += 2 * head_width
        for i in range(pool_rows // tok):
            pool_scr[shard, i * tok : (i + 1) * tok, :] = pieces[k][:, at : at + 2 * head_width].astype(F32)
            at += 2 * head_width
        key = lax.broadcasted_iota(jnp.int32, (total, tok), 0)
        query = lax.broadcasted_iota(jnp.int32, (total, tok), 1) + (cached + shard * tok)
        last = jnp.where(key < cached, live - 1, query)
        bias_scr[:, place * tok : (place + 1) * tok] = jnp.where(key > last, NEGATIVE, 0.0)
    for p in range(kv_dev * pairs):
        for h in range(2):
            at = (p % pairs * 2 + h) * 2 * tok
            qt_scr[p // pairs, :, at : at + 2 * tok] = q_scr[p, h].T.astype(BF16)
    per_dev = pool_rows // page_size
    for j in range(page_limit):
        slot = table_ref[0, j]
        source = pl.multiple_of((slot % per_dev) * page_size, page_size)
        flat_scr[j * page_size : (j + 1) * page_size, :] = pool_scr[
            slot // per_dev, pl.ds(source, page_size), :
        ]
    flat = flat_scr[:, :head_width]
    rolled = pltpu.roll(flat, HD, 1)
    low = lax.broadcasted_iota(jnp.int32, flat.shape, 1) < HD
    zero = jnp.zeros_like(flat)
    key_scr[0] = jnp.where(low, flat, zero).astype(BF16)
    key_scr[1] = jnp.where(low, zero, rolled).astype(BF16)
    key_scr[2] = jnp.where(low, rolled, zero).astype(BF16)
    key_scr[3] = jnp.where(low, zero, flat).astype(BF16)
    value_scr[...] = flat_scr[:, head_width:].T.astype(BF16)

    def one_set(i, carry):
        g, a = i // 2, i % 2
        wide = n_req * tok
        scores = jnp.dot(key_scr[i], qt_scr[g], preferred_element_type=F32)
        weights, dens = [], []
        for p in range(pairs):
            part = scores[:, p * wide : (p + 1) * wide] + bias_scr[...]
            sink = sink_ref[own * (kv_dev * per_kv) + g * per_kv + 2 * p + a]
            top = jnp.maximum(jnp.max(part, axis=0, keepdims=True), sink)
            expo = jnp.exp(part - top)
            dens.append(jnp.sum(expo, axis=0, keepdims=True) + jnp.exp(sink - top))
            weights.append(expo.astype(BF16))
        values = value_scr[pl.ds(pl.multiple_of(g * HD, HD), HD), :]
        summed = jnp.dot(values, jnp.concatenate(weights, axis=1), preferred_element_type=F32)
        for p in range(pairs):
            row = pl.multiple_of((g * per_kv + 2 * p + a) * HD, HD)
            out_ref[pl.ds(row, HD), :] = (summed[:, p * wide : (p + 1) * wide] / dens[p]).astype(BF16)
        return carry

    lax.fori_loop(0, 2 * kv_dev, one_set, 0, unroll=True)


def attention(pages, table, sinks, cosine, sine, pieces, kv_dev, per_kv, pool_rows, page_size):
    n_req = len(pieces)
    tok = pieces[0].shape[0]
    total = table.shape[1] * page_size + n_req * tok
    head_width = kv_dev * HD
    return pl.pallas_call(
        functools.partial(attention_kernel, kv_dev=kv_dev, per_kv=per_kv, page_size=page_size),
        out_shape=jax.ShapeDtypeStruct((per_kv * head_width, n_req * tok), BF16),
        in_specs=[smem()] * 3 + [vmem()] * (2 + n_req),
        out_specs=vmem(),
        scratch_shapes=[
            pltpu.VMEM((kv_dev * per_kv // 2, 2, 2 * tok, 2 * HD), F32),
            pltpu.VMEM((kv_dev, 2 * HD, per_kv // 2 * n_req * tok), BF16),
            pltpu.VMEM((n_req, pool_rows, 2 * head_width), F32),
            pltpu.VMEM((total, 2 * head_width), F32),
            pltpu.VMEM((2 * kv_dev, total, head_width), BF16),
            pltpu.VMEM((head_width, total), BF16),
            pltpu.VMEM((total, n_req * tok), F32),
        ],
        compiler_params=params(),
        cost_estimate=FREE,
        name="attention",
    )(pages, table, sinks, cosine, sine, *pieces)


def pool_kernel(slots_ref, cos_ref, sin_ref, pool_ref, *rest, page_size):
    pairs, out_ref, fresh_scr = rest[:-2], rest[-2], rest[-1]
    own = lax.axis_index("req")
    tok = pairs[0].shape[0] // 2
    kv_width = pairs[0].shape[1] // 2
    for k in range(2 * len(pairs)):
        piece = pairs[k // 2][k % 2 * tok : (k % 2 + 1) * tok, :]
        row = pl.multiple_of(jnp.bitwise_xor(own, k) * tok, tok)
        cosine = cos_ref[pl.ds(row, tok), :]
        sine = sin_ref[pl.ds(row, tok), :]
        for col in range(0, kv_width, 128):
            turned = turn(piece[:, col : col + 128].astype(F32), cosine, sine).astype(BF16)
            fresh_scr[pl.ds(row, tok), col : col + 128] = turned
        fresh_scr[pl.ds(row, tok), kv_width:] = piece[:, kv_width:]
    out_ref[...] = pool_ref[...]
    slots_dev = out_ref.shape[0]
    for n in range(slots_ref.shape[1]):
        slot = slots_ref[0, n]

        @pl.when(slot // slots_dev == own)
        def _(slot=slot, n=n):
            out_ref[slot % slots_dev] = fresh_scr[n * page_size : (n + 1) * page_size, :]


def write_pool(slots, cosine, sine, pool, pairs):
    rows, width = pairs[0].shape
    return pl.pallas_call(
        functools.partial(pool_kernel, page_size=pool.shape[1]),
        out_shape=jax.ShapeDtypeStruct(pool.shape, BF16),
        in_specs=[smem()] + [vmem()] * (3 + len(pairs)),
        out_specs=vmem(),
        scratch_shapes=[pltpu.VMEM((rows * len(pairs), width), BF16)],
        compiler_params=params(),
        cost_estimate=FREE,
        name="write_pool",
    )(slots, cosine, sine, pool, *pairs)


def project_kernel(*refs, n_ctx, counts, pairs):
    contexts = refs[:n_ctx]
    weights = refs[n_ctx:-2]
    send_ref, keep_ref = refs[-2:]
    half = contexts[0].shape[1] // 2
    for n, (i, b) in enumerate(pairs):
        at = sum(counts[:b])
        row = 0
        for piece in weights[at : at + counts[b]]:
            rows = slice(row, row + piece.shape[0])
            terms = jnp.dot(piece[...], contexts[i][...], preferred_element_type=F32).astype(BF16)
            keep_ref[n, rows, :] = terms[:, :half]
            send_ref[n, rows, :] = terms[:, half:]
            row += piece.shape[0]


def project(contexts, blocks, pairs):
    tokens = contexts[0].shape[1]
    cols = sum(piece.shape[0] for piece in blocks[0])
    shape = jax.ShapeDtypeStruct((len(pairs), cols, tokens // 2), BF16)
    flat = [piece for block in blocks for piece in block]
    counts = tuple(len(block) for block in blocks)
    return pl.pallas_call(
        functools.partial(project_kernel, n_ctx=len(contexts), counts=counts, pairs=pairs),
        out_shape=[shape, shape],
        in_specs=[vmem()] * (len(contexts) + len(flat)),
        out_specs=[vmem()] * 2,
        compiler_params=params(),
        cost_estimate=FREE,
        name="project",
    )(*contexts, *flat)


def fold_rows(cols):
    return -(-cols // 32) * 16


def pair_kernel(keep_ref, got_ref, *out_refs, counts):
    cols, width = keep_ref.shape[1:]
    rows = out_refs[0].shape[1]
    tok = width // 2
    low = lax.broadcasted_iota(jnp.int32, (rows, width), 1) < tok
    at = 0
    for i, count in enumerate(counts):
        for b in range(count):
            both = keep_ref[at].astype(F32) + got_ref[at].astype(F32)
            top = both[:rows]
            rest = jnp.concatenate([both[rows:], jnp.zeros((2 * rows - cols, width), F32)], axis=0)
            out_refs[2 * i][b] = jnp.where(low, top, pltpu.roll(rest, tok, 1)).astype(out_refs[2 * i].dtype)
            out_refs[2 * i + 1][b] = jnp.where(low, pltpu.roll(top, tok, 1), rest).astype(BF16)
            at += 1


def pair_sum(keep, got, counts, own_first):
    cols, width = keep.shape[1:]
    shapes = [jax.ShapeDtypeStruct((c, fold_rows(cols), width), BF16) for c in counts for _ in range(2)]
    if own_first:
        shapes[0] = jax.ShapeDtypeStruct(shapes[0].shape, F32)
    return pl.pallas_call(
        functools.partial(pair_kernel, counts=counts),
        out_shape=shapes,
        in_specs=[vmem()] * 2,
        out_specs=[vmem()] * len(shapes),
        compiler_params=params(),
        cost_estimate=FREE,
        name="pair_sum",
    )(keep, got)


def final_kernel(hidden_ref, *rest, places):
    parts, out_ref, scr = rest[:-2], rest[-2], rest[-1]
    own = lax.axis_index("exp")
    inner = is_inner(own)
    tok, width = hidden_ref.shape
    rows = parts[0].shape[1]
    cols = width // lax.axis_size("exp")
    for (first, second), bits in zip(zip(parts[0::2], parts[1::2]), places):
        for b, (inner_bits, outer_bits) in enumerate(bits):
            bit = jnp.where(inner, inner_bits, outer_bits)
            both = first[b].astype(F32) + second[b].astype(F32)
            row = pl.multiple_of(jnp.bitwise_xor(own, bit) * cols, 8)
            scr[pl.ds(row, rows), :] = both
            scr[pl.ds(row + rows, cols - rows), :] = pltpu.roll(both, tok, 1)[: cols - rows]
    attn = scr[...].T[:tok]
    out_ref[...] = (hidden_ref[...].astype(F32) + attn).astype(BF16)


def finish(hidden, parts, places):
    return pl.pallas_call(
        functools.partial(final_kernel, places=places),
        out_shape=jax.ShapeDtypeStruct(hidden.shape, BF16),
        in_specs=[vmem()] * (1 + len(parts)),
        out_specs=vmem(),
        scratch_shapes=[pltpu.VMEM((hidden.shape[1], parts[0].shape[2]), F32)],
        compiler_params=params(),
        cost_estimate=FREE,
        name="finish",
    )(hidden, *parts)


def paired_plan(
    hidden_in, queries, new_kv, kv_pool, page_table, new_slots, cached_pages, sinks, out_weight
):
    tok = hidden_in.shape[1]
    n_req = lax.axis_size("req")
    head_count = sinks.shape[0]
    kv_width = new_kv.shape[2] // 2
    kv_heads = kv_width // HD
    slots_dev, page_size = kv_pool.shape[1:3]
    pool_rows = slots_dev * page_size
    weight = out_weight.T
    cols = weight.shape[0]
    cut = cols // 32 * 16
    cuts = (slice(0, cut), slice(cut, cols))
    first = swap_blocks(weight, NEAR_BIT, FAR_BIT)

    pieces = pack(queries[0], new_kv[0], kv_pool[0].reshape(pool_rows, 2 * kv_width), n_req)
    pieces = [pieces[0]] + [swap(pieces[k], k, 0) for k in range(1, n_req)]
    second = [swap_blocks(weight[cuts[0]], FAR_BIT, NEAR_BIT)]
    second += [swap_blocks(weight[cuts[1]], FAR_BIT, NEAR_BIT)]

    position = cached_pages[0] * page_size + jnp.arange(n_req * tok)
    frequency = THETA ** (-2.0 * jnp.arange(HD // 2).astype(F32) / HD)
    angles = position.astype(F32)[:, None] * frequency[None, :]
    cosine, sine = jnp.cos(angles), jnp.sin(angles)
    cosine = jnp.concatenate([cosine] * 4, axis=1)
    sine = jnp.concatenate([-sine, sine, -sine, sine], axis=1)

    ctx = attention(
        cached_pages, page_table, sinks, cosine, sine, pieces, kv_heads // n_req,
        head_count // kv_heads, pool_rows, page_size,
    )
    chip_rows = jnp.concatenate([new_kv[0], pieces[1][:, -2 * kv_width :]], axis=0)
    ctx, first, chip_rows = lax.optimization_barrier((ctx, first, chip_rows))
    ctx_mate = swap(ctx, 0, PAIR_BIT)
    inner = is_inner(lax.axis_index("exp"))
    far = [jnp.where(inner, piece, first[rows]) for rows, piece in zip(cuts, second)]
    both = [swap(chunk, 0, NEAR_BIT) for chunk in far]
    fresh = swap(chip_rows, 2, 0)

    def both_sides(contexts, blocks, pairs, own_first):
        send, keep = project(contexts, blocks, pairs)
        counts = tuple(n for n in (sum(i == c for c, _ in pairs) for i in range(len(contexts))) if n)
        return pair_sum(keep, swap(send, 1, 0), counts, own_first)

    parts = []
    ctx, fresh = lax.optimization_barrier((ctx, fresh))
    own_part, over_y = both_sides([ctx], [[weight], [first]], ((0, 0), (0, 1)), True)
    parts += [own_part, swap(over_y, 2, 0)]
    pool_out = write_pool(new_slots, cosine, sine, kv_pool[0], [chip_rows, fresh])
    ctx_mate, pool_out = lax.optimization_barrier((ctx_mate, pool_out))
    ctx_mate, parts[1] = lax.optimization_barrier((ctx_mate, parts[1]))
    over_pair, over_both = both_sides([ctx_mate], [[weight], [first], second], ((0, 0), (0, 1), (0, 2)), False)
    parts += [swap(over_pair, 0, PAIR_BIT), swap(over_both, 2, PAIR_BIT)]
    own_part, over_y, over_pair, over_both = both_sides([ctx, ctx_mate], [second, both], ((0, 0), (0, 1), (1, 1)), True)
    parts += [own_part, swap(over_y, 2, 0)]
    parts += [swap(over_pair, 0, PAIR_BIT), swap(over_both, 2, PAIR_BIT)]
    own_bits, first_bits, second_bits, both_bits = (
        (0, 0), (NEAR_BIT, FAR_BIT), (FAR_BIT, NEAR_BIT), (FAR_BIT ^ NEAR_BIT,) * 2
    )

    def of_mate(bits):
        return PAIR_BIT ^ bits[1], PAIR_BIT ^ bits[0]

    places = (
        (own_bits, first_bits),
        (of_mate(own_bits), of_mate(first_bits), of_mate(second_bits)),
        (second_bits, both_bits),
        (of_mate(both_bits),),
    )
    layer_out = finish(hidden_in[0], parts, places)
    return (layer_out[None], pool_out[None])


def solution(mesh):
    paired = mesh.shape["req"] == 4 and mesh.shape["exp"] == 8
    return jax.shard_map(
        paired_plan if paired else general_plan,
        mesh=mesh,
        in_specs=(
            P("exp", "req", None),
            P("exp", "req", None),
            P("exp", "req", None),
            P("exp", "req", None, None),
            P("exp", None),
            P("exp", None),
            P("exp"),
            P(),
            P("req", "exp"),
        ),
        out_specs=(P("exp", "req", None), P("exp", "req", None, None)),
        check_vma=False,
    )
```

```python
import functools
import math

import jax
import jax.numpy as jnp
from jax import lax
from jax.experimental import pallas as pl
from jax.experimental.pallas import tpu as pltpu
from jax.sharding import PartitionSpec as P

HD = 64


THETA = 150000.0
NEGATIVE = -1e30


def rotate(values, positions):
    half_width = values.shape[-1] // 2
    frequency = THETA ** (-2.0 * jnp.arange(half_width).astype(jnp.float32) / values.shape[-1])
    angles = positions.astype(jnp.float32)[:, None] * frequency[None, :]
    cosine = jnp.cos(angles)[:, None, :]
    sine_part = jnp.sin(angles)[:, None, :]
    lower_half = values[..., :half_width]
    upper_half = values[..., half_width:]
    return jnp.concatenate(
        [
            lower_half * cosine - upper_half * sine_part,
            upper_half * cosine + lower_half * sine_part,
        ],
        axis=-1,
    )


def spread_heads(rows, head_total, kv_heads, dev_count):
    per_dev = head_total // dev_count
    per_kv = head_total // kv_heads
    repeat = max(1, per_kv // per_dev)
    kv_dev = max(1, per_dev // per_kv)
    count = rows.shape[0]
    split = jnp.repeat(rows.reshape(count, 2, kv_heads, HD), repeat, axis=2)
    split = split.reshape(count, 2, dev_count, kv_dev * HD)
    return jnp.transpose(split, (0, 2, 1, 3)).reshape(count, dev_count, 2 * kv_dev * HD)


def general_plan(
    hidden_in, queries, new_kv, kv_pool, page_table, new_slots, cached_pages, sinks, out_weight
):
    tok_dev = hidden_in.shape[1]
    n_req = lax.axis_size("req")
    own_index = lax.axis_index("req")
    fresh_count = tok_dev * n_req
    head_count = sinks.shape[0]
    kv_width = new_kv.shape[2] // 2
    kv_heads = kv_width // HD
    per_kv = head_count // kv_heads
    heads_dev = head_count // n_req
    kv_dev = max(1, heads_dev // per_kv)
    per_dev_group = heads_dev // kv_dev
    head_width = 2 * kv_dev * HD
    slots_dev = kv_pool.shape[1]
    page_size = kv_pool.shape[2]
    slot_total = slots_dev * n_req
    page_limit = page_table.shape[1]
    fresh_pages = new_slots.shape[1]
    page_count = cached_pages[0]
    start_pos = page_count * page_size
    own_pos = start_pos + own_index * tok_dev + jnp.arange(tok_dev)
    q_rot = rotate(queries[0].reshape(tok_dev, head_count, HD).astype(jnp.float32), own_pos).astype(
        jnp.bfloat16
    )
    k_rot = rotate(
        new_kv[0, :, :kv_width].reshape(tok_dev, kv_heads, HD).astype(jnp.float32), own_pos
    ).astype(jnp.bfloat16)
    kv_rot = jnp.concatenate([k_rot.reshape(tok_dev, kv_width), new_kv[0, :, kv_width:]], axis=1)
    slot_all = jnp.arange(slot_total)
    page_index = jnp.arange(page_limit)
    cached_hit = (page_table[0][None, :] == slot_all[:, None]) & (page_index[None, :] < page_count)
    is_cached = jnp.any(cached_hit, axis=1)
    cached_base = jnp.sum(jnp.where(cached_hit, page_index[None, :], 0), axis=1) * page_size
    fresh_hit = new_slots[0][None, :] == slot_all[:, None]
    is_fresh = jnp.any(fresh_hit, axis=1)
    fresh_base = (
        start_pos
        + jnp.sum(jnp.where(fresh_hit, jnp.arange(fresh_pages)[None, :], 0), axis=1) * page_size
    )
    key_pos = (
        jnp.where(is_fresh, fresh_base, cached_base)[:, None] + jnp.arange(page_size)[None, :]
    ).reshape(-1)
    key_live = jnp.repeat(is_cached | is_fresh, page_size)
    all_fresh = lax.all_gather(kv_rot, "req", axis=0, tiled=True)
    own_hit = lax.dynamic_slice_in_dim(fresh_hit, own_index * slots_dev, slots_dev, 0)
    own_fresh = lax.dynamic_slice_in_dim(is_fresh, own_index * slots_dev, slots_dev, 0)
    appended = jnp.dot(
        own_hit.astype(jnp.bfloat16),
        all_fresh.reshape(fresh_pages, page_size * 2 * kv_width),
        preferred_element_type=jnp.float32,
    )
    appended = appended.astype(jnp.bfloat16).reshape(slots_dev, page_size, 2 * kv_width)
    local_pages = jnp.where(own_fresh[:, None, None], appended, kv_pool[0])
    head_pool = lax.all_to_all(
        spread_heads(
            local_pages.reshape(slots_dev * page_size, 2 * kv_width), head_count, kv_heads, n_req
        ),
        "req",
        split_axis=1,
        concat_axis=0,
        tiled=True,
    )
    head_pool = head_pool.reshape(slot_total * page_size, head_width)
    q_here = lax.all_to_all(
        q_rot.reshape(tok_dev, n_req, heads_dev * HD),
        "req",
        split_axis=1,
        concat_axis=0,
        tiled=True,
    )
    q_here = q_here.reshape(fresh_count, heads_dev * HD)
    key_total = slot_total * page_size
    all_keys = head_pool[:, : kv_dev * HD].reshape(key_total, kv_dev, HD)
    all_values = head_pool[:, kv_dev * HD :].reshape(key_total, kv_dev, HD)
    sink_mine = lax.dynamic_slice_in_dim(sinks, own_index * heads_dev, heads_dev, 0).reshape(
        kv_dev, per_dev_group
    )
    scale = 1.0 / math.sqrt(HD)
    query_block = math.gcd(fresh_count, 128)
    contexts = []
    for block_start in range(0, fresh_count, query_block):
        block_queries = q_here[block_start : block_start + query_block].reshape(
            query_block, kv_dev, per_dev_group, HD
        )
        query_pos = start_pos + block_start + jnp.arange(query_block)
        visible = key_live[None, :] & (key_pos[None, :] <= query_pos[:, None])
        scores = (
            jnp.einsum(
                "tghd,kgd->tghk", block_queries, all_keys, preferred_element_type=jnp.float32
            )
            * scale
        )
        scores = jnp.where(visible[:, None, None, :], scores, NEGATIVE)
        top_score = jnp.maximum(jnp.max(scores, axis=-1), sink_mine[None])
        expo = jnp.where(visible[:, None, None, :], jnp.exp(scores - top_score[..., None]), 0.0)
        denominator = jnp.sum(expo, axis=-1) + jnp.exp(sink_mine[None] - top_score)
        weighted = jnp.einsum(
            "tghk,kgd->tghd",
            expo.astype(jnp.bfloat16),
            all_values,
            preferred_element_type=jnp.float32,
        )
        contexts.append(
            (weighted / denominator[..., None])
            .astype(jnp.bfloat16)
            .reshape(query_block, heads_dev * HD)
        )
    context = jnp.concatenate(contexts, axis=0)
    terms = jnp.dot(
        context,
        lax.all_gather(out_weight, "exp", axis=1, tiled=True),
        preferred_element_type=jnp.float32,
    ).astype(jnp.bfloat16)
    width = terms.shape[1]
    arrived = lax.all_to_all(
        terms.reshape(n_req, tok_dev, width), "req", split_axis=0, concat_axis=0, tiled=True
    )
    attn = jnp.sum(arrived.astype(jnp.float32), axis=0)
    layer_out = (hidden_in[0].astype(jnp.float32) + attn).astype(jnp.bfloat16)
    return (layer_out[None], local_pages[None])


VMEM_LIMIT = 24 * 1024 * 1024
FREE = pl.CostEstimate(flops=0, bytes_accessed=0, transcendentals=0)
F32 = jnp.float32
BF16 = jnp.bfloat16

PAIR_BIT, NEAR_BIT, FAR_BIT = 2, 1, 6
ORDER = (0, 2, 1, 3)


def vmem():
    return pl.BlockSpec(memory_space=pltpu.VMEM)


def smem():
    return pl.BlockSpec(memory_space=pltpu.SMEM)


def params():
    return pltpu.CompilerParams(vmem_limit_bytes=VMEM_LIMIT)


def swap(values, req_bits, exp_bits):
    if not exp_bits:
        return lax.ppermute(values, "req", [(i, i ^ req_bits) for i in range(lax.axis_size("req"))])
    if not req_bits:
        return lax.ppermute(values, "exp", [(i, i ^ exp_bits) for i in range(lax.axis_size("exp"))])
    rows, cols = lax.axis_size("req"), lax.axis_size("exp")
    pairs = [
        (i * cols + j, (i ^ req_bits) * cols + (j ^ exp_bits)) for i in range(rows) for j in range(cols)
    ]
    return lax.ppermute(values, ("req", "exp"), pairs)


def is_inner(index):
    return (index & 2) * 2 != (index & 4)


def swap_blocks(values, inner_bits, outer_bits):
    pairs = [(i, i ^ (inner_bits if is_inner(i) else outer_bits)) for i in range(lax.axis_size("exp"))]
    return lax.ppermute(values, "exp", pairs)


def pack_kernel(q_ref, kv_ref, pool_ref, *rest):
    outs, sems = rest[:-1], rest[-1]
    n_req = len(outs)
    own = lax.axis_index("req")
    tok = q_ref.shape[0]
    q_width = q_ref.shape[1] // n_req
    kv_width = kv_ref.shape[1] // 2
    head_width = kv_width // n_req
    copies = []

    def copy(source, target):
        copies.append(pltpu.make_async_copy(source, target, sems.at[len(copies)]))
        copies[-1].start()

    for k in (3, 2, 1, 0):
        out = outs[k]
        dest = jnp.bitwise_xor(own, k)
        col = pl.multiple_of(dest * q_width, 128)
        copy(q_ref.at[:, pl.ds(col, q_width)], out.at[:, pl.ds(0, q_width)])
        at = q_width
        blocks = [(kv_ref, 0)]
        blocks += [(pool_ref, i * tok) for i in range(pool_ref.shape[0] // tok)]
        for block, row in blocks:
            for half in range(2):
                col = pl.multiple_of(half * kv_width + dest * head_width, 128)
                copy(
                    block.at[pl.ds(row, tok), pl.ds(col, head_width)],
                    out.at[:, pl.ds(at, head_width)],
                )
                at += head_width
        if k == 1:
            copy(kv_ref, out.at[:, pl.ds(at, 2 * kv_width)])
    for one in copies:
        one.wait()


def pack(q, kv, pool, n_req):
    tok = q.shape[0]
    blocks = 1 + pool.shape[0] // tok
    width = (q.shape[1] + blocks * kv.shape[1]) // n_req
    widths = [width + (kv.shape[1] if k == 1 else 0) for k in range(n_req)]
    return pl.pallas_call(
        pack_kernel,
        out_shape=[jax.ShapeDtypeStruct((tok, w), BF16) for w in widths],
        in_specs=[pl.BlockSpec(memory_space=pltpu.MemorySpace.HBM)] * 3,
        out_specs=[vmem()] * n_req,
        scratch_shapes=[pltpu.SemaphoreType.DMA((n_req * (1 + 2 * blocks) + 1,))],
        compiler_params=params(),
        cost_estimate=FREE,
        name="pack",
    )(q, kv, pool)


def turn(values, cosine, sine):
    lane = lax.broadcasted_iota(jnp.int32, values.shape, 1)
    other = jnp.where(lane % HD < HD // 2, pltpu.roll(values, 128 - HD // 2, 1), pltpu.roll(values, HD // 2, 1))
    return values * cosine + other * sine


def attention_kernel(
    pages_ref, table_ref, sink_ref, cos_ref, sin_ref, *rest, kv_dev, per_kv, page_size
):
    n_req = len(rest) - 8
    pieces, out_ref = rest[:n_req], rest[n_req]
    q_scr, qt_scr, pool_scr, flat_scr, key_scr, value_scr, bias_scr = rest[n_req + 1 :]
    own = lax.axis_index("req")
    tok = pieces[0].shape[0]
    q_width = kv_dev * per_kv * HD
    head_width = kv_dev * HD
    page_limit = table_ref.shape[1]
    cached = page_limit * page_size
    fresh = tok * n_req
    total = cached + fresh
    pool_rows = pool_scr.shape[1]
    live = pages_ref[0] * page_size
    pairs = per_kv // 2
    for place, k in enumerate(ORDER):
        shard = jnp.bitwise_xor(own, k)
        row = pl.multiple_of(shard * tok, tok)
        cosine = cos_ref[pl.ds(row, tok), :]
        sine = sin_ref[pl.ds(row, tok), :]
        for p in range(kv_dev * pairs):
            col = p * 2 * HD
            turned = turn(pieces[k][:, col : col + 2 * HD].astype(F32), cosine, sine).astype(BF16)
            q_scr[p, place // 2, place % 2 * tok : (place % 2 + 1) * tok, :] = turned.astype(F32) * (1.0 / math.sqrt(HD))
        at = q_width
        key_row = pl.multiple_of(cached + row, tok)
        flat_scr[pl.ds(key_row, tok), :head_width] = turn(
            pieces[k][:, at : at + head_width].astype(F32), cosine, sine
        )
        flat_scr[pl.ds(key_row, tok), head_width:] = pieces[k][
            :, at + head_width : at + 2 * head_width
        ].astype(F32)
        at += 2 * head_width
        for i in range(pool_rows // tok):
            pool_scr[shard, i * tok : (i + 1) * tok, :] = pieces[k][:, at : at + 2 * head_width].astype(F32)
            at += 2 * head_width
        key = lax.broadcasted_iota(jnp.int32, (total, tok), 0)
        query = lax.broadcasted_iota(jnp.int32, (total, tok), 1) + (cached + shard * tok)
        last = jnp.where(key < cached, live - 1, query)
        bias_scr[:, place * tok : (place + 1) * tok] = jnp.where(key > last, NEGATIVE, 0.0)
    for p in range(kv_dev * pairs):
        for h in range(2):
            at = (p % pairs * 2 + h) * 2 * tok
            qt_scr[p // pairs, :, at : at + 2 * tok] = q_scr[p, h].T.astype(BF16)
    per_dev = pool_rows // page_size
    for j in range(page_limit):
        slot = table_ref[0, j]
        source = pl.multiple_of((slot % per_dev) * page_size, page_size)
        flat_scr[j * page_size : (j + 1) * page_size, :] = pool_scr[
            slot // per_dev, pl.ds(source, page_size), :
        ]
    flat = flat_scr[:, :head_width]
    rolled = pltpu.roll(flat, HD, 1)
    low = lax.broadcasted_iota(jnp.int32, flat.shape, 1) < HD
    zero = jnp.zeros_like(flat)
    key_scr[0] = jnp.where(low, flat, zero).astype(BF16)
    key_scr[1] = jnp.where(low, zero, rolled).astype(BF16)
    key_scr[2] = jnp.where(low, rolled, zero).astype(BF16)
    key_scr[3] = jnp.where(low, zero, flat).astype(BF16)
    value_scr[...] = flat_scr[:, head_width:].T.astype(BF16)

    def one_set(i, carry):
        g, a = i // 2, i % 2
        wide = n_req * tok
        scores = jnp.dot(key_scr[i], qt_scr[g], preferred_element_type=F32)
        weights, dens = [], []
        for p in range(pairs):
            part = scores[:, p * wide : (p + 1) * wide] + bias_scr[...]
            sink = sink_ref[own * (kv_dev * per_kv) + g * per_kv + 2 * p + a]
            top = jnp.maximum(jnp.max(part, axis=0, keepdims=True), sink)
            expo = jnp.exp(part - top)
            dens.append(jnp.sum(expo, axis=0, keepdims=True) + jnp.exp(sink - top))
            weights.append(expo.astype(BF16))
        values = value_scr[pl.ds(pl.multiple_of(g * HD, HD), HD), :]
        summed = jnp.dot(values, jnp.concatenate(weights, axis=1), preferred_element_type=F32)
        for p in range(pairs):
            row = pl.multiple_of((g * per_kv + 2 * p + a) * HD, HD)
            out_ref[pl.ds(row, HD), :] = (summed[:, p * wide : (p + 1) * wide] / dens[p]).astype(BF16)
        return carry

    lax.fori_loop(0, 2 * kv_dev, one_set, 0, unroll=True)


def attention(pages, table, sinks, cosine, sine, pieces, kv_dev, per_kv, pool_rows, page_size):
    n_req = len(pieces)
    tok = pieces[0].shape[0]
    total = table.shape[1] * page_size + n_req * tok
    head_width = kv_dev * HD
    return pl.pallas_call(
        functools.partial(attention_kernel, kv_dev=kv_dev, per_kv=per_kv, page_size=page_size),
        out_shape=jax.ShapeDtypeStruct((per_kv * head_width, n_req * tok), BF16),
        in_specs=[smem()] * 3 + [vmem()] * (2 + n_req),
        out_specs=vmem(),
        scratch_shapes=[
            pltpu.VMEM((kv_dev * per_kv // 2, 2, 2 * tok, 2 * HD), F32),
            pltpu.VMEM((kv_dev, 2 * HD, per_kv // 2 * n_req * tok), BF16),
            pltpu.VMEM((n_req, pool_rows, 2 * head_width), F32),
            pltpu.VMEM((total, 2 * head_width), F32),
            pltpu.VMEM((2 * kv_dev, total, head_width), BF16),
            pltpu.VMEM((head_width, total), BF16),
            pltpu.VMEM((total, n_req * tok), F32),
        ],
        compiler_params=params(),
        cost_estimate=FREE,
        name="attention",
    )(pages, table, sinks, cosine, sine, *pieces)


def pool_kernel(slots_ref, cos_ref, sin_ref, pool_ref, *rest, page_size):
    pairs, out_ref, fresh_scr = rest[:-2], rest[-2], rest[-1]
    own = lax.axis_index("req")
    tok = pairs[0].shape[0] // 2
    kv_width = pairs[0].shape[1] // 2
    for k in range(2 * len(pairs)):
        piece = pairs[k // 2][k % 2 * tok : (k % 2 + 1) * tok, :]
        row = pl.multiple_of(jnp.bitwise_xor(own, k) * tok, tok)
        cosine = cos_ref[pl.ds(row, tok), :]
        sine = sin_ref[pl.ds(row, tok), :]
        for col in range(0, kv_width, 128):
            turned = turn(piece[:, col : col + 128].astype(F32), cosine, sine).astype(BF16)
            fresh_scr[pl.ds(row, tok), col : col + 128] = turned
        fresh_scr[pl.ds(row, tok), kv_width:] = piece[:, kv_width:]
    out_ref[...] = pool_ref[...]
    slots_dev = out_ref.shape[0]
    for n in range(slots_ref.shape[1]):
        slot = slots_ref[0, n]

        @pl.when(slot // slots_dev == own)
        def _(slot=slot, n=n):
            out_ref[slot % slots_dev] = fresh_scr[n * page_size : (n + 1) * page_size, :]


def write_pool(slots, cosine, sine, pool, pairs):
    rows, width = pairs[0].shape
    return pl.pallas_call(
        functools.partial(pool_kernel, page_size=pool.shape[1]),
        out_shape=jax.ShapeDtypeStruct(pool.shape, BF16),
        in_specs=[smem()] + [vmem()] * (3 + len(pairs)),
        out_specs=vmem(),
        scratch_shapes=[pltpu.VMEM((rows * len(pairs), width), BF16)],
        compiler_params=params(),
        cost_estimate=FREE,
        name="write_pool",
    )(slots, cosine, sine, pool, *pairs)


def project_kernel(ctx_ref, *refs, counts, pairs, tokens):
    weights = refs[:-2]
    send_ref, keep_ref = refs[-2:]
    half = tokens // 2
    for b in range(len(counts)):
        used = [(n, i) for n, (i, block) in enumerate(pairs) if block == b]
        low, high = min(i for _, i in used), max(i for _, i in used) + 1
        at = sum(counts[:b])
        row = 0
        for piece in weights[at : at + counts[b]]:
            rows = slice(row, row + piece.shape[0])
            terms = jnp.dot(
                piece[...], ctx_ref[:, low * tokens : high * tokens], preferred_element_type=F32
            ).astype(BF16)
            for n, i in used:
                start = (i - low) * tokens
                keep_ref[n, rows, :] = terms[:, start : start + half]
                send_ref[n, rows, :] = terms[:, start + half : start + tokens]
            row += piece.shape[0]


def project(contexts, blocks, pairs):
    tokens = contexts[0].shape[1]
    side_by_side = contexts[0] if len(contexts) == 1 else jnp.concatenate(contexts, axis=1)
    cols = sum(piece.shape[0] for piece in blocks[0])
    shape = jax.ShapeDtypeStruct((len(pairs), cols, tokens // 2), BF16)
    flat = [piece for block in blocks for piece in block]
    counts = tuple(len(block) for block in blocks)
    return pl.pallas_call(
        functools.partial(project_kernel, counts=counts, pairs=pairs, tokens=tokens),
        out_shape=[shape, shape],
        in_specs=[vmem()] * (1 + len(flat)),
        out_specs=[vmem()] * 2,
        compiler_params=params(),
        cost_estimate=FREE,
        name="project",
    )(side_by_side, *flat)


def fold_rows(cols):
    return -(-cols // 32) * 16


def pair_kernel(keep_ref, got_ref, *out_refs, counts):
    cols, width = keep_ref.shape[1:]
    rows = out_refs[0].shape[1]
    tok = width // 2
    low = lax.broadcasted_iota(jnp.int32, (rows, width), 1) < tok
    at = 0
    for i, count in enumerate(counts):
        for b in range(count):
            both = keep_ref[at].astype(F32) + got_ref[at].astype(F32)
            top = both[:rows]
            rest = jnp.concatenate([both[rows:], jnp.zeros((2 * rows - cols, width), F32)], axis=0)
            out_refs[2 * i][b] = jnp.where(low, top, pltpu.roll(rest, tok, 1)).astype(out_refs[2 * i].dtype)
            out_refs[2 * i + 1][b] = jnp.where(low, pltpu.roll(top, tok, 1), rest).astype(BF16)
            at += 1


def pair_sum(keep, got, counts, own_first):
    cols, width = keep.shape[1:]
    shapes = [jax.ShapeDtypeStruct((c, fold_rows(cols), width), BF16) for c in counts for _ in range(2)]
    if own_first:
        shapes[0] = jax.ShapeDtypeStruct(shapes[0].shape, F32)
    return pl.pallas_call(
        functools.partial(pair_kernel, counts=counts),
        out_shape=shapes,
        in_specs=[vmem()] * 2,
        out_specs=[vmem()] * len(shapes),
        compiler_params=params(),
        cost_estimate=FREE,
        name="pair_sum",
    )(keep, got)


def final_kernel(hidden_ref, *rest, places):
    parts, out_ref, scr = rest[:-2], rest[-2], rest[-1]
    own = lax.axis_index("exp")
    inner = is_inner(own)
    tok, width = hidden_ref.shape
    rows = parts[0].shape[1]
    cols = width // lax.axis_size("exp")
    for (first, second), bits in zip(zip(parts[0::2], parts[1::2]), places):
        for b, (inner_bits, outer_bits) in enumerate(bits):
            bit = jnp.where(inner, inner_bits, outer_bits)
            both = first[b].astype(F32) + second[b].astype(F32)
            row = pl.multiple_of(jnp.bitwise_xor(own, bit) * cols, 8)
            scr[pl.ds(row, rows), :] = both
            scr[pl.ds(row + rows, cols - rows), :] = pltpu.roll(both, tok, 1)[: cols - rows]
    attn = scr[...].T[:tok]
    out_ref[...] = (hidden_ref[...].astype(F32) + attn).astype(BF16)


def finish(hidden, parts, places):
    return pl.pallas_call(
        functools.partial(final_kernel, places=places),
        out_shape=jax.ShapeDtypeStruct(hidden.shape, BF16),
        in_specs=[vmem()] * (1 + len(parts)),
        out_specs=vmem(),
        scratch_shapes=[pltpu.VMEM((hidden.shape[1], parts[0].shape[2]), F32)],
        compiler_params=params(),
        cost_estimate=FREE,
        name="finish",
    )(hidden, *parts)


def paired_plan(
    hidden_in, queries, new_kv, kv_pool, page_table, new_slots, cached_pages, sinks, out_weight
):
    tok = hidden_in.shape[1]
    n_req = lax.axis_size("req")
    head_count = sinks.shape[0]
    kv_width = new_kv.shape[2] // 2
    kv_heads = kv_width // HD
    slots_dev, page_size = kv_pool.shape[1:3]
    pool_rows = slots_dev * page_size
    weight = out_weight.T
    cols = weight.shape[0]
    cut = cols // 32 * 16
    cuts = (slice(0, cut), slice(cut, cols))
    first = swap_blocks(weight, NEAR_BIT, FAR_BIT)

    pieces = pack(queries[0], new_kv[0], kv_pool[0].reshape(pool_rows, 2 * kv_width), n_req)
    pieces = [pieces[0]] + [swap(pieces[k], k, 0) for k in range(1, n_req)]
    second = [swap_blocks(weight[cuts[0]], FAR_BIT, NEAR_BIT)]
    second += [swap_blocks(weight[cuts[1]], FAR_BIT, NEAR_BIT)]

    position = cached_pages[0] * page_size + jnp.arange(n_req * tok)
    frequency = THETA ** (-2.0 * jnp.arange(HD // 2).astype(F32) / HD)
    angles = position.astype(F32)[:, None] * frequency[None, :]
    cosine, sine = jnp.cos(angles), jnp.sin(angles)
    cosine = jnp.concatenate([cosine] * 4, axis=1)
    sine = jnp.concatenate([-sine, sine, -sine, sine], axis=1)

    ctx = attention(
        cached_pages, page_table, sinks, cosine, sine, pieces, kv_heads // n_req,
        head_count // kv_heads, pool_rows, page_size,
    )
    chip_rows = jnp.concatenate([new_kv[0], pieces[1][:, -2 * kv_width :]], axis=0)
    ctx, first, chip_rows = lax.optimization_barrier((ctx, first, chip_rows))
    ctx_mate = swap(ctx, 0, PAIR_BIT)
    inner = is_inner(lax.axis_index("exp"))
    far = [jnp.where(inner, piece, first[rows]) for rows, piece in zip(cuts, second)]
    both = [swap(chunk, 0, NEAR_BIT) for chunk in far]
    fresh = swap(chip_rows, 2, 0)

    def both_sides(contexts, blocks, pairs, own_first):
        send, keep = project(contexts, blocks, pairs)
        counts = tuple(n for n in (sum(i == c for c, _ in pairs) for i in range(len(contexts))) if n)
        return pair_sum(keep, swap(send, 1, 0), counts, own_first)

    parts = []
    ctx, fresh = lax.optimization_barrier((ctx, fresh))
    own_part, over_y = both_sides([ctx], [[weight], [first]], ((0, 0), (0, 1)), True)
    parts += [own_part, swap(over_y, 2, 0)]
    pool_out = write_pool(new_slots, cosine, sine, kv_pool[0], [chip_rows, fresh])
    ctx_mate, pool_out = lax.optimization_barrier((ctx_mate, pool_out))
    ctx_mate, parts[1] = lax.optimization_barrier((ctx_mate, parts[1]))
    over_pair, over_both = both_sides([ctx_mate], [[weight], [first], second], ((0, 0), (0, 1), (0, 2)), False)
    parts += [swap(over_pair, 0, PAIR_BIT), swap(over_both, 2, PAIR_BIT)]
    own_part, over_y, over_pair, over_both = both_sides([ctx, ctx_mate], [second, both], ((0, 0), (0, 1), (1, 1)), True)
    parts += [own_part, swap(over_y, 2, 0)]
    parts += [swap(over_pair, 0, PAIR_BIT), swap(over_both, 2, PAIR_BIT)]
    own_bits, first_bits, second_bits, both_bits = (
        (0, 0), (NEAR_BIT, FAR_BIT), (FAR_BIT, NEAR_BIT), (FAR_BIT ^ NEAR_BIT,) * 2
    )

    def of_mate(bits):
        return PAIR_BIT ^ bits[1], PAIR_BIT ^ bits[0]

    places = (
        (own_bits, first_bits),
        (of_mate(own_bits), of_mate(first_bits), of_mate(second_bits)),
        (second_bits, both_bits),
        (of_mate(both_bits),),
    )
    layer_out = finish(hidden_in[0], parts, places)
    return (layer_out[None], pool_out[None])


def solution(mesh):
    paired = mesh.shape["req"] == 4 and mesh.shape["exp"] == 8
    return jax.shard_map(
        paired_plan if paired else general_plan,
        mesh=mesh,
        in_specs=(
            P("exp", "req", None),
            P("exp", "req", None),
            P("exp", "req", None),
            P("exp", "req", None, None),
            P("exp", None),
            P("exp", None),
            P("exp"),
            P(),
            P("req", "exp"),
        ),
        out_specs=(P("exp", "req", None), P("exp", "req", None, None)),
        check_vma=False,
    )
```

```python
import functools
import math

import jax
import jax.numpy as jnp
from jax import lax
from jax.experimental import pallas as pl
from jax.experimental.pallas import tpu as pltpu
from jax.sharding import PartitionSpec as P

HD = 64


THETA = 150000.0
NEGATIVE = -1e30


def rotate(values, positions):
    half_width = values.shape[-1] // 2
    frequency = THETA ** (-2.0 * jnp.arange(half_width).astype(jnp.float32) / values.shape[-1])
    angles = positions.astype(jnp.float32)[:, None] * frequency[None, :]
    cosine = jnp.cos(angles)[:, None, :]
    sine_part = jnp.sin(angles)[:, None, :]
    lower_half = values[..., :half_width]
    upper_half = values[..., half_width:]
    return jnp.concatenate(
        [
            lower_half * cosine - upper_half * sine_part,
            upper_half * cosine + lower_half * sine_part,
        ],
        axis=-1,
    )


def spread_heads(rows, head_total, kv_heads, dev_count):
    per_dev = head_total // dev_count
    per_kv = head_total // kv_heads
    repeat = max(1, per_kv // per_dev)
    kv_dev = max(1, per_dev // per_kv)
    count = rows.shape[0]
    split = jnp.repeat(rows.reshape(count, 2, kv_heads, HD), repeat, axis=2)
    split = split.reshape(count, 2, dev_count, kv_dev * HD)
    return jnp.transpose(split, (0, 2, 1, 3)).reshape(count, dev_count, 2 * kv_dev * HD)


def general_plan(
    hidden_in, queries, new_kv, kv_pool, page_table, new_slots, cached_pages, sinks, out_weight
):
    tok_dev = hidden_in.shape[1]
    n_req = lax.axis_size("req")
    own_index = lax.axis_index("req")
    fresh_count = tok_dev * n_req
    head_count = sinks.shape[0]
    kv_width = new_kv.shape[2] // 2
    kv_heads = kv_width // HD
    per_kv = head_count // kv_heads
    heads_dev = head_count // n_req
    kv_dev = max(1, heads_dev // per_kv)
    per_dev_group = heads_dev // kv_dev
    head_width = 2 * kv_dev * HD
    slots_dev = kv_pool.shape[1]
    page_size = kv_pool.shape[2]
    slot_total = slots_dev * n_req
    page_limit = page_table.shape[1]
    fresh_pages = new_slots.shape[1]
    page_count = cached_pages[0]
    start_pos = page_count * page_size
    own_pos = start_pos + own_index * tok_dev + jnp.arange(tok_dev)
    q_rot = rotate(queries[0].reshape(tok_dev, head_count, HD).astype(jnp.float32), own_pos).astype(
        jnp.bfloat16
    )
    k_rot = rotate(
        new_kv[0, :, :kv_width].reshape(tok_dev, kv_heads, HD).astype(jnp.float32), own_pos
    ).astype(jnp.bfloat16)
    kv_rot = jnp.concatenate([k_rot.reshape(tok_dev, kv_width), new_kv[0, :, kv_width:]], axis=1)
    slot_all = jnp.arange(slot_total)
    page_index = jnp.arange(page_limit)
    cached_hit = (page_table[0][None, :] == slot_all[:, None]) & (page_index[None, :] < page_count)
    is_cached = jnp.any(cached_hit, axis=1)
    cached_base = jnp.sum(jnp.where(cached_hit, page_index[None, :], 0), axis=1) * page_size
    fresh_hit = new_slots[0][None, :] == slot_all[:, None]
    is_fresh = jnp.any(fresh_hit, axis=1)
    fresh_base = (
        start_pos
        + jnp.sum(jnp.where(fresh_hit, jnp.arange(fresh_pages)[None, :], 0), axis=1) * page_size
    )
    key_pos = (
        jnp.where(is_fresh, fresh_base, cached_base)[:, None] + jnp.arange(page_size)[None, :]
    ).reshape(-1)
    key_live = jnp.repeat(is_cached | is_fresh, page_size)
    all_fresh = lax.all_gather(kv_rot, "req", axis=0, tiled=True)
    own_hit = lax.dynamic_slice_in_dim(fresh_hit, own_index * slots_dev, slots_dev, 0)
    own_fresh = lax.dynamic_slice_in_dim(is_fresh, own_index * slots_dev, slots_dev, 0)
    appended = jnp.dot(
        own_hit.astype(jnp.bfloat16),
        all_fresh.reshape(fresh_pages, page_size * 2 * kv_width),
        preferred_element_type=jnp.float32,
    )
    appended = appended.astype(jnp.bfloat16).reshape(slots_dev, page_size, 2 * kv_width)
    local_pages = jnp.where(own_fresh[:, None, None], appended, kv_pool[0])
    head_pool = lax.all_to_all(
        spread_heads(
            local_pages.reshape(slots_dev * page_size, 2 * kv_width), head_count, kv_heads, n_req
        ),
        "req",
        split_axis=1,
        concat_axis=0,
        tiled=True,
    )
    head_pool = head_pool.reshape(slot_total * page_size, head_width)
    q_here = lax.all_to_all(
        q_rot.reshape(tok_dev, n_req, heads_dev * HD),
        "req",
        split_axis=1,
        concat_axis=0,
        tiled=True,
    )
    q_here = q_here.reshape(fresh_count, heads_dev * HD)
    key_total = slot_total * page_size
    all_keys = head_pool[:, : kv_dev * HD].reshape(key_total, kv_dev, HD)
    all_values = head_pool[:, kv_dev * HD :].reshape(key_total, kv_dev, HD)
    sink_mine = lax.dynamic_slice_in_dim(sinks, own_index * heads_dev, heads_dev, 0).reshape(
        kv_dev, per_dev_group
    )
    scale = 1.0 / math.sqrt(HD)
    query_block = math.gcd(fresh_count, 128)
    contexts = []
    for block_start in range(0, fresh_count, query_block):
        block_queries = q_here[block_start : block_start + query_block].reshape(
            query_block, kv_dev, per_dev_group, HD
        )
        query_pos = start_pos + block_start + jnp.arange(query_block)
        visible = key_live[None, :] & (key_pos[None, :] <= query_pos[:, None])
        scores = (
            jnp.einsum(
                "tghd,kgd->tghk", block_queries, all_keys, preferred_element_type=jnp.float32
            )
            * scale
        )
        scores = jnp.where(visible[:, None, None, :], scores, NEGATIVE)
        top_score = jnp.maximum(jnp.max(scores, axis=-1), sink_mine[None])
        expo = jnp.where(visible[:, None, None, :], jnp.exp(scores - top_score[..., None]), 0.0)
        denominator = jnp.sum(expo, axis=-1) + jnp.exp(sink_mine[None] - top_score)
        weighted = jnp.einsum(
            "tghk,kgd->tghd",
            expo.astype(jnp.bfloat16),
            all_values,
            preferred_element_type=jnp.float32,
        )
        contexts.append(
            (weighted / denominator[..., None])
            .astype(jnp.bfloat16)
            .reshape(query_block, heads_dev * HD)
        )
    context = jnp.concatenate(contexts, axis=0)
    terms = jnp.dot(
        context,
        lax.all_gather(out_weight, "exp", axis=1, tiled=True),
        preferred_element_type=jnp.float32,
    ).astype(jnp.bfloat16)
    width = terms.shape[1]
    arrived = lax.all_to_all(
        terms.reshape(n_req, tok_dev, width), "req", split_axis=0, concat_axis=0, tiled=True
    )
    attn = jnp.sum(arrived.astype(jnp.float32), axis=0)
    layer_out = (hidden_in[0].astype(jnp.float32) + attn).astype(jnp.bfloat16)
    return (layer_out[None], local_pages[None])


VMEM_LIMIT = 24 * 1024 * 1024
FREE = pl.CostEstimate(flops=0, bytes_accessed=0, transcendentals=0)
F32 = jnp.float32
BF16 = jnp.bfloat16

PAIR_BIT, NEAR_BIT, FAR_BIT = 2, 1, 6
ORDER = (0, 2, 1, 3)


def vmem():
    return pl.BlockSpec(memory_space=pltpu.VMEM)


def smem():
    return pl.BlockSpec(memory_space=pltpu.SMEM)


def params():
    return pltpu.CompilerParams(vmem_limit_bytes=VMEM_LIMIT)


def swap(values, req_bits, exp_bits):
    if not exp_bits:
        return lax.ppermute(values, "req", [(i, i ^ req_bits) for i in range(lax.axis_size("req"))])
    if not req_bits:
        return lax.ppermute(values, "exp", [(i, i ^ exp_bits) for i in range(lax.axis_size("exp"))])
    rows, cols = lax.axis_size("req"), lax.axis_size("exp")
    pairs = [
        (i * cols + j, (i ^ req_bits) * cols + (j ^ exp_bits)) for i in range(rows) for j in range(cols)
    ]
    return lax.ppermute(values, ("req", "exp"), pairs)


def is_inner(index):
    return (index & 2) * 2 != (index & 4)


def swap_blocks(values, inner_bits, outer_bits):
    pairs = [(i, i ^ (inner_bits if is_inner(i) else outer_bits)) for i in range(lax.axis_size("exp"))]
    return lax.ppermute(values, "exp", pairs)


def pack_kernel(q_ref, kv_ref, pool_ref, *rest):
    outs, sems = rest[:-1], rest[-1]
    n_req = len(outs)
    own = lax.axis_index("req")
    tok = q_ref.shape[0]
    q_width = q_ref.shape[1] // n_req
    kv_width = kv_ref.shape[1] // 2
    head_width = kv_width // n_req
    copies = []

    def copy(source, target):
        copies.append(pltpu.make_async_copy(source, target, sems.at[len(copies)]))
        copies[-1].start()

    for k in (3, 2, 1, 0):
        out = outs[k]
        dest = jnp.bitwise_xor(own, k)
        col = pl.multiple_of(dest * q_width, 128)
        copy(q_ref.at[:, pl.ds(col, q_width)], out.at[:, pl.ds(0, q_width)])
        at = q_width
        blocks = [(kv_ref, 0)]
        blocks += [(pool_ref, i * tok) for i in range(pool_ref.shape[0] // tok)]
        for block, row in blocks:
            for half in range(2):
                col = pl.multiple_of(half * kv_width + dest * head_width, 128)
                copy(
                    block.at[pl.ds(row, tok), pl.ds(col, head_width)],
                    out.at[:, pl.ds(at, head_width)],
                )
                at += head_width
        if k == 1:
            copy(kv_ref, out.at[:, pl.ds(at, 2 * kv_width)])
    for one in copies:
        one.wait()


def pack(q, kv, pool, n_req):
    tok = q.shape[0]
    blocks = 1 + pool.shape[0] // tok
    width = (q.shape[1] + blocks * kv.shape[1]) // n_req
    widths = [width + (kv.shape[1] if k == 1 else 0) for k in range(n_req)]
    return pl.pallas_call(
        pack_kernel,
        out_shape=[jax.ShapeDtypeStruct((tok, w), BF16) for w in widths],
        in_specs=[pl.BlockSpec(memory_space=pltpu.MemorySpace.HBM)] * 3,
        out_specs=[vmem()] * n_req,
        scratch_shapes=[pltpu.SemaphoreType.DMA((n_req * (1 + 2 * blocks) + 1,))],
        compiler_params=params(),
        cost_estimate=FREE,
        name="pack",
    )(q, kv, pool)


def turn(values, cosine, sine):
    lane = lax.broadcasted_iota(jnp.int32, values.shape, 1)
    other = jnp.where(lane % HD < HD // 2, pltpu.roll(values, 128 - HD // 2, 1), pltpu.roll(values, HD // 2, 1))
    return values * cosine + other * sine


def attention_kernel(
    pages_ref, table_ref, sink_ref, cos_ref, sin_ref, *rest, kv_dev, per_kv, page_size
):
    n_req = len(rest) - 8
    pieces, out_ref = rest[:n_req], rest[n_req]
    q_scr, qt_scr, pool_scr, flat_scr, key_scr, value_scr, bias_scr = rest[n_req + 1 :]
    own = lax.axis_index("req")
    tok = pieces[0].shape[0]
    q_width = kv_dev * per_kv * HD
    head_width = kv_dev * HD
    page_limit = table_ref.shape[1]
    cached = page_limit * page_size
    fresh = tok * n_req
    total = cached + fresh
    pool_rows = pool_scr.shape[1]
    live = pages_ref[0] * page_size
    pairs = per_kv // 2
    for place, k in enumerate(ORDER):
        shard = jnp.bitwise_xor(own, k)
        row = pl.multiple_of(shard * tok, tok)
        cosine = cos_ref[pl.ds(row, tok), :]
        sine = sin_ref[pl.ds(row, tok), :]
        for p in range(kv_dev * pairs):
            col = p * 2 * HD
            turned = turn(pieces[k][:, col : col + 2 * HD].astype(F32), cosine, sine).astype(BF16)
            q_scr[p, place // 2, place % 2 * tok : (place % 2 + 1) * tok, :] = turned.astype(F32) * (1.0 / math.sqrt(HD))
        at = q_width
        key_row = pl.multiple_of(cached + row, tok)
        flat_scr[pl.ds(key_row, tok), :head_width] = turn(
            pieces[k][:, at : at + head_width].astype(F32), cosine, sine
        )
        flat_scr[pl.ds(key_row, tok), head_width:] = pieces[k][
            :, at + head_width : at + 2 * head_width
        ].astype(F32)
        at += 2 * head_width
        for i in range(pool_rows // tok):
            pool_scr[shard, i * tok : (i + 1) * tok, :] = pieces[k][:, at : at + 2 * head_width].astype(F32)
            at += 2 * head_width
        key = lax.broadcasted_iota(jnp.int32, (total, tok), 0)
        query = lax.broadcasted_iota(jnp.int32, (total, tok), 1) + (cached + shard * tok)
        last = jnp.where(key < cached, live - 1, query)
        bias_scr[:, place * tok : (place + 1) * tok] = jnp.where(key > last, NEGATIVE, 0.0)
    for p in range(kv_dev * pairs):
        for h in range(2):
            at = (p % pairs * 2 + h) * 2 * tok
            qt_scr[p // pairs, :, at : at + 2 * tok] = q_scr[p, h].T.astype(BF16)
    per_dev = pool_rows // page_size
    for j in range(page_limit):
        slot = table_ref[0, j]
        source = pl.multiple_of((slot % per_dev) * page_size, page_size)
        flat_scr[j * page_size : (j + 1) * page_size, :] = pool_scr[
            slot // per_dev, pl.ds(source, page_size), :
        ]
    flat = flat_scr[:, :head_width]
    rolled = pltpu.roll(flat, HD, 1)
    low = lax.broadcasted_iota(jnp.int32, flat.shape, 1) < HD
    zero = jnp.zeros_like(flat)
    key_scr[0] = jnp.where(low, flat, zero).astype(BF16)
    key_scr[1] = jnp.where(low, zero, rolled).astype(BF16)
    key_scr[2] = jnp.where(low, rolled, zero).astype(BF16)
    key_scr[3] = jnp.where(low, zero, flat).astype(BF16)
    value_scr[...] = flat_scr[:, head_width:].T.astype(BF16)

    def one_set(i, carry):
        g, a = i // 2, i % 2
        wide = n_req * tok
        scores = jnp.dot(key_scr[i], qt_scr[g], preferred_element_type=F32)
        weights, dens = [], []
        for p in range(pairs):
            part = scores[:, p * wide : (p + 1) * wide] + bias_scr[...]
            sink = sink_ref[own * (kv_dev * per_kv) + g * per_kv + 2 * p + a]
            top = jnp.maximum(jnp.max(part, axis=0, keepdims=True), sink)
            expo = jnp.exp(part - top)
            dens.append(jnp.sum(expo, axis=0, keepdims=True) + jnp.exp(sink - top))
            weights.append(expo.astype(BF16))
        values = value_scr[pl.ds(pl.multiple_of(g * HD, HD), HD), :]
        summed = jnp.dot(values, jnp.concatenate(weights, axis=1), preferred_element_type=F32)
        for p in range(pairs):
            row = pl.multiple_of((g * per_kv + 2 * p + a) * HD, HD)
            out_ref[pl.ds(row, HD), :] = (summed[:, p * wide : (p + 1) * wide] / dens[p]).astype(BF16)
        return carry

    lax.fori_loop(0, 2 * kv_dev, one_set, 0, unroll=True)


def attention(pages, table, sinks, cosine, sine, pieces, kv_dev, per_kv, pool_rows, page_size):
    n_req = len(pieces)
    tok = pieces[0].shape[0]
    total = table.shape[1] * page_size + n_req * tok
    head_width = kv_dev * HD
    return pl.pallas_call(
        functools.partial(attention_kernel, kv_dev=kv_dev, per_kv=per_kv, page_size=page_size),
        out_shape=jax.ShapeDtypeStruct((per_kv * head_width, n_req * tok), BF16),
        in_specs=[smem()] * 3 + [vmem()] * (2 + n_req),
        out_specs=vmem(),
        scratch_shapes=[
            pltpu.VMEM((kv_dev * per_kv // 2, 2, 2 * tok, 2 * HD), F32),
            pltpu.VMEM((kv_dev, 2 * HD, per_kv // 2 * n_req * tok), BF16),
            pltpu.VMEM((n_req, pool_rows, 2 * head_width), F32),
            pltpu.VMEM((total, 2 * head_width), F32),
            pltpu.VMEM((2 * kv_dev, total, head_width), BF16),
            pltpu.VMEM((head_width, total), BF16),
            pltpu.VMEM((total, n_req * tok), F32),
        ],
        compiler_params=params(),
        cost_estimate=FREE,
        name="attention",
    )(pages, table, sinks, cosine, sine, *pieces)


def pool_kernel(slots_ref, cos_ref, sin_ref, pool_ref, *rest, page_size):
    pairs, out_ref, fresh_scr = rest[:-2], rest[-2], rest[-1]
    own = lax.axis_index("req")
    tok = pairs[0].shape[0] // 2
    kv_width = pairs[0].shape[1] // 2
    for k in range(2 * len(pairs)):
        piece = pairs[k // 2][k % 2 * tok : (k % 2 + 1) * tok, :]
        row = pl.multiple_of(jnp.bitwise_xor(own, k) * tok, tok)
        cosine = cos_ref[pl.ds(row, tok), :]
        sine = sin_ref[pl.ds(row, tok), :]
        for col in range(0, kv_width, 128):
            turned = turn(piece[:, col : col + 128].astype(F32), cosine, sine).astype(BF16)
            fresh_scr[pl.ds(row, tok), col : col + 128] = turned
        fresh_scr[pl.ds(row, tok), kv_width:] = piece[:, kv_width:]
    out_ref[...] = pool_ref[...]
    slots_dev = out_ref.shape[0]
    for n in range(slots_ref.shape[1]):
        slot = slots_ref[0, n]

        @pl.when(slot // slots_dev == own)
        def _(slot=slot, n=n):
            out_ref[slot % slots_dev] = fresh_scr[n * page_size : (n + 1) * page_size, :]


def write_pool(slots, cosine, sine, pool, pairs):
    rows, width = pairs[0].shape
    return pl.pallas_call(
        functools.partial(pool_kernel, page_size=pool.shape[1]),
        out_shape=jax.ShapeDtypeStruct(pool.shape, BF16),
        in_specs=[smem()] + [vmem()] * (3 + len(pairs)),
        out_specs=vmem(),
        scratch_shapes=[pltpu.VMEM((rows * len(pairs), width), BF16)],
        compiler_params=params(),
        cost_estimate=FREE,
        name="write_pool",
    )(slots, cosine, sine, pool, *pairs)


def project_kernel(*refs, n_ctx, counts, pairs):
    contexts = refs[:n_ctx]
    weights = refs[n_ctx:-2]
    send_ref, keep_ref = refs[-2:]
    half = contexts[0].shape[1] // 2
    for n, (i, b) in enumerate(pairs):
        at = sum(counts[:b])
        row = 0
        for piece in weights[at : at + counts[b]]:
            rows = slice(row, row + piece.shape[0])
            terms = jnp.dot(piece[...], contexts[i][...], preferred_element_type=F32).astype(BF16)
            keep_ref[n, rows, :] = terms[:, :half]
            send_ref[n, rows, :] = terms[:, half:]
            row += piece.shape[0]


def project(contexts, blocks, pairs):
    tokens = contexts[0].shape[1]
    cols = sum(piece.shape[0] for piece in blocks[0])
    shape = jax.ShapeDtypeStruct((len(pairs), cols, tokens // 2), BF16)
    flat = [piece for block in blocks for piece in block]
    counts = tuple(len(block) for block in blocks)
    return pl.pallas_call(
        functools.partial(project_kernel, n_ctx=len(contexts), counts=counts, pairs=pairs),
        out_shape=[shape, shape],
        in_specs=[vmem()] * (len(contexts) + len(flat)),
        out_specs=[vmem()] * 2,
        compiler_params=params(),
        cost_estimate=FREE,
        name="project",
    )(*contexts, *flat)


def fold_rows(cols):
    return -(-cols // 32) * 16


def pair_kernel(keep_ref, got_ref, *out_refs, counts):
    cols, width = keep_ref.shape[1:]
    rows = out_refs[0].shape[1]
    tok = width // 2
    low = lax.broadcasted_iota(jnp.int32, (rows, width), 1) < tok
    at = 0
    for i, count in enumerate(counts):
        for b in range(count):
            both = keep_ref[at].astype(F32) + got_ref[at].astype(F32)
            top = both[:rows]
            rest = jnp.concatenate([both[rows:], jnp.zeros((2 * rows - cols, width), F32)], axis=0)
            out_refs[2 * i][b] = jnp.where(low, top, pltpu.roll(rest, tok, 1)).astype(out_refs[2 * i].dtype)
            out_refs[2 * i + 1][b] = jnp.where(low, pltpu.roll(top, tok, 1), rest).astype(BF16)
            at += 1


def pair_sum(keep, got, counts, own_first):
    cols, width = keep.shape[1:]
    shapes = [jax.ShapeDtypeStruct((c, fold_rows(cols), width), BF16) for c in counts for _ in range(2)]
    if own_first:
        shapes[0] = jax.ShapeDtypeStruct(shapes[0].shape, F32)
    return pl.pallas_call(
        functools.partial(pair_kernel, counts=counts),
        out_shape=shapes,
        in_specs=[vmem()] * 2,
        out_specs=[vmem()] * len(shapes),
        compiler_params=params(),
        cost_estimate=FREE,
        name="pair_sum",
    )(keep, got)


def final_kernel(hidden_ref, *rest, places):
    parts, out_ref, scr = rest[:-2], rest[-2], rest[-1]
    own = lax.axis_index("exp")
    inner = is_inner(own)
    tok, width = hidden_ref.shape
    rows = parts[0].shape[1]
    cols = width // lax.axis_size("exp")
    for (first, second), bits in zip(zip(parts[0::2], parts[1::2]), places):
        for b, (inner_bits, outer_bits) in enumerate(bits):
            bit = jnp.where(inner, inner_bits, outer_bits)
            both = first[b].astype(F32) + second[b].astype(F32)
            row = pl.multiple_of(jnp.bitwise_xor(own, bit) * cols, 8)
            scr[pl.ds(row, rows), :] = both
            scr[pl.ds(row + rows, cols - rows), :] = pltpu.roll(both, tok, 1)[: cols - rows]
    attn = scr[...].T[:tok]
    out_ref[...] = (hidden_ref[...].astype(F32) + attn).astype(BF16)


def finish(hidden, parts, places):
    return pl.pallas_call(
        functools.partial(final_kernel, places=places),
        out_shape=jax.ShapeDtypeStruct(hidden.shape, BF16),
        in_specs=[vmem()] * (1 + len(parts)),
        out_specs=vmem(),
        scratch_shapes=[pltpu.VMEM((hidden.shape[1], parts[0].shape[2]), F32)],
        compiler_params=params(),
        cost_estimate=FREE,
        name="finish",
    )(hidden, *parts)


def paired_plan(
    hidden_in, queries, new_kv, kv_pool, page_table, new_slots, cached_pages, sinks, out_weight
):
    tok = hidden_in.shape[1]
    n_req = lax.axis_size("req")
    head_count = sinks.shape[0]
    kv_width = new_kv.shape[2] // 2
    kv_heads = kv_width // HD
    slots_dev, page_size = kv_pool.shape[1:3]
    pool_rows = slots_dev * page_size
    weight = out_weight.T
    cols = weight.shape[0]
    cut = cols // 32 * 16
    cuts = (slice(0, cut), slice(cut, cols))
    first = swap_blocks(weight, NEAR_BIT, FAR_BIT)

    pieces = pack(queries[0], new_kv[0], kv_pool[0].reshape(pool_rows, 2 * kv_width), n_req)
    pieces = [pieces[0]] + [swap(pieces[k], k, 0) for k in range(1, n_req)]
    second = [swap_blocks(weight[cuts[0]], FAR_BIT, NEAR_BIT)]
    second += [swap_blocks(weight[cuts[1]], FAR_BIT, NEAR_BIT)]

    position = cached_pages[0] * page_size + jnp.arange(n_req * tok)
    frequency = THETA ** (-2.0 * jnp.arange(HD // 2).astype(F32) / HD)
    angles = position.astype(F32)[:, None] * frequency[None, :]
    cosine, sine = jnp.cos(angles), jnp.sin(angles)
    cosine = jnp.concatenate([cosine] * 4, axis=1)
    sine = jnp.concatenate([-sine, sine, -sine, sine], axis=1)

    ctx = attention(
        cached_pages, page_table, sinks, cosine, sine, pieces, kv_heads // n_req,
        head_count // kv_heads, pool_rows, page_size,
    )
    chip_rows = jnp.concatenate([new_kv[0], pieces[1][:, -2 * kv_width :]], axis=0)
    ctx, first, chip_rows = lax.optimization_barrier((ctx, first, chip_rows))
    ctx_mate = swap(ctx, 0, PAIR_BIT)
    inner = is_inner(lax.axis_index("exp"))
    far = [jnp.where(inner, piece, first[rows]) for rows, piece in zip(cuts, second)]
    both = [swap(chunk, 0, NEAR_BIT) for chunk in far]
    fresh = swap(chip_rows, 2, 0)

    def both_sides(contexts, blocks, pairs, own_first):
        send, keep = project(contexts, blocks, pairs)
        counts = tuple(n for n in (sum(i == c for c, _ in pairs) for i in range(len(contexts))) if n)
        return pair_sum(keep, swap(send, 1, 0), counts, own_first)

    parts = []
    ctx, fresh = lax.optimization_barrier((ctx, fresh))
    own_part, over_y = both_sides([ctx], [[weight], [first]], ((0, 0), (0, 1)), True)
    parts += [own_part, swap(over_y, 2, 0)]
    ctx_mate, parts[1] = lax.optimization_barrier((ctx_mate, parts[1]))
    over_pair, over_both = both_sides([ctx_mate], [[weight], [first], second], ((0, 0), (0, 1), (0, 2)), False)
    parts += [swap(over_pair, 0, PAIR_BIT), swap(over_both, 2, PAIR_BIT)]
    own_part, over_y, over_pair, over_both = both_sides([ctx, ctx_mate], [second, both], ((0, 0), (0, 1), (1, 1)), True)
    own_part, fresh = lax.optimization_barrier((own_part, fresh))
    parts += [own_part, swap(over_y, 2, 0)]
    parts += [swap(over_pair, 0, PAIR_BIT), swap(over_both, 2, PAIR_BIT)]
    own_bits, first_bits, second_bits, both_bits = (
        (0, 0), (NEAR_BIT, FAR_BIT), (FAR_BIT, NEAR_BIT), (FAR_BIT ^ NEAR_BIT,) * 2
    )

    def of_mate(bits):
        return PAIR_BIT ^ bits[1], PAIR_BIT ^ bits[0]

    places = (
        (own_bits, first_bits),
        (of_mate(own_bits), of_mate(first_bits), of_mate(second_bits)),
        (second_bits, both_bits),
        (of_mate(both_bits),),
    )
    pool_out = write_pool(new_slots, cosine, sine, kv_pool[0], [chip_rows, fresh])
    hidden, pool_out = lax.optimization_barrier((hidden_in[0], pool_out))
    layer_out = finish(hidden, parts, places)
    return (layer_out[None], pool_out[None])


def solution(mesh):
    paired = mesh.shape["req"] == 4 and mesh.shape["exp"] == 8
    return jax.shard_map(
        paired_plan if paired else general_plan,
        mesh=mesh,
        in_specs=(
            P("exp", "req", None),
            P("exp", "req", None),
            P("exp", "req", None),
            P("exp", "req", None, None),
            P("exp", None),
            P("exp", None),
            P("exp"),
            P(),
            P("req", "exp"),
        ),
        out_specs=(P("exp", "req", None), P("exp", "req", None, None)),
        check_vma=False,
    )
```
